128 devices in a mesh: brick: 32 (over z, y, core), batch: 4 (over x).
Axes of the slice: x: 4, y: 4, z: 4, core: 2. Of those that a mesh axis runs over, the one named last changes fastest.
Arguments:
- crossings: int32 [16384, 8], P(('brick', 'batch')), may hold values from 0 to 31, all different within a row; in each aligned block of 128 rows (0 to 127, 128 to 255, ...) at most 64 rows name the same one
- lattice: int32 [3, 8, 4, 16384], P(None, None, None, ('brick', 'batch')), may hold values from 0 to 38
- offsets: float32 [3, 8, 4, 16384], P(None, None, None, ('brick', 'batch')), may hold values from 0 to 1
- target: float32 [3, 16384], P(None, ('brick', 'batch')), may hold values from 0 to 1
- planes: bfloat16 [32, 1600, 144], P('brick'), may hold values from -6 to 6
- line_factors: bfloat16 [32, 40, 144], P('brick'), may hold values from -6 to 6
- layer_one: bfloat16 [32, 144, 128], P('brick'), may hold values from -0.5 to 0.5
- layer_two: bfloat16 [32, 128, 128], P('brick'), may hold values from -0.5 to 0.5
- layer_out: bfloat16 [32, 128, 64], P('brick'), may hold values from -0.5 to 0.5
- density_head: bfloat16 [32, 128], P('brick'), may hold values from -0.5 to 0.5
- density_bias: float32 [32], P('brick'), may hold values from -2 to 1
- decoder_in: bfloat16 [64, 256], replicated, may hold values from -0.75 to 0.75
- decoder_out: bfloat16 [3, 256], replicated, may hold values from -0.375 to 0.375
Outputs:
- grad_planes: float32 [32, 1600, 144], P('brick')
- grad_lines: float32 [32, 40, 144], P('brick')
- grad_layer_one: float32 [32, 144, 128], P('brick')
- grad_layer_two: float32 [32, 128, 128], P('brick')
- grad_layer_out: float32 [32, 128, 64], P('brick')
- grad_density_head: float32 [32, 128], P('brick')
- grad_density_bias: float32 [32], P('brick')
- grad_decoder_in: float32 [64, 256], replicated
- grad_decoder_out: float32 [3, 256], replicated
- objective: float32 [], replicated
The draws below stay inside these ranges and needn't reach their ends.
Inputs may be any that keep to these rules, and one draw needn't show every extreme that they name: `crossings`: A ray's 8 bricks are distinct. Among the rays of one device at most 64 cross any one brick, and in every draw some device has exactly 64 rays crossing one brick.
All inputs are finite; a program needn't handle non-finite values.
Results may differ from the reference program's by a relative error of at most 0.0098.
Values may be sent and summed in bfloat16 or wider, within the bound.
A program may use at most 64 MiB of HBM per device.

```python
import math
import jax
import jax.numpy as jnp
import numpy as np
from jax import lax

VM = 144
HID = 128
FEAT = 64
DEC = 256
G = 40
K = 8
SAMP = 4
R_DEV = 128
CAP = 64
RAYS = 16384
BRICKS = 32
N_BRICK = 32
N_BATCH = 4


def plant(result, key, least, high):
    spot = [jax.random.randint(jax.random.fold_in(key, axis), (), 0, length) for axis, length in enumerate(result.shape)]
    main_axis = result.shape.index(max(result.shape))
    beside = spot[:main_axis] + [(spot[main_axis] + 1) % result.shape[main_axis]] + spot[main_axis + 1:]
    return result.at[tuple(spot)].set(least).at[tuple(beside)].set(high)


def block_levels(stream_key, shape, cuts, least, largest):
    def one(dim, shards_of):
        steps = jax.random.uniform(jax.random.fold_in(jax.random.fold_in(stream_key, 6), dim), (shards_of,), jnp.float32, least / len(cuts), largest / len(cuts))
        return jnp.repeat(jnp.exp(steps), shape[dim] // shards_of).reshape((-1,) + (1,) * (len(shape) - dim - 1))

    factor_of = one(*cuts[0])
    for cut in cuts[1:]:
        factor_of = factor_of * one(*cut)
    return factor_of


def shared_out(own_key, own, number, rows, number_of, top, limit, lean):
    ranking = jax.random.permutation(own_key, number_of)
    heavy_load, usual = load_shares(number_of, rows * top, limit, lean, True), load_shares(number_of, rows * top, limit, lean, False)
    places = jnp.arange(number_of)

    def named(lengths, turn):
        used = int((lengths > 0).sum())
        fixed = max(1, used // 4)
        moved = fixed + (places - fixed + turn * (used - fixed)) % max(1, number_of - fixed)
        return jnp.zeros((number_of,), jnp.int32).at[ranking[jnp.where(places < fixed, places, moved)]].set(jnp.asarray(lengths, jnp.int32))

    lengths = jnp.where(number % 4 == 0, named(heavy_load, number // 4), named(usual, number - number // 4 - 1))
    mixed = jax.random.permutation(jax.random.fold_in(own, 3), number_of)
    giver, sink = mixed[0:number_of // 2 * 2:2], mixed[1:number_of // 2 * 2:2]
    margin = jnp.minimum(lengths[giver] - 1, limit - lengths[sink]) // 2
    margin = jnp.where((giver == ranking[0]) | (sink == ranking[0]) | (lengths[sink] == 0), 0, jnp.maximum(margin, 0))
    moved = jax.random.randint(jax.random.fold_in(own, 4), (number_of // 2,), 0, 1 << 20) % (margin + 1)
    lengths = lengths.at[giver].add(-moved).at[sink].add(moved)
    labels = jnp.searchsorted(jnp.cumsum(lengths), jnp.arange(rows * top), side="right").astype(jnp.int32)
    listing = labels.reshape(top, rows).T
    listing = listing[jax.random.permutation(jax.random.fold_in(own, 1), rows)]
    turn = jax.random.randint(jax.random.fold_in(own, 2), (rows, 1), 0, top)
    return jnp.take_along_axis(listing, (jnp.arange(top)[None, :] + turn) % top, axis=1)


def load_shares(amount, total, bound, skew, full):
    loads = [(1 << 20) // math.isqrt(rank ** skew) + 1 for rank in range(1, amount + 1)]
    largest = bound if full else min(bound, max(-(-total // amount), total * loads[0] // sum(loads)))
    least = 1 if total - largest >= amount - 1 else 0
    given, rest = [largest] + [least] * (amount - 1), total - largest - least * (amount - 1)
    while rest > 0:
        movable = [i for i in range(1, amount) if given[i] < largest] or [i for i in range(1, amount) if given[i] < bound]
        pool, left = sum([loads[i] for i in movable]), rest
        for i in movable:
            more = min(bound - given[i], max(1, left * loads[i] // pool), rest)
            given[i] = given[i] + more
            rest = rest - more
    return np.array(given)


def noise(key, extent, scale, bound, shards=(), kind=jnp.bfloat16):
    array = jax.random.normal(key, extent, jnp.float32) * scale
    if len(shards) > 0:
        array = block_levels(key, extent, shards, -0.22, 0.18) * array
    return jnp.clip(array, min=-bound, max=bound).astype(kind)


def setup_inputs(seed: int = 0) -> dict:
    key_list = jax.random.split(jax.random.key(seed), 14)
    crossings_keys = jax.random.split(jax.random.fold_in(key_list[0], 1), RAYS // R_DEV)
    crossings_turns = jax.random.permutation(jax.random.fold_in(key_list[0], 3), RAYS // R_DEV)
    crossings = jax.vmap(lambda own, number: shared_out(jax.random.fold_in(key_list[0], 2), own, number, R_DEV, N_BRICK, K, CAP, 1))(crossings_keys, crossings_turns).reshape((RAYS, K))
    lattice = plant(jax.random.randint(key_list[1], (3, K, SAMP, RAYS), 0, G - 1), jax.random.fold_in(key_list[1], 1), 0, (G - 1) - 1).astype(jnp.int32)
    offsets = jnp.clip(1.0 * jax.random.uniform(key_list[2], (3, K, SAMP, RAYS), jnp.float32) ** block_levels(key_list[2], (3, K, SAMP, RAYS), ((3, 128),), -0.2, 0.2), 0.0, 1.0)
    target = jnp.clip(1.0 * jax.random.uniform(key_list[3], (3, RAYS), jnp.float32) ** block_levels(key_list[3], (3, RAYS), ((1, 128),), -0.2, 0.2), 0.0, 1.0)
    planes = noise(key_list[4], (BRICKS, G * G, VM), 1.0, 6.0, ((0, 32),))
    line_factors = noise(key_list[5], (BRICKS, G, VM), 1.0, 6.0, ((0, 32),))
    layer_one = noise(key_list[6], (BRICKS, VM, HID), VM ** -0.5, 0.5, ((0, 32),))
    layer_two = noise(key_list[7], (BRICKS, HID, HID), HID ** -0.5, 0.5, ((0, 32),))
    layer_out = noise(key_list[8], (BRICKS, HID, FEAT), HID ** -0.5, 0.5, ((0, 32),))
    density_head = noise(key_list[9], (BRICKS, HID), HID ** -0.5, 0.5, ((0, 32),))
    density_bias = jnp.clip(-2.0 + 3.0 * jax.random.uniform(key_list[10], (BRICKS,), jnp.float32) ** block_levels(key_list[10], (BRICKS,), ((0, 32),), -0.2, 0.2), -2.0, 1.0)
    decoder_in = noise(key_list[11], (FEAT, DEC), FEAT ** -0.5, 0.75)
    decoder_out = noise(key_list[12], (3, DEC), DEC ** -0.5, 0.375)
    return dict(crossings=crossings, lattice=lattice, offsets=offsets, target=target, planes=planes, line_factors=line_factors, layer_one=layer_one, layer_two=layer_two, layer_out=layer_out, density_head=density_head, density_bias=density_bias, decoder_in=decoder_in, decoder_out=decoder_out)


STEP_LENGTH = 0.1
coord_pairs = ((0, 1, 2), (0, 2, 1), (1, 2, 0))


def silu_slope(values):
    sigmoid = jax.nn.sigmoid(values)
    return sigmoid * (1.0 + values * (1.0 - sigmoid))


def hat_weight(values):
    return jnp.maximum(0.0, 1.0 - jnp.abs(values))


def rounded(values):
    return lax.optimization_barrier(values.astype(jnp.bfloat16))


def contract_rows(left_side, right_side):
    return lax.dot_general(left_side, right_side, (((0,), (0,)), ((), ())), preferred_element_type=jnp.float32)


def contract_last(left_side, right_side):
    return lax.dot_general(left_side, right_side, (((1,), (1,)), ((), ())), preferred_element_type=jnp.float32)


def mlp_forward(vm_feature, layer_one, layer_two, layer_out, density_head, density_bias):
    pre_one = jnp.dot(vm_feature, layer_one, preferred_element_type=jnp.float32)
    hidden_one = jax.nn.silu(pre_one).astype(jnp.bfloat16)
    pre_two = jnp.dot(hidden_one, layer_two, preferred_element_type=jnp.float32)
    hidden_two = jax.nn.silu(pre_two).astype(jnp.bfloat16)
    features = jnp.dot(hidden_two, layer_out, preferred_element_type=jnp.float32).astype(jnp.bfloat16)
    density_pre = jnp.dot(hidden_two, density_head, preferred_element_type=jnp.float32) + density_bias
    density = jax.nn.softplus(density_pre).astype(jnp.bfloat16)
    return features, density, (pre_one, hidden_one, pre_two, hidden_two, density_pre)


def mlp_backward(vm_feature, weights, grad_features, grad_density):
    layer_one, layer_two, layer_out, density_head, density_bias = weights
    unused_one, unused_two, saved_values = mlp_forward(vm_feature, layer_one, layer_two, layer_out, density_head, density_bias)
    pre_one, hidden_one, pre_two, hidden_two, density_pre = saved_values
    grad_zeta = rounded(grad_density.astype(jnp.float32) * jax.nn.sigmoid(density_pre))
    grad_bias = jnp.sum(grad_zeta.astype(jnp.float32))
    grad_out = contract_rows(hidden_two, grad_features)
    grad_head = jnp.dot(grad_zeta, hidden_two, preferred_element_type=jnp.float32)
    back_two = contract_last(grad_features, layer_out) + grad_zeta.astype(jnp.float32)[:, None] * density_head.astype(jnp.float32)[None, :]
    grad_pre_two = (back_two * silu_slope(pre_two)).astype(jnp.bfloat16)
    grad_two = contract_rows(hidden_one, grad_pre_two)
    back_one = contract_last(grad_pre_two, layer_two)
    grad_pre_one = (back_one * silu_slope(pre_one)).astype(jnp.bfloat16)
    grad_one = contract_rows(vm_feature, grad_pre_one)
    grad_vm = contract_last(grad_pre_one, layer_one)
    return grad_vm, (grad_one, grad_two, grad_out, grad_head, grad_bias)


def corner_terms(position, corner, brick_of):
    plane_terms = []
    line_terms = []
    for axis_one, axis_two, axis_line in coord_pairs:
        pair_planes = []
        for step_one in (0, 1):
            for step_two in (0, 1):
                point_one = corner[axis_one] + step_one
                point_two = corner[axis_two] + step_two
                weights = rounded(hat_weight(position[axis_one] - point_one.astype(jnp.float32)) * hat_weight(position[axis_two] - point_two.astype(jnp.float32)))
                row_index = (brick_of * G + point_one) * G + point_two
                pair_planes.append((row_index, weights.astype(jnp.float32)))
        pair_lines = []
        for step_line in (0, 1):
            point_line = corner[axis_line] + step_line
            weights = rounded(hat_weight(position[axis_line] - point_line.astype(jnp.float32)))
            pair_lines.append((brick_of * G + point_line, weights.astype(jnp.float32)))
        plane_terms.append(pair_planes)
        line_terms.append(pair_lines)
    return plane_terms, line_terms


def reference(crossings, lattice, offsets, target, planes, line_factors, layer_one, layer_two, layer_out, density_head, density_bias, decoder_in, decoder_out):
    ray_count = crossings.shape[0]
    comp_width = VM // 3
    position = jnp.transpose(lattice.astype(jnp.float32) + offsets, (0, 3, 1, 2)).reshape(3, -1)
    corner = jnp.transpose(lattice, (0, 3, 1, 2)).reshape(3, -1)
    segment_brick = crossings.reshape(-1)
    brick_of = jnp.repeat(segment_brick, SAMP)
    plane_table = planes.reshape(N_BRICK * G * G, 3, comp_width)
    line_table = line_factors.reshape(N_BRICK * G, 3, comp_width)
    plane_terms, line_terms = corner_terms(position, corner, brick_of)
    plane_parts = []
    line_parts = []
    for pair_index in range(3):
        plane_value = jnp.zeros((position.shape[1], comp_width), jnp.float32)
        for row_index, weights in plane_terms[pair_index]:
            plane_value = plane_value + weights[:, None] * plane_table[row_index, pair_index].astype(jnp.float32)
        line_value = jnp.zeros((position.shape[1], comp_width), jnp.float32)
        for row_index, weights in line_terms[pair_index]:
            line_value = line_value + weights[:, None] * line_table[row_index, pair_index].astype(jnp.float32)
        plane_parts.append(plane_value)
        line_parts.append(line_value)
    vm_feature = (jnp.concatenate(plane_parts, axis=1) * jnp.concatenate(line_parts, axis=1)).astype(jnp.bfloat16)

    segment_count = segment_brick.shape[0]
    onehot = (segment_brick[:, None] == jnp.arange(N_BRICK, dtype=jnp.int32)[None, :]).astype(jnp.int32)
    segment_rank = jnp.sum((jnp.cumsum(onehot, axis=0) - onehot) * onehot, axis=1).astype(jnp.int32)
    brick_slots = N_BRICK * N_BATCH * CAP
    vm_buffer = jnp.zeros((N_BRICK, brick_slots, SAMP, VM), jnp.bfloat16)
    vm_buffer = vm_buffer.at[segment_brick, segment_rank].set(vm_feature.reshape(segment_count, SAMP, VM))
    vm_buffer = vm_buffer.reshape(N_BRICK, brick_slots * SAMP, VM)
    weight_stack = (layer_one, layer_two, layer_out, density_head, density_bias)

    def forward_brick(items):
        features, density, unused = mlp_forward(items[0], items[1], items[2], items[3], items[4], items[5])
        return features, density

    feature_buffer, density_buffer = lax.map(forward_brick, (vm_buffer,) + weight_stack)
    features = feature_buffer.reshape(N_BRICK, brick_slots, SAMP, FEAT)[segment_brick, segment_rank]
    density = density_buffer.reshape(N_BRICK, brick_slots, SAMP)[segment_brick, segment_rank]
    features = features.reshape(ray_count, K * SAMP, FEAT).astype(jnp.float32)
    density = density.reshape(ray_count, K * SAMP)

    optical_depth = STEP_LENGTH * density.astype(jnp.float32)
    before = jnp.cumsum(optical_depth, axis=1) - optical_depth
    transmit = jnp.exp(-before)
    survive = jnp.exp(-optical_depth)
    weight = transmit * (1.0 - survive)
    composite = jnp.einsum("rn,rnf->rf", weight, features).astype(jnp.bfloat16)

    loss_scale = RAYS ** -0.5
    decoder_pre = jnp.dot(composite, decoder_in, preferred_element_type=jnp.float32)
    decoder_hidden = jax.nn.silu(decoder_pre).astype(jnp.bfloat16)
    logits = contract_last(decoder_out, decoder_hidden)
    colors = jax.nn.sigmoid(logits)
    errors = colors - target
    objective = loss_scale * jnp.sum(errors * errors)
    grad_logits = (2.0 * loss_scale * errors * colors * (1.0 - colors)).astype(jnp.bfloat16)
    grad_decoder_out = jnp.dot(grad_logits, decoder_hidden, preferred_element_type=jnp.float32)
    back_decoder = contract_rows(grad_logits, decoder_out)
    grad_decoder_pre = (back_decoder * silu_slope(decoder_pre)).astype(jnp.bfloat16)
    grad_decoder_in = contract_rows(composite, grad_decoder_pre)
    grad_composite = contract_last(grad_decoder_pre, decoder_in)

    grad_weight = jnp.einsum("rnf,rf->rn", features, grad_composite)
    grad_features = (weight[:, :, None] * grad_composite[:, None, :]).astype(jnp.bfloat16)
    carried = grad_weight * weight
    later_sum = jnp.sum(carried, axis=1, keepdims=True) - jnp.cumsum(carried, axis=1)
    grad_density = (STEP_LENGTH * (grad_weight * transmit * survive - later_sum)).astype(jnp.bfloat16)

    grad_feature_buffer = jnp.zeros((N_BRICK, brick_slots, SAMP, FEAT), jnp.bfloat16)
    grad_feature_buffer = grad_feature_buffer.at[segment_brick, segment_rank].set(grad_features.reshape(segment_count, SAMP, FEAT))
    grad_density_buffer = jnp.zeros((N_BRICK, brick_slots, SAMP), jnp.bfloat16)
    grad_density_buffer = grad_density_buffer.at[segment_brick, segment_rank].set(grad_density.reshape(segment_count, SAMP))

    def backward_brick(items):
        return mlp_backward(items[0], items[1:6], items[6], items[7])

    grad_vm_buffer, mlp_grads = lax.map(backward_brick, (vm_buffer,) + weight_stack + (grad_feature_buffer.reshape(N_BRICK, brick_slots * SAMP, FEAT), grad_density_buffer.reshape(N_BRICK, brick_slots * SAMP)))
    grad_vm = grad_vm_buffer.reshape(N_BRICK, brick_slots, SAMP, VM)[segment_brick, segment_rank].reshape(-1, VM)

    grad_plane_table = jnp.zeros((N_BRICK * G * G, 3, comp_width), jnp.float32)
    grad_line_table = jnp.zeros((N_BRICK * G, 3, comp_width), jnp.float32)
    for pair_index in range(3):
        columns = slice(pair_index * comp_width, (pair_index + 1) * comp_width)
        grad_plane = rounded(grad_vm[:, columns] * line_parts[pair_index]).astype(jnp.float32)
        grad_line = rounded(grad_vm[:, columns] * plane_parts[pair_index]).astype(jnp.float32)
        for row_index, weights in plane_terms[pair_index]:
            grad_plane_table = grad_plane_table.at[row_index, pair_index].add(weights[:, None] * grad_plane)
        for row_index, weights in line_terms[pair_index]:
            grad_line_table = grad_line_table.at[row_index, pair_index].add(weights[:, None] * grad_line)
    grad_planes = grad_plane_table.reshape(N_BRICK, G * G, VM)
    grad_lines = grad_line_table.reshape(N_BRICK, G, VM)
    grad_one, grad_two, grad_out, grad_head, grad_bias = mlp_grads
    return (grad_planes, grad_lines, grad_one, grad_two, grad_out, grad_head, grad_bias, grad_decoder_in, grad_decoder_out, objective)
```

```python
import functools

import jax
import jax.numpy as jnp
from jax import lax
from jax.experimental import pallas as pl
from jax.experimental.pallas import tpu as pltpu
from jax.sharding import PartitionSpec as P

STEP_LENGTH = 0.1
MESH = pl.DeviceIdType.MESH
F32 = jnp.float32
BF16 = jnp.bfloat16

BRICKS = 32
BATCH = 4
RAYS = 128
CROSS = 8
CAP = 64
SLOTS = BRICKS * CAP
G = 40
VM = 144
COMP = 48
HID = 128
FEAT = 64
AUG = 80
DEC = 256
STRIPE = 5
STRIPES = 8
LOCAL = (STRIPE + 1) * G
WIDE = STRIPES * COMP
PEERS = 4
CHUNK = PEERS * 256
CHUNKS = BRICKS // PEERS
SAMPLES = BRICKS * CAP * 4
MSG = 48
PACK = 768
SHARD = PACK // BATCH
PAIRS = ((0, 1, 2), (0, 2, 1), (1, 2, 0))
VMEM_SPEC = pl.BlockSpec(memory_space=pltpu.VMEM)
SMEM_SPEC = pl.BlockSpec(memory_space=pltpu.SMEM)


def mm(a, b):
    return lax.dot_general(a, b, (((1,), (0,)), ((), ())), preferred_element_type=F32)


def nt(a, b):
    return lax.dot_general(a, b, (((1,), (1,)), ((), ())), preferred_element_type=F32)


def tn(a, b):
    return lax.dot_general(a, b, (((0,), (0,)), ((), ())), preferred_element_type=F32)


def split3(x):
    one = x.astype(BF16)
    rest = x - one.astype(F32)
    two = rest.astype(BF16)
    three = (rest - two.astype(F32)).astype(BF16)
    return one, two, three


def iota(shape, axis, kind=jnp.int32):
    return lax.broadcasted_iota(jnp.int32, shape, axis).astype(kind)


def eye(n):
    return jnp.where(iota((n, n), 0) == iota((n, n), 1), 1.0, 0.0).astype(BF16)


def sigmoid(v):
    return 0.5 * jnp.tanh(0.5 * v) + 0.5


def low_half(shape):
    return iota(shape, len(shape) - 1) < CAP


def swap(x):
    return pltpu.roll(x, CAP, 1)


def brick_barrier(me, extra=()):
    barrier = pltpu.get_barrier_semaphore()

    def one(d, carry):
        pl.semaphore_signal(
            barrier, inc=1, device_id={"brick": lax.rem(me + d, BRICKS)}, device_id_type=MESH
        )
        return carry

    lax.fori_loop(1, BRICKS, one, 0)
    for peer in extra:
        pl.semaphore_signal(barrier, inc=1, device_id={"batch": peer}, device_id_type=MESH)
    pl.semaphore_wait(barrier, BRICKS - 1 + len(extra))


def to_brick(src, dst, send_sem, recv_sem, d, peer):
    return pltpu.make_async_remote_copy(
        src_ref=src,
        dst_ref=dst,
        send_sem=send_sem.at[d],
        recv_sem=recv_sem.at[d],
        device_id={"brick": peer},
        device_id_type=MESH,
    )


def exchange_start(me, sent, got, send_sem, recv_sem):
    def one(d, carry):
        peer = lax.rem(me + d, BRICKS)
        to_brick(sent.at[peer], got.at[me], send_sem, recv_sem, d, peer).start()
        return carry

    lax.fori_loop(1, BRICKS, one, 0)


def exchange_wait(me, sent, got, send_sem, recv_sem):
    def one(d, carry):
        peer = lax.rem(me + d, BRICKS)
        to_brick(sent.at[peer], got.at[me], send_sem, recv_sem, d, peer).wait()
        return carry

    lax.fori_loop(1, BRICKS, one, 0)


def rays_to_bricks(
    crossings,
    lattice,
    offsets,
    planes,
    line_factors,
    layer_one,
    layer_two,
    layer_out,
    density_head,
    positions,
    ray_slots,
    slot_cross,
    plane_t,
    line_t,
    one_t,
    two_t,
    out_t,
    out_aug,
    sent,
    got,
    send_sem,
    recv_sem,
):
    me = lax.axis_index("brick")
    brick_barrier(me)
    named = crossings[...]
    brick_lane = iota((RAYS, BRICKS), 1)
    crosses = jnp.zeros((RAYS, BRICKS), F32)
    order = jnp.zeros((RAYS, BRICKS), F32)
    for k in range(CROSS):
        hit = jnp.where(named[:, k : k + 1] == brick_lane, 1.0, 0.0)
        crosses = crosses + hit
        order = order + float(k) * hit
    before = jnp.where(iota((RAYS, RAYS), 0) > iota((RAYS, RAYS), 1), 1.0, 0.0).astype(BF16)
    rank = mm(before, crosses.astype(BF16))
    rank = jnp.where(crosses > 0.0, rank, -1.0)
    lane = iota((BRICKS, SLOTS), 1)
    first = iota((BRICKS, SLOTS), 0) * CAP
    spread = jnp.where((lane >= first) & (lane < first + CAP), 1.0, 0.0).astype(BF16)
    place = (iota((RAYS, SLOTS), 1) & (CAP - 1)).astype(F32)
    chosen = jnp.where(mm(rank.astype(BF16), spread) == place, 1.0, 0.0)
    order_wide = mm(order.astype(BF16), spread)
    cross_of = jnp.sum(chosen * order_wide, axis=0, keepdims=True)
    chosen = chosen.astype(BF16)
    ray_slots[...] = chosen
    slot_cross[...] = jnp.broadcast_to(cross_of, (8, SLOTS))
    pad = jnp.zeros((2, RAYS), F32)
    rows = []
    for k in range(CROSS):
        for odd in range(2):
            for c in range(3):
                for half in range(2):
                    s = 2 * half + odd
                    rows.append(
                        lattice[c, k, s : s + 1, :].astype(F32) + offsets[c, k, s : s + 1, :]
                    )
            rows.append(pad)
    stacked = jnp.concatenate(split3(jnp.concatenate(rows, axis=0)), axis=0)
    height = CROSS * 16
    moved = mm(stacked, chosen)
    moved = moved[:height] + moved[height : 2 * height] + moved[2 * height :]
    picked = jnp.zeros((16, SLOTS), F32)
    for k in range(CROSS):
        picked = jnp.where(cross_of == float(k), moved[16 * k : 16 * k + 16], picked)
    low = low_half((8, 128))
    for tile in range(BRICKS // 2):
        x = picked[:, 128 * tile : 128 * tile + 128]
        even, odd = x[:8], x[8:]
        sent[2 * tile] = jnp.where(low, even, swap(odd))
        sent[2 * tile + 1] = jnp.where(low, swap(even), odd)
    exchange_start(me, sent, got, send_sem, recv_sem)
    got[me] = sent[me]

    unit = eye(VM)
    for h in range(STRIPES):
        first_row = STRIPE * G * h
        height = min(LOCAL, G * G - first_row)
        turned = nt(unit, planes[0, first_row : first_row + height, :])
        if height < LOCAL:
            turned = jnp.concatenate([turned, jnp.zeros((VM, LOCAL - height), F32)], axis=1)
        for p in range(3):
            plane_t[p, COMP * h : COMP * h + COMP, :] = turned[COMP * p : COMP * p + COMP].astype(
                BF16
            )
    turned = nt(unit, line_factors[0])
    wide = jnp.concatenate([turned, turned, turned, jnp.zeros((VM, 8), F32)], axis=1)
    row, column = iota((VM, 128), 0), iota((VM, 128), 1)
    keep = (
        ((row < 48) & (column < 40))
        | ((row >= 48) & (row < 96) & (column >= 40) & (column < 80))
        | ((row >= 96) & (column >= 80) & (column < 120))
    )
    line_t[...] = jnp.where(keep, wide, 0.0).astype(BF16)
    unit = eye(HID)
    one_t[...] = nt(unit, layer_one[0]).astype(BF16)
    two_t[...] = nt(unit, layer_two[0]).astype(BF16)
    rows = [
        nt(eye(FEAT), layer_out[0]),
        density_head[...].astype(F32),
        jnp.zeros((AUG - FEAT - 1, HID), F32),
    ]
    both = jnp.concatenate(rows, axis=0).astype(BF16)
    out_t[...] = both
    out_aug[...] = nt(unit, both).astype(BF16)

    exchange_wait(me, sent, got, send_sem, recv_sem)
    positions[...] = got[...]


def hat(x):
    return jnp.maximum(0.0, 1.0 - jnp.abs(x))


def tables(positions):
    coords = []
    for c in range(3):
        parts = [
            positions[p, 2 * c + half : 2 * c + half + 1, :]
            for p in range(PEERS)
            for half in range(2)
        ]
        coords.append(jnp.concatenate(parts, axis=1))
    points = iota((G, CHUNK), 0, F32)
    return coords, [hat(coord - points) for coord in coords]


def stripe_weights(coords, hats, pair):
    a, b, line = PAIRS[pair]
    stripe = jnp.floor(coords[a] * (1.0 / STRIPE))
    local = coords[a] - float(STRIPE) * stripe
    near = hat(local - iota((8, CHUNK), 0, F32))
    weights = jnp.concatenate(
        [near[i : i + 1] * hats[b] for i in range(STRIPE + 1)], axis=0
    ).astype(BF16)
    return stripe, weights


def line_table(hats):
    rows = [hats[PAIRS[p][2]] for p in range(3)] + [jnp.zeros((8, CHUNK), F32)]
    return jnp.concatenate(rows, axis=0).astype(BF16)


def within_crossing(zeta, peer):
    low = low_half((1, 128))
    depths = []
    for half in range(2):
        at = 256 * peer + 128 * half
        z = zeta[:, at : at + 128]
        density = jnp.maximum(z, 0.0) + jnp.log1p(jnp.exp(-jnp.abs(z)))
        depths.append(STEP_LENGTH * density.astype(BF16).astype(F32))
    d0, d1 = depths
    r0, r1 = swap(d0), swap(d1)
    both = d0 + r0
    b0 = jnp.where(low, 0.0, r0)
    b1 = both + jnp.where(low, 0.0, r1)
    total = both + (d1 + r1)
    return (d0, d1), (b0, b1), total


def brick_forward(
    positions,
    plane_t,
    line_t,
    one_t,
    two_t,
    out_t,
    bias,
    message,
    vm_out,
    plane_out,
    line_out,
    h1_out,
    s1_out,
    h2_out,
    s2_out,
    feat_out,
    zeta_out,
):
    coords, hats = tables(positions)
    values = []
    for pair in range(3):
        stripe, weights = stripe_weights(coords, hats, pair)
        wide = mm(plane_t[pair], weights)
        value = wide[:COMP]
        for h in range(1, STRIPES):
            value = jnp.where(stripe == float(h), wide[COMP * h : COMP * h + COMP], value)
        values.append(value)
    plane_value = jnp.concatenate(values, axis=0)
    line_value = mm(line_t[...], line_table(hats))
    vm = (plane_value * line_value).astype(BF16)
    vm_out[...] = vm
    plane_out[...] = plane_value.astype(BF16)
    line_out[...] = line_value.astype(BF16)
    a1 = mm(one_t[...], vm)
    g1 = sigmoid(a1)
    h1 = (a1 * g1).astype(BF16)
    h1_out[...] = h1
    s1_out[...] = (g1 * (1.0 + a1 * (1.0 - g1))).astype(BF16)
    a2 = mm(two_t[...], h1)
    g2 = sigmoid(a2)
    h2 = (a2 * g2).astype(BF16)
    h2_out[...] = h2
    s2_out[...] = (g2 * (1.0 + a2 * (1.0 - g2))).astype(BF16)
    wide = mm(out_t[...], h2)
    feat = wide[:FEAT].astype(BF16)
    feat_out[...] = feat
    zeta = wide[FEAT : FEAT + 1] + bias[0]
    zeta_out[...] = jnp.broadcast_to(zeta, (8, CHUNK))
    low = low_half((FEAT // 2, 128))
    for peer in range(PEERS):
        depths, befores, total = within_crossing(zeta, peer)
        summed = jnp.zeros((FEAT, 128), F32)
        for half in range(2):
            weight = jnp.exp(-befores[half]) * (1.0 - jnp.exp(-depths[half]))
            at = 256 * peer + 128 * half
            summed = summed + weight * feat[:, at : at + 128].astype(F32)
        summed = summed + swap(summed)
        folded = jnp.where(low, summed[: FEAT // 2], summed[FEAT // 2 :])
        parts = [part.astype(F32) for part in split3(total)]
        rows = [folded] + parts + [jnp.zeros((MSG - FEAT // 2 - 3, 128), F32)]
        message[peer] = jnp.concatenate(rows, axis=0).astype(BF16)


def by_cross(row, cross_mask, ray_slots):
    parts = split3(row * cross_mask)
    out = nt(jnp.concatenate(parts, axis=0), ray_slots)
    return out[0:8] + out[8:16] + out[16:24]


def to_slots(table, cross_mask, ray_slots):
    out = mm(jnp.concatenate(split3(table), axis=0), ray_slots)
    out = out[0:8] + out[8:16] + out[16:24]
    return jnp.sum(out * cross_mask, axis=0, keepdims=True)


def rays_train(
    message,
    ray_slots_ref,
    slot_cross,
    target,
    decoder_in,
    decoder_out,
    back,
    decoder_sum,
    got,
    sent,
    back_got,
    decoder_sent,
    decoder_got,
    partial,
    gathered,
    send_sem,
    recv_sem,
    send_sem2,
    recv_sem2,
    send_sem3,
    recv_sem3,
):
    me = lax.axis_index("brick")
    brick_barrier(me)
    exchange_start(me, message, got, send_sem, recv_sem)
    got[me] = message[me]
    ray_slots = ray_slots_ref[...]
    cross_mask = jnp.where(slot_cross[...] == iota((8, SLOTS), 0, F32), 1.0, 0.0)
    low = low_half((FEAT // 2, 128))
    low_row = low_half((1, 128))
    exchange_wait(me, message, got, send_sem, recv_sem)
    half = FEAT // 2
    depth_rows = []
    for tile in range(BRICKS // 2):
        even, odd = got[2 * tile].astype(F32), got[2 * tile + 1].astype(F32)
        e, o = even[:half], odd[:half]
        lanes = slice(128 * tile, 128 * tile + 128)
        gathered[:half, lanes] = jnp.where(low, e, swap(o))
        gathered[half:, lanes] = jnp.where(low, swap(e), o)
        e = even[half : half + 1] + even[half + 1 : half + 2] + even[half + 2 : half + 3]
        o = odd[half : half + 1] + odd[half + 1 : half + 2] + odd[half + 2 : half + 3]
        depth_rows.append(jnp.where(low_row, e, o))
    depth = jnp.concatenate(depth_rows, axis=1)
    by_ray = by_cross(depth, cross_mask, ray_slots)
    running = jnp.zeros((1, RAYS), F32)
    befores = []
    for k in range(CROSS):
        befores.append(running)
        running = running + by_ray[k : k + 1]
    enter = to_slots(jnp.exp(-jnp.concatenate(befores, axis=0)), cross_mask, ray_slots)
    partials = gathered[...]
    scaled = partials * enter
    high = scaled.astype(BF16)
    rest = (scaled - high.astype(F32)).astype(BF16)
    composite = nt(jnp.concatenate([high, rest], axis=0), ray_slots)
    composite = (composite[:FEAT] + composite[FEAT:]).astype(BF16)
    decoder_pre = tn(decoder_in[...], composite)
    gate = sigmoid(decoder_pre)
    decoder_hidden = (decoder_pre * gate).astype(BF16)
    logits = mm(decoder_out[...], decoder_hidden)
    colors = sigmoid(logits)
    errors = colors - target[...]
    scale = float(RAYS * BRICKS * BATCH) ** (-0.5)
    objective = scale * jnp.sum(errors * errors)
    grad_logits = (2.0 * scale * errors * colors * (1.0 - colors)).astype(BF16)
    grad_out = nt(grad_logits, decoder_hidden)
    back_decoder = tn(decoder_out[...], grad_logits)
    grad_pre = (back_decoder * (gate * (1.0 + decoder_pre * (1.0 - gate)))).astype(BF16)
    grad_in = nt(composite, grad_pre)
    grad_composite = mm(decoder_in[...], grad_pre).astype(BF16)

    decoder_sent[...] = jnp.zeros_like(decoder_sent)
    for j in range(8):
        decoder_sent[j] = grad_in[8 * j : 8 * j + 8, :128]
        decoder_sent[8 + j] = grad_in[8 * j : 8 * j + 8, 128:]
    rows = [
        grad_out[:, :128],
        grad_out[:, 128:],
        jnp.full((2, 128), objective, F32),
    ]
    decoder_sent[16] = jnp.concatenate(rows, axis=0)
    exchange_start(me, decoder_sent, decoder_got, send_sem3, recv_sem3)
    decoder_got[me] = decoder_sent[me]

    grad_slots = mm(grad_composite, ray_slots)
    along = jnp.sum(partials * grad_slots, axis=0, keepdims=True) * enter
    by_ray = by_cross(along, cross_mask, ray_slots)
    running = jnp.zeros((1, RAYS), F32)
    laters = []
    for k in reversed(range(CROSS)):
        laters.insert(0, running)
        running = running + by_ray[k : k + 1]
    later = to_slots(jnp.concatenate(laters, axis=0), cross_mask, ray_slots)
    for tile in range(BRICKS // 2):
        lanes = slice(128 * tile, 128 * tile + 128)
        top, bottom = grad_slots[:half, lanes], grad_slots[half:, lanes]
        scalars = [part.astype(F32) for part in split3(enter[:, lanes]) + split3(later[:, lanes])]
        scalars = jnp.concatenate(scalars + [jnp.zeros((2, 128), F32)], axis=0)
        low8 = low_half((8, 128))
        turned = swap(scalars)
        fill = jnp.zeros((MSG - half - 8, 128), F32)
        rows = [jnp.where(low, top, swap(bottom)), jnp.where(low8, scalars, turned), fill]
        sent[2 * tile] = jnp.concatenate(rows, axis=0).astype(BF16)
        rows = [jnp.where(low, swap(top), bottom), jnp.where(low8, turned, scalars), fill]
        sent[2 * tile + 1] = jnp.concatenate(rows, axis=0).astype(BF16)
    exchange_start(me, sent, back_got, send_sem2, recv_sem2)
    back_got[me] = sent[me]
    exchange_wait(me, decoder_sent, decoder_got, send_sem3, recv_sem3)
    total = decoder_got[0]
    for j in range(1, BRICKS):
        total = total + decoder_got[j]
    decoder_sum[...] = total
    exchange_wait(me, sent, back_got, send_sem2, recv_sem2)
    back[...] = back_got[...]


def brick_backward(
    positions,
    back,
    vm_in,
    plane_in,
    line_in,
    h1_in,
    s1_in,
    h2_in,
    s2_in,
    feat_in,
    zeta_in,
    layer_one,
    layer_two,
    out_aug,
    packed,
    bias_grad,
    acc_planes,
    acc_lines,
    acc_one,
    acc_two,
    acc_out,
    acc_bias,
):
    step = pl.program_id(0)

    @pl.when(step == 0)
    def _():
        for ref in (acc_planes, acc_lines, acc_one, acc_two, acc_out, acc_bias):
            ref[...] = jnp.zeros_like(ref)

    zeta = zeta_in[0:1, :]
    low = low_half((FEAT // 2, 128))
    low_row = low_half((1, 128))
    half = FEAT // 2
    grad_feats, grad_zetas = [], []
    for peer in range(PEERS):
        depths, befores, total = within_crossing(zeta, peer)
        got = back[peer].astype(F32)
        m = got[:half]
        turned = swap(m)
        grads = jnp.concatenate([jnp.where(low, m, turned), jnp.where(low, turned, m)], axis=0)
        enter = got[half : half + 1] + got[half + 1 : half + 2] + got[half + 2 : half + 3]
        later = got[half + 3 : half + 4] + got[half + 4 : half + 5] + got[half + 5 : half + 6]
        grad_weights, carried, lit = [], [], []
        for j in range(2):
            at = 256 * peer + 128 * j
            transmit = enter * jnp.exp(-befores[j])
            survive = jnp.exp(-depths[j])
            weight = transmit * (1.0 - survive)
            grad_weight = jnp.sum(
                grads * feat_in[:, at : at + 128].astype(F32), axis=0, keepdims=True
            )
            grad_feats.append(weight * grads)
            carried.append(grad_weight * weight)
            lit.append(grad_weight * transmit * survive)
        v0, v1 = carried
        r0, r1 = swap(v0), swap(v1)
        laters = (
            jnp.where(low_row, r0, 0.0) + (v1 + r1) + later,
            jnp.where(low_row, r1, 0.0) + later,
        )
        for j in range(2):
            at = 256 * peer + 128 * j
            grad_density = (STEP_LENGTH * (lit[j] - laters[j])).astype(BF16).astype(F32)
            gate = sigmoid(zeta[:, at : at + 128])
            grad_zetas.append((grad_density * gate).astype(BF16).astype(F32))
    grad_zeta = jnp.concatenate(grad_zetas, axis=1)
    acc_bias[...] += jnp.full((8, 128), jnp.sum(grad_zeta), F32)
    rows = [jnp.concatenate(grad_feats, axis=1), grad_zeta]
    rows.append(jnp.zeros((AUG - FEAT - 1, CHUNK), F32))
    grad_aug = jnp.concatenate(rows, axis=0).astype(BF16)
    acc_out[...] += nt(h2_in[...], grad_aug)
    grad_a2 = (mm(out_aug[...], grad_aug) * s2_in[...].astype(F32)).astype(BF16)
    acc_two[...] += nt(h1_in[...], grad_a2)
    grad_a1 = (mm(layer_two[0], grad_a2) * s1_in[...].astype(F32)).astype(BF16)
    acc_one[...] += nt(vm_in[...], grad_a1)
    grad_vm = mm(layer_one[0], grad_a1)
    grad_plane = (grad_vm * line_in[...].astype(F32)).astype(BF16)
    grad_line = (grad_vm * plane_in[...].astype(F32)).astype(BF16)
    coords, hats = tables(positions)
    acc_lines[...] += nt(line_table(hats), grad_line)
    for pair in range(3):
        stripe, weights = stripe_weights(coords, hats, pair)
        piece = grad_plane[COMP * pair : COMP * pair + COMP]
        masked = [
            piece * jnp.where(stripe == float(h), 1.0, 0.0).astype(BF16) for h in range(STRIPES)
        ]
        acc_planes[pair] += nt(weights, jnp.concatenate(masked, axis=0))

    @pl.when(step == CHUNKS - 1)
    def _():
        bias_grad[...] = acc_bias[...]
        for pair in range(3):
            at = STRIPE * G * pair
            over = pltpu.roll(acc_planes[pair, STRIPE * G :, :], COMP, 1)
            packed[at : at + G, :] = acc_planes[pair, :G, :] + over
            packed[at + G : at + STRIPE * G, :] = acc_planes[pair, G : STRIPE * G, :]
        at = 3 * STRIPE * G
        packed[at : at + VM, 0:128] = acc_one[...]
        packed[at : at + HID, 128:256] = acc_two[...]
        packed[at + HID : at + VM, 128:384] = jnp.zeros((VM - HID, 256), F32)
        for pair in range(3):
            r = slice(G * pair, G * pair + G)
            block = [acc_out[r, :], acc_lines[r, COMP * pair : COMP * pair + COMP]]
            packed[at + G * pair : at + G * pair + G, 256:384] = jnp.concatenate(block, axis=1)
        block = [acc_out[3 * G :, :], jnp.zeros((8, COMP), F32)]
        packed[at + 3 * G : at + HID, 256:384] = jnp.concatenate(block, axis=1)
        packed[at + VM :, :] = jnp.zeros((PACK - at - VM, WIDE), F32)


def add_up(
    packed,
    decoder_sum,
    bias_grad,
    planes,
    lines,
    one,
    two,
    out,
    head,
    bias,
    decoder_in,
    decoder_out,
    objective,
    sent,
    got,
    whole,
    small,
    small_sent,
    decoder_got,
    send_rs,
    recv_rs,
    send_ag,
    recv_ag,
    send_small,
    recv_small,
    send_dec,
    recv_dec,
):
    me = lax.axis_index("brick")
    x = lax.axis_index("batch")
    peers = [lax.rem(x + d, BATCH) for d in range(1, BATCH)]
    brick_barrier(me, peers)
    small_sent[0:8] = decoder_sum[...]
    small_sent[8:16] = bias_grad[...]
    sent[...] = packed[...].astype(BF16)

    def remote(src, dst, send_sem, recv_sem, peer):
        return pltpu.make_async_remote_copy(
            src_ref=src,
            dst_ref=dst,
            send_sem=send_sem,
            recv_sem=recv_sem,
            device_id={"batch": peer},
            device_id_type=MESH,
        )

    def rows(i):
        return pl.ds(pl.multiple_of(i * SHARD, SHARD), SHARD)

    smalls = [
        remote(small_sent, small.at[x], send_small.at[d], recv_small.at[d], peer)
        for d, peer in enumerate(peers)
    ]
    scatters = [
        remote(sent.at[rows(peer)], got.at[d], send_rs.at[d], recv_rs.at[d], peer)
        for d, peer in enumerate(peers)
    ]
    for copy in smalls + scatters:
        copy.start()
    small[x] = small_sent[...]
    for copy in smalls:
        copy.wait()
    total = (small[0] + small[1]) + (small[2] + small[3])
    bias[...] = total[8:9, 0:1]
    decoder_got[me] = total[0:8]

    def spread(d, carry):
        peer = lax.rem(me + d, BRICKS)
        to_brick(decoder_got.at[me], decoder_got.at[me], send_dec, recv_dec, d, peer).start()
        return carry

    lax.fori_loop(1, BRICKS, spread, 0)
    for copy in scatters:
        copy.wait()
    summed = packed[rows(x), :]
    for d in range(BATCH - 1):
        summed = summed + got[d].astype(F32)
    whole[rows(x), :] = summed.astype(BF16)
    gathers = [
        remote(whole.at[rows(x)], whole.at[rows(x)], send_ag.at[d], recv_ag.at[d], peer)
        for d, peer in enumerate(peers)
    ]
    for copy in gathers:
        copy.start()

    def spread_wait(d, carry):
        peer = lax.rem(me + d, BRICKS)
        to_brick(decoder_got.at[me], decoder_got.at[me], send_dec, recv_dec, d, peer).wait()
        return carry

    lax.fori_loop(1, BRICKS, spread_wait, 0)
    for j in range(8):
        decoder_in[8 * j : 8 * j + 8, 0:128] = decoder_got[j]
        decoder_in[8 * j : 8 * j + 8, 128:256] = decoder_got[8 + j]
    last = decoder_got[16]
    decoder_out[:, 0:128] = last[0:3]
    decoder_out[:, 128:256] = last[3:6]
    objective[...] = last[6:7, 0:1]
    for copy in gathers:
        copy.wait()
    wide = STRIPE * G
    for h in range(STRIPES):
        parts = [
            whole[wide * p : wide * p + wide, COMP * h : COMP * h + COMP].astype(F32)
            for p in range(3)
        ]
        planes[0, wide * h : wide * h + wide, :] = jnp.concatenate(parts, axis=1)
    at = 3 * wide
    one[0] = whole[at : at + VM, 0:128].astype(F32)
    two[0] = whole[at : at + HID, 128:256].astype(F32)
    block = whole[at : at + HID, 256:384]
    out[0] = block[:, :FEAT].astype(F32)
    pick = jnp.where((iota((8, 128), 0) == 0) & (iota((8, 128), 1) == FEAT), 1.0, 0.0)
    head[...] = nt(pick.astype(BF16), block)[0:1]
    block = block.astype(F32)
    lines[0] = jnp.concatenate([block[G * p : G * p + G, AUG:] for p in range(3)], axis=1)


def shape(dims, kind=F32):
    return jax.ShapeDtypeStruct(dims, kind)


def on_device(
    crossings,
    lattice,
    offsets,
    target,
    planes,
    line_factors,
    layer_one,
    layer_two,
    layer_out,
    density_head,
    density_bias,
    decoder_in,
    decoder_out,
):
    dma = pltpu.SemaphoreType.DMA
    (
        positions,
        ray_slots,
        slot_cross,
        plane_t,
        line_t,
        one_t,
        two_t,
        out_t,
        out_aug,
    ) = pl.pallas_call(
        rays_to_bricks,
        out_shape=(
            shape((BRICKS, 8, 128)),
            shape((RAYS, SLOTS), BF16),
            shape((8, SLOTS)),
            shape((3, WIDE, LOCAL), BF16),
            shape((VM, 128), BF16),
            shape((HID, VM), BF16),
            shape((HID, HID), BF16),
            shape((AUG, HID), BF16),
            shape((HID, AUG), BF16),
        ),
        in_specs=[VMEM_SPEC] * 9,
        out_specs=[VMEM_SPEC] * 9,
        scratch_shapes=[
            pltpu.VMEM((BRICKS, 8, 128), F32),
            pltpu.VMEM((BRICKS, 8, 128), F32),
            dma((BRICKS,)),
            dma((BRICKS,)),
        ],
        compiler_params=pltpu.CompilerParams(collective_id=0, has_side_effects=True),
        name="rays_to_bricks",
    )(
        crossings,
        lattice,
        offsets,
        planes,
        line_factors,
        layer_one,
        layer_two,
        layer_out,
        density_head,
    )

    def whole(*dims):
        return pl.BlockSpec(dims, lambda i: (0,) * len(dims))

    def lanes(rows):
        return pl.BlockSpec((rows, CHUNK), lambda i: (0, i))

    def by_peer(rows):
        return pl.BlockSpec((PEERS, rows, 128), lambda i: (i, 0, 0))

    saved_rows = (VM, VM, VM, HID, HID, HID, HID, FEAT)
    saved_specs = [lanes(rows) for rows in saved_rows] + [lanes(8)]
    message, *saved = pl.pallas_call(
        brick_forward,
        grid=(CHUNKS,),
        out_shape=[shape((BRICKS, MSG, 128), BF16)]
        + [shape((rows, SAMPLES), BF16) for rows in saved_rows]
        + [shape((8, SAMPLES))],
        in_specs=[
            by_peer(8),
            whole(3, WIDE, LOCAL),
            whole(VM, 128),
            whole(HID, VM),
            whole(HID, HID),
            whole(AUG, HID),
            SMEM_SPEC,
        ],
        out_specs=[by_peer(MSG)] + saved_specs,
        name="brick_forward",
    )(positions, plane_t, line_t, one_t, two_t, out_t, density_bias)

    back, decoder_sum = pl.pallas_call(
        rays_train,
        out_shape=(shape((BRICKS, MSG, 128), BF16), shape((8, 128))),
        in_specs=[VMEM_SPEC] * 6,
        out_specs=[VMEM_SPEC] * 2,
        scratch_shapes=[
            pltpu.VMEM((BRICKS, MSG, 128), BF16),
            pltpu.VMEM((BRICKS, MSG, 128), BF16),
            pltpu.VMEM((BRICKS, MSG, 128), BF16),
            pltpu.VMEM((BRICKS, 8, 128), F32),
            pltpu.VMEM((BRICKS, 8, 128), F32),
            pltpu.VMEM((8, 128), F32),
            pltpu.VMEM((FEAT, SLOTS), F32),
        ]
        + [dma((BRICKS,))] * 6,
        compiler_params=pltpu.CompilerParams(collective_id=1, has_side_effects=True),
        name="rays_train",
    )(message, ray_slots, slot_cross, target, decoder_in, decoder_out)

    packed, bias_grad = pl.pallas_call(
        brick_backward,
        grid=(CHUNKS,),
        out_shape=(shape((PACK, WIDE)), shape((8, 128))),
        in_specs=[by_peer(8), by_peer(MSG)]
        + saved_specs
        + [whole(1, VM, HID), whole(1, HID, HID), whole(HID, AUG)],
        out_specs=[whole(PACK, WIDE), whole(8, 128)],
        scratch_shapes=[
            pltpu.VMEM((3, LOCAL, WIDE), F32),
            pltpu.VMEM((128, VM), F32),
            pltpu.VMEM((VM, HID), F32),
            pltpu.VMEM((HID, HID), F32),
            pltpu.VMEM((HID, AUG), F32),
            pltpu.VMEM((8, 128), F32),
        ],
        name="brick_backward",
    )(positions, back, *saved, layer_one, layer_two, out_aug)

    outs = pl.pallas_call(
        add_up,
        out_shape=(
            shape((1, G * G, VM)),
            shape((1, G, VM)),
            shape((1, VM, HID)),
            shape((1, HID, HID)),
            shape((1, HID, FEAT)),
            shape((1, HID)),
            shape((1, 1)),
            shape((FEAT, DEC)),
            shape((3, DEC)),
            shape((1, 1)),
        ),
        in_specs=[VMEM_SPEC] * 3,
        out_specs=[VMEM_SPEC] * 10,
        scratch_shapes=[
            pltpu.VMEM((PACK, WIDE), BF16),
            pltpu.VMEM((BATCH - 1, SHARD, WIDE), BF16),
            pltpu.VMEM((PACK, WIDE), BF16),
            pltpu.VMEM((BATCH, 16, 128), F32),
            pltpu.VMEM((16, 128), F32),
            pltpu.VMEM((BRICKS, 8, 128), F32),
        ]
        + [dma((BATCH - 1,))] * 6
        + [dma((BRICKS,))] * 2,
        compiler_params=pltpu.CompilerParams(collective_id=2, has_side_effects=True),
        name="add_up",
    )(packed, decoder_sum, bias_grad)
    outs = list(outs)
    outs[6] = outs[6].reshape(1)
    outs[9] = outs[9].reshape(())
    return tuple(outs)


def solution(mesh):
    placed = (
        P(("brick", "batch"), None),
        P(None, None, None, ("brick", "batch")),
        P(None, None, None, ("brick", "batch")),
        P(None, ("brick", "batch")),
        P("brick", None, None),
        P("brick", None, None),
        P("brick", None, None),
        P("brick", None, None),
        P("brick", None, None),
        P("brick", None),
        P("brick"),
        P(),
        P(),
    )
    return jax.shard_map(
        on_device,
        mesh=mesh,
        in_specs=placed,
        out_specs=(
            P("brick", None, None),
            P("brick", None, None),
            P("brick", None, None),
            P("brick", None, None),
            P("brick", None, None),
            P("brick", None),
            P("brick"),
            P(),
            P(),
            P(),
        ),
        check_vma=False,
    )
```

```python
import jax
import jax.numpy as jnp
from jax import lax
from jax.experimental import pallas as pl
from jax.experimental.pallas import tpu as pltpu
from jax.sharding import PartitionSpec as P

STEP_LENGTH = 0.1
MESH = pl.DeviceIdType.MESH
F32 = jnp.float32
BF16 = jnp.bfloat16

BRICKS = 32
BATCH = 4
RAYS = 128
CROSS = 8
CAP = 64
SLOTS = BRICKS * CAP
G = 40
VM = 144
COMP = 48
HID = 128
FEAT = 64
AUG = 80
DEC = 256
STRIPE = 5
STRIPES = 8
LOCAL = (STRIPE + 1) * G
WIDE = STRIPES * COMP
PEERS = 4
CHUNK = PEERS * 256
CHUNKS = BRICKS // PEERS
SAMPLES = BRICKS * CAP * 4
MSG = 40
HALF = FEAT // 2
UNITS = (48, 80, 80, 80)
BASES = (0, 384, 1024, 1664)
PACK = 2304
PAIRS = ((0, 1, 2), (0, 2, 1), (1, 2, 0))
VMEM_SPEC = pl.BlockSpec(memory_space=pltpu.VMEM)
SMEM_SPEC = pl.BlockSpec(memory_space=pltpu.SMEM)


def mm(a, b):
    return lax.dot_general(a, b, (((1,), (0,)), ((), ())), preferred_element_type=F32)


def nt(a, b):
    return lax.dot_general(a, b, (((1,), (1,)), ((), ())), preferred_element_type=F32)


def tn(a, b):
    return lax.dot_general(a, b, (((0,), (0,)), ((), ())), preferred_element_type=F32)


def split3(x):
    one = x.astype(BF16)
    rest = x - one.astype(F32)
    two = rest.astype(BF16)
    three = (rest - two.astype(F32)).astype(BF16)
    return one, two, three


def iota(shape, axis, kind=jnp.int32):
    return lax.broadcasted_iota(jnp.int32, shape, axis).astype(kind)


def eye(n):
    return jnp.where(iota((n, n), 0) == iota((n, n), 1), 1.0, 0.0).astype(BF16)


def sigmoid(v):
    return 0.5 * jnp.tanh(0.5 * v) + 0.5


def low_half(shape):
    return iota(shape, len(shape) - 1) < CAP


def swap(x):
    return pltpu.roll(x, CAP, 1)


def hat(x):
    return jnp.maximum(0.0, 1.0 - jnp.abs(x))


def place_rays(crossings, lattice, offsets, ray_slots, slot_cross, sent):
    named = crossings[...]
    brick_row = iota((BRICKS, RAYS), 0)
    crosses = jnp.zeros((BRICKS, RAYS), F32)
    order = jnp.zeros((BRICKS, RAYS), F32)
    for k in range(CROSS):
        hit = jnp.where(named[k : k + 1, :] == brick_row, 1.0, 0.0)
        crosses = crosses + hit
        order = order + float(k) * hit
    before = jnp.where(iota((RAYS, RAYS), 0) < iota((RAYS, RAYS), 1), 1.0, 0.0).astype(BF16)
    rank = mm(crosses.astype(BF16), before)
    rank = jnp.where(crosses > 0.0, rank, -1.0)
    lane = iota((BRICKS, SLOTS), 1)
    first = iota((BRICKS, SLOTS), 0) * CAP
    spread = jnp.where((lane >= first) & (lane < first + CAP), 1.0, 0.0).astype(BF16)
    place = (iota((RAYS, SLOTS), 1) & (CAP - 1)).astype(F32)
    chosen = jnp.where(tn(rank.astype(BF16), spread) == place, 1.0, 0.0)
    order_wide = tn(order.astype(BF16), spread)
    cross_of = jnp.sum(chosen * order_wide, axis=0, keepdims=True)
    chosen = chosen.astype(BF16)
    ray_slots[...] = chosen
    slot_cross[...] = jnp.broadcast_to(cross_of, (8, SLOTS))
    pad = jnp.zeros((2, RAYS), F32)
    rows = []
    for k in range(CROSS):
        for odd in range(2):
            for c in range(3):
                for half in range(2):
                    s = 2 * half + odd
                    rows.append(
                        lattice[c, k, s : s + 1, :].astype(F32) + offsets[c, k, s : s + 1, :]
                    )
            rows.append(pad)
    stacked = jnp.concatenate(split3(jnp.concatenate(rows, axis=0)), axis=0)
    height = CROSS * 16
    moved = mm(stacked, chosen)
    moved = moved[:height] + moved[height : 2 * height] + moved[2 * height :]
    picked = jnp.zeros((16, SLOTS), F32)
    for k in range(CROSS):
        picked = jnp.where(cross_of == float(k), moved[16 * k : 16 * k + 16], picked)
    low = low_half((8, 128))
    for tile in range(BRICKS // 2):
        x = picked[:, 128 * tile : 128 * tile + 128]
        even, odd = x[:8], x[8:]
        sent[2 * tile] = jnp.where(low, even, swap(odd))
        sent[2 * tile + 1] = jnp.where(low, swap(even), odd)


def turn_weights(
    planes,
    line_factors,
    layer_one,
    layer_two,
    layer_out,
    density_head,
    plane_t,
    line_t,
    one_t,
    two_t,
    out_t,
    out_aug,
):
    for h in range(STRIPES):
        at = STRIPE * G * h
        width = min(LOCAL, G * G - at)
        part = planes[0, :, at : at + width]
        if width < LOCAL:
            part = jnp.concatenate([part, jnp.zeros((VM, LOCAL - width), BF16)], axis=1)
        for p in range(3):
            plane_t[p, COMP * h : COMP * h + COMP, :] = part[COMP * p : COMP * p + COMP]
    turned = nt(eye(VM), line_factors[0])
    wide = jnp.concatenate([turned, turned, turned, jnp.zeros((VM, 8), F32)], axis=1)
    row, column = iota((VM, 128), 0), iota((VM, 128), 1)
    keep = (
        ((row < 48) & (column < 40))
        | ((row >= 48) & (row < 96) & (column >= 40) & (column < 80))
        | ((row >= 96) & (column >= 80) & (column < 120))
    )
    line_t[...] = jnp.where(keep, wide, 0.0).astype(BF16)
    unit = eye(HID)
    one_t[...] = nt(unit, layer_one[0]).astype(BF16)
    two_t[...] = nt(unit, layer_two[0]).astype(BF16)
    rows = [
        layer_out[0].astype(F32),
        density_head[...].astype(F32),
        jnp.zeros((AUG - FEAT - 1, HID), F32),
    ]
    both = jnp.concatenate(rows, axis=0).astype(BF16)
    out_t[...] = both
    out_aug[...] = nt(unit, both).astype(BF16)


def coordinate(positions, peers, c):
    parts = [
        positions[p, 2 * c + half : 2 * c + half + 1, :] for p in peers for half in range(2)
    ]
    return jnp.concatenate(parts, axis=1)


def stripe_weights(along, other_hat):
    stripe = jnp.floor(along * (1.0 / STRIPE))
    local = along - float(STRIPE) * stripe
    near = hat(local - iota((8, CHUNK), 0, F32))
    weights = jnp.concatenate(
        [near[i : i + 1] * other_hat for i in range(STRIPE + 1)], axis=0
    ).astype(BF16)
    return stripe, weights


def line_table(hats):
    rows = [hats[PAIRS[p][2]] for p in range(3)] + [jnp.zeros((8, CHUNK), F32)]
    return jnp.concatenate(rows, axis=0).astype(BF16)


def within_crossing(zeta, peer):
    low = low_half((1, 128))
    depths = []
    for half in range(2):
        at = 256 * peer + 128 * half
        z = zeta[:, at : at + 128]
        density = jnp.maximum(z, 0.0) + jnp.log1p(jnp.exp(-jnp.abs(z)))
        depths.append(STEP_LENGTH * density.astype(BF16).astype(F32))
    d0, d1 = depths
    r0, r1 = swap(d0), swap(d1)
    both = d0 + r0
    b0 = jnp.where(low, 0.0, r0)
    b1 = both + jnp.where(low, 0.0, r1)
    total = both + (d1 + r1)
    return (d0, d1), (b0, b1), total


def by_cross(row, cross_mask, ray_slots):
    out = nt(jnp.concatenate(split3(row * cross_mask), axis=0), ray_slots)
    return out[0:8] + out[8:16] + out[16:24]


def to_slots(table, cross_mask, ray_slots):
    out = mm(jnp.concatenate(split3(table), axis=0), ray_slots)
    out = out[0:8] + out[8:16] + out[16:24]
    return jnp.sum(out * cross_mask, axis=0, keepdims=True)


class Brick:
    def __init__(self):
        self.me = lax.axis_index("brick")
        self.z = self.me // 8
        self.y = lax.rem(self.me // 2, 4)
        self.core = lax.rem(self.me, 2)

    def peer(self, q, j, sign=1):
        dz = jnp.minimum(q, CHUNKS - 1 - q)
        dy = 2 * (1 - q // 4) + j // 2
        z = lax.rem(self.z + sign * dz + 4, 4)
        y = lax.rem(self.y + sign * dy + 4, 4)
        return (z * 4 + y) * 2 + lax.rem(self.core + j % 2, 2)


class Exchange:
    def __init__(self, me, sent, got, send_sem, recv_sem):
        self.me, self.sent, self.got = me, sent, got
        self.send_sem, self.recv_sem = send_sem, recv_sem

    def copy(self, peer, slot):
        return pltpu.make_async_remote_copy(
            src_ref=self.sent.at[peer],
            dst_ref=self.got.at[slot],
            send_sem=self.send_sem.at[peer],
            recv_sem=self.recv_sem.at[slot],
            device_id={"brick": peer},
            device_id_type=MESH,
        )

    def send(self, peer):
        self.copy(peer, self.me).start()

    def receive(self, peer):
        self.copy(peer, peer).wait_recv()

    def others(self, act):
        def one(d, carry):
            act(lax.rem(self.me + d, BRICKS))
            return carry

        lax.fori_loop(1, BRICKS, one, 0)

    def sends_done(self):
        self.others(lambda peer: self.copy(peer, self.me).wait_send())


def train(
    crossings,
    lattice,
    offsets,
    target,
    planes,
    line_factors,
    layer_one,
    layer_two,
    layer_out,
    density_head,
    bias,
    decoder_in,
    decoder_out,
    whole_out,
    decoder_sums,
    small_sums,
    pos_sent,
    pos_got,
    msg_sent,
    msg_got,
    back_sent,
    back_got,
    dec_sent,
    dec_got,
    dec_all,
    small_sent,
    small_got,
    ray_slots_ref,
    slot_cross,
    plane_t,
    line_t,
    one_t,
    two_t,
    out_t,
    out_aug,
    vm_s,
    plane_s,
    line_s,
    h1_s,
    s1_s,
    h2_s,
    s2_s,
    feat_s,
    zeta_s,
    gathered,
    acc_planes,
    acc_lines,
    acc_one,
    acc_two,
    acc_out,
    acc_bias,
    own,
    first_got,
    second,
    second_got,
    whole,
    pos_ss,
    pos_rs,
    msg_ss,
    msg_rs,
    back_ss,
    back_rs,
    dec_ss,
    dec_rs,
    all_ss,
    all_rs,
    small_ss,
    small_rs,
    sum_ss,
    sum_rs,
):
    at = Brick()
    me = at.me
    x = lax.axis_index("batch")
    x_peers = [lax.rem(x + d, BATCH) for d in range(1, BATCH)]
    barrier = pltpu.get_barrier_semaphore()

    def greet(d, carry):
        pl.semaphore_signal(
            barrier, inc=1, device_id={"brick": lax.rem(me + d, BRICKS)}, device_id_type=MESH
        )
        return carry

    lax.fori_loop(1, BRICKS, greet, 0)
    for peer in x_peers:
        pl.semaphore_signal(barrier, inc=1, device_id={"batch": peer}, device_id_type=MESH)

    pos = Exchange(me, pos_sent, pos_got, pos_ss, pos_rs)
    msg = Exchange(me, msg_sent, msg_got, msg_ss, msg_rs)
    back = Exchange(me, back_sent, back_got, back_ss, back_rs)
    dec = Exchange(me, dec_sent, dec_got, dec_ss, dec_rs)

    def send_near_first(exchange):
        def one(i, carry):
            for j in range(PEERS):
                peer = at.peer(CHUNKS - 1 - i, j, -1)

                @pl.when(peer != me)
                def _():
                    exchange.send(peer)

            return carry

        lax.fori_loop(0, CHUNKS, one, 0)

    place_rays(crossings, lattice, offsets, ray_slots_ref, slot_cross, pos_sent)
    pl.semaphore_wait(barrier, BRICKS - 1 + BATCH - 1)
    send_near_first(pos)
    pos_got[me] = pos_sent[me]
    turn_weights(
        planes,
        line_factors,
        layer_one,
        layer_two,
        layer_out,
        density_head,
        plane_t,
        line_t,
        one_t,
        two_t,
        out_t,
        out_aug,
    )
    for ref in (acc_lines, acc_one, acc_two, acc_out, acc_bias, dec_sent):
        ref[...] = jnp.zeros_like(ref)

    def forward(q, carry):
        peers = [at.peer(q, j) for j in range(PEERS)]
        for p in peers:

            @pl.when(p != me)
            def _():
                pos.receive(p)

        lanes = pl.ds(pl.multiple_of(q * CHUNK, CHUNK), CHUNK)
        coords = [coordinate(pos_got, peers, c) for c in range(3)]
        points = iota((G, CHUNK), 0, F32)
        hats = [hat(coord - points) for coord in coords]
        values = []
        for pair in range(3):
            a, b, line = PAIRS[pair]
            stripe, weights = stripe_weights(coords[a], hats[b])
            wide = mm(plane_t[pair], weights)
            value = wide[:COMP]
            for h in range(1, STRIPES):
                value = jnp.where(stripe == float(h), wide[COMP * h : COMP * h + COMP], value)
            values.append(value)
        plane_value = jnp.concatenate(values, axis=0)
        line_value = mm(line_t[...], line_table(hats))
        vm = (plane_value * line_value).astype(BF16)
        vm_s[:, lanes] = vm
        plane_s[:, lanes] = plane_value.astype(BF16)
        line_s[:, lanes] = line_value.astype(BF16)
        a1 = mm(one_t[...], vm)
        g1 = sigmoid(a1)
        v1 = a1 * g1
        h1 = v1.astype(BF16)
        h1_s[:, lanes] = h1
        s1_s[:, lanes] = (g1 + v1 * (1.0 - g1)).astype(BF16)
        a2 = mm(two_t[...], h1)
        g2 = sigmoid(a2)
        v2 = a2 * g2
        h2 = v2.astype(BF16)
        h2_s[:, lanes] = h2
        s2_s[:, lanes] = (g2 + v2 * (1.0 - g2)).astype(BF16)
        wide = mm(out_t[...], h2)
        feat = wide[:FEAT].astype(BF16)
        feat_s[:, lanes] = feat
        zeta = wide[FEAT : FEAT + 1] + bias[0]
        zeta_s[:, lanes] = jnp.broadcast_to(zeta, (8, CHUNK))
        low = low_half((HALF, 128))
        for j, p in enumerate(peers):
            depths, befores, total = within_crossing(zeta, j)
            summed = jnp.zeros((FEAT, 128), F32)
            for half in range(2):
                weight = jnp.exp(-befores[half]) * (1.0 - jnp.exp(-depths[half]))
                lane = 256 * j + 128 * half
                summed = summed + weight * feat[:, lane : lane + 128].astype(F32)
            summed = summed + swap(summed)
            folded = jnp.where(low, summed[:HALF], summed[HALF:])
            parts = [part.astype(F32) for part in split3(total)]
            rows = [folded] + parts + [jnp.zeros((MSG - HALF - 3, 128), F32)]
            msg_sent[p] = jnp.concatenate(rows, axis=0).astype(BF16)

            @pl.when(p != me)
            def _():
                msg.send(p)

        return carry

    lax.fori_loop(0, CHUNKS, forward, 0)
    msg_got[me] = msg_sent[me]

    ray_slots = ray_slots_ref[...]
    cross_mask = jnp.where(slot_cross[...] == iota((8, SLOTS), 0, F32), 1.0, 0.0)
    low = low_half((HALF, 128))
    low_row = low_half((1, 128))
    low8 = low_half((8, 128))
    msg.others(msg.receive)
    depth_rows = []
    for tile in range(BRICKS // 2):
        even, odd = msg_got[2 * tile].astype(F32), msg_got[2 * tile + 1].astype(F32)
        e, o = even[:HALF], odd[:HALF]
        lanes = slice(128 * tile, 128 * tile + 128)
        gathered[:HALF, lanes] = jnp.where(low, e, swap(o))
        gathered[HALF:, lanes] = jnp.where(low, swap(e), o)
        e = even[HALF : HALF + 1] + even[HALF + 1 : HALF + 2] + even[HALF + 2 : HALF + 3]
        o = odd[HALF : HALF + 1] + odd[HALF + 1 : HALF + 2] + odd[HALF + 2 : HALF + 3]
        depth_rows.append(jnp.where(low_row, e, o))
    depth = jnp.concatenate(depth_rows, axis=1)
    by_ray = by_cross(depth, cross_mask, ray_slots)
    running = jnp.zeros((1, RAYS), F32)
    befores = []
    for k in range(CROSS):
        befores.append(running)
        running = running + by_ray[k : k + 1]
    enter = to_slots(jnp.exp(-jnp.concatenate(befores, axis=0)), cross_mask, ray_slots)
    partials = gathered[...]
    scaled = partials * enter
    high = scaled.astype(BF16)
    rest = (scaled - high.astype(F32)).astype(BF16)
    composite = nt(jnp.concatenate([high, rest], axis=0), ray_slots)
    composite = (composite[:FEAT] + composite[FEAT:]).astype(BF16)
    decoder_pre = tn(decoder_in[...], composite)
    gate = sigmoid(decoder_pre)
    decoder_hidden = (decoder_pre * gate).astype(BF16)
    logits = mm(decoder_out[...], decoder_hidden)
    colors = sigmoid(logits)
    errors = colors - target[...]
    scale = float(RAYS * BRICKS * BATCH) ** (-0.5)
    grad_logits = (2.0 * scale * errors * colors * (1.0 - colors)).astype(BF16)
    back_decoder = tn(decoder_out[...], grad_logits)
    grad_pre = (back_decoder * (gate * (1.0 + decoder_pre * (1.0 - gate)))).astype(BF16)
    grad_composite = mm(decoder_in[...], grad_pre).astype(BF16)
    grad_slots = mm(grad_composite, ray_slots)
    along = jnp.sum(partials * grad_slots, axis=0, keepdims=True) * enter
    by_ray = by_cross(along, cross_mask, ray_slots)
    running = jnp.zeros((1, RAYS), F32)
    laters = []
    for k in reversed(range(CROSS)):
        laters.insert(0, running)
        running = running + by_ray[k : k + 1]
    later = to_slots(jnp.concatenate(laters, axis=0), cross_mask, ray_slots)
    for tile in range(BRICKS // 2):
        lanes = slice(128 * tile, 128 * tile + 128)
        top, bottom = grad_slots[:HALF, lanes], grad_slots[HALF:, lanes]
        scalars = [part.astype(F32) for part in split3(enter[:, lanes]) + split3(later[:, lanes])]
        scalars = jnp.concatenate(scalars + [jnp.zeros((2, 128), F32)], axis=0)
        turned = swap(scalars)
        rows = [jnp.where(low, top, swap(bottom)), jnp.where(low8, scalars, turned)]
        back_sent[2 * tile] = jnp.concatenate(rows, axis=0).astype(BF16)
        rows = [jnp.where(low, swap(top), bottom), jnp.where(low8, turned, scalars)]
        back_sent[2 * tile + 1] = jnp.concatenate(rows, axis=0).astype(BF16)
    send_near_first(back)
    back_got[me] = back_sent[me]

    objective = scale * jnp.sum(errors * errors)
    grad_out = nt(grad_logits, decoder_hidden)
    grad_in = nt(composite, grad_pre)
    for j in range(8):
        dec_sent[j] = grad_in[8 * j : 8 * j + 8, :128]
        dec_sent[8 + j] = grad_in[8 * j : 8 * j + 8, 128:]
    rows = [grad_out[:, :128], grad_out[:, 128:], jnp.full((2, 128), objective, F32)]
    dec_sent[16] = jnp.concatenate(rows, axis=0)
    dec.others(dec.send)
    dec_got[me] = dec_sent[me]

    def backward(i, carry):
        q = CHUNKS - 1 - i
        peers = [at.peer(q, j) for j in range(PEERS)]
        for p in peers:

            @pl.when(p != me)
            def _():
                back.receive(p)

        lanes = pl.ds(pl.multiple_of(q * CHUNK, CHUNK), CHUNK)
        zeta = zeta_s[0:1, lanes]
        feat = feat_s[:, lanes].astype(F32)
        grad_feats, grad_zetas = [], []
        for j, p in enumerate(peers):
            depths, befores, total = within_crossing(zeta, j)
            got = back_got[p].astype(F32)
            m = got[:HALF]
            turned = swap(m)
            grads = jnp.concatenate([jnp.where(low, m, turned), jnp.where(low, turned, m)], axis=0)
            enter = got[HALF : HALF + 1] + got[HALF + 1 : HALF + 2] + got[HALF + 2 : HALF + 3]
            later = got[HALF + 3 : HALF + 4] + got[HALF + 4 : HALF + 5] + got[HALF + 5 : HALF + 6]
            carried, lit = [], []
            for half in range(2):
                lane = 256 * j + 128 * half
                transmit = enter * jnp.exp(-befores[half])
                survive = jnp.exp(-depths[half])
                weight = transmit * (1.0 - survive)
                grad_weight = jnp.sum(grads * feat[:, lane : lane + 128], axis=0, keepdims=True)
                grad_feats.append(weight * grads)
                carried.append(grad_weight * weight)
                lit.append(grad_weight * transmit * survive)
            c0, c1 = carried
            r0, r1 = swap(c0), swap(c1)
            laters = (
                jnp.where(low_row, r0, 0.0) + (c1 + r1) + later,
                jnp.where(low_row, r1, 0.0) + later,
            )
            for half in range(2):
                lane = 256 * j + 128 * half
                grad_density = (STEP_LENGTH * (lit[half] - laters[half])).astype(BF16)
                gate = sigmoid(zeta[:, lane : lane + 128])
                grad_zetas.append((grad_density.astype(F32) * gate).astype(BF16).astype(F32))
        grad_zeta = jnp.concatenate(grad_zetas, axis=1)
        acc_bias[...] += jnp.full((8, 128), jnp.sum(grad_zeta), F32)
        rows = [jnp.concatenate(grad_feats, axis=1), grad_zeta]
        rows.append(jnp.zeros((AUG - FEAT - 1, CHUNK), F32))
        grad_aug = jnp.concatenate(rows, axis=0).astype(BF16)
        acc_out[...] += nt(grad_aug, h2_s[:, lanes])
        grad_a2 = (mm(out_aug[...], grad_aug) * s2_s[:, lanes].astype(F32)).astype(BF16)
        acc_two[...] += nt(h1_s[:, lanes], grad_a2)
        grad_a1 = (mm(layer_two[0], grad_a2) * s1_s[:, lanes].astype(F32)).astype(BF16)
        acc_one[...] += nt(vm_s[:, lanes], grad_a1)
        grad_vm = mm(layer_one[0], grad_a1)
        grad_line = (grad_vm * plane_s[:, lanes].astype(F32)).astype(BF16)
        line_s[:, lanes] = (grad_vm * line_s[:, lanes].astype(F32)).astype(BF16)
        points = iota((G, CHUNK), 0, F32)
        hats = [hat(coordinate(pos_got, peers, c) - points) for c in range(3)]
        acc_lines[...] += nt(grad_line, line_table(hats))
        return carry

    lax.fori_loop(0, CHUNKS, backward, 0)

    partner_a = x + 1 - 2 * lax.rem(x, 2)
    partner_b = BATCH - 1 - x
    keep_a = lax.rem((x + 1) // 2, 2)
    keep_b = x // 2
    partners = (partner_a, partner_b)
    keeps = (keep_a, keep_b)

    def across(src, dst, stage, step, side, partner):
        n = (stage * 4 + step) * 2 + side
        return pltpu.make_async_remote_copy(
            src_ref=src,
            dst_ref=dst,
            send_sem=sum_ss.at[n],
            recv_sem=sum_rs.at[n],
            device_id={"batch": partner},
            device_id_type=MESH,
        )

    def span(start, size):
        return pl.ds(pl.multiple_of(start, 16), size)

    def transfer(stage, step, side):
        u, base = UNITS[stage], BASES[stage]
        start = base + 4 * u * side
        half_rows = BASES[stage] // 2 + 2 * u * side
        quarter_rows = BASES[stage] // 4 + u * side
        one, two = keeps[side], keeps[1 - side]
        near, far = partners[side], partners[1 - side]
        if step == 0:
            return across(
                own.at[span(start + 2 * u * (1 - one), 2 * u)],
                first_got.at[span(half_rows, 2 * u)],
                stage,
                step,
                side,
                near,
            )
        if step == 1:
            return across(
                second.at[span(half_rows + u * (1 - two), u)],
                second_got.at[span(quarter_rows, u)],
                stage,
                step,
                side,
                far,
            )
        if step == 2:
            rows = span(start + 2 * u * one + u * two, u)
            return across(whole.at[rows], whole.at[rows], stage, step, side, far)
        rows = span(start + 2 * u * one, 2 * u)
        return across(whole.at[rows], whole.at[rows], stage, step, side, near)

    def advance(stage, step):
        u, base = UNITS[stage], BASES[stage]
        for side in range(2):
            start = base + 4 * u * side
            half_rows = BASES[stage] // 2 + 2 * u * side
            quarter_rows = BASES[stage] // 4 + u * side
            one, two = keeps[side], keeps[1 - side]
            if step > 0:
                transfer(stage, step - 1, side).wait()
            if step == 1:
                mine = own[span(start + 2 * u * one, 2 * u), :].astype(F32)
                theirs = first_got[span(half_rows, 2 * u), :].astype(F32)
                second[span(half_rows, 2 * u), :] = (mine + theirs).astype(BF16)
            if step == 2:
                mine = second[span(half_rows + u * two, u), :].astype(F32)
                theirs = second_got[span(quarter_rows, u), :].astype(F32)
                whole[span(start + 2 * u * one + u * two, u), :] = (mine + theirs).astype(BF16)
            if step < 4:
                transfer(stage, step, side).start()

    def slot(t):
        for stage in range(4):
            if 0 <= t - stage <= 4:
                advance(stage, t - stage)

    own[0:VM, :] = acc_one[...].astype(BF16)
    own[VM : VM + HID, :] = acc_two[...].astype(BF16)
    own[VM + HID : VM + HID + FEAT, :] = acc_out[:FEAT, :].astype(BF16)
    column = iota((COMP, 128), 1)
    diagonal = jnp.where(column < G, acc_lines[:COMP, :], 0.0)
    diagonal = jnp.where((column >= G) & (column < 2 * G), acc_lines[COMP : 2 * COMP, :], diagonal)
    diagonal = jnp.where(
        (column >= 2 * G) & (column < 3 * G), acc_lines[2 * COMP :, :], diagonal
    )
    own[VM + HID + FEAT : BASES[1], :] = diagonal.astype(BF16)
    slot(0)

    dec.others(dec.receive)
    total = dec_got[0]
    for j in range(1, BRICKS):
        total = total + dec_got[j]
    small_sent[0:8] = total
    small_sent[8:16] = jnp.concatenate(
        [acc_bias[0:1, :], acc_out[FEAT : FEAT + 1, :], jnp.zeros((6, 128), F32)], axis=0
    )

    def small_copy(d, peer):
        return pltpu.make_async_remote_copy(
            src_ref=small_sent,
            dst_ref=small_got.at[x],
            send_sem=small_ss.at[d],
            recv_sem=small_rs.at[d],
            device_id={"batch": peer},
            device_id_type=MESH,
        )

    for d, peer in enumerate(x_peers):
        small_copy(d, peer).start()
    small_got[x] = small_sent[...]

    def spread_copy(peer, slot):
        return pltpu.make_async_remote_copy(
            src_ref=dec_all.at[me],
            dst_ref=dec_all.at[slot],
            send_sem=all_ss.at[peer],
            recv_sem=all_rs.at[slot],
            device_id={"brick": peer},
            device_id_type=MESH,
        )

    for pair in range(3):
        a, b, line = PAIRS[pair]
        acc_planes[...] = jnp.zeros_like(acc_planes)

        def scatter(q, carry):
            peers = [at.peer(q, j) for j in range(PEERS)]
            lanes = pl.ds(pl.multiple_of(q * CHUNK, CHUNK), CHUNK)
            points = iota((G, CHUNK), 0, F32)
            other_hat = hat(coordinate(pos_got, peers, b) - points)
            stripe, weights = stripe_weights(coordinate(pos_got, peers, a), other_hat)
            piece = line_s[COMP * pair : COMP * pair + COMP, lanes]
            masked = [
                piece * jnp.where(stripe == float(h), 1.0, 0.0).astype(BF16)
                for h in range(STRIPES)
            ]
            acc_planes[...] += nt(jnp.concatenate(masked, axis=0), weights)
            return carry

        lax.fori_loop(0, CHUNKS, scatter, 0)
        side = STRIPE * G
        acc_planes[COMP:, :G] += acc_planes[: WIDE - COMP, side:]
        turned = nt(eye(side), acc_planes[:, :side].astype(BF16)).astype(BF16)
        base = BASES[pair + 1]
        for tile in range(3):
            own[base + side * tile : base + side * tile + side, :] = turned[
                :, 128 * tile : 128 * tile + 128
            ]
        own[base + 3 * side : base + 640, :] = jnp.zeros((640 - 3 * side, 128), BF16)
        slot(pair + 1)
        if pair == 0:
            for d, peer in enumerate(x_peers):
                small_copy(d, peer).wait()
            small = (small_got[0] + small_got[1]) + (small_got[2] + small_got[3])
            small_sums[...] = small
            dec_all[me] = small[0:8]
            dec.others(lambda peer: spread_copy(peer, me).start())
    for t in range(4, 8):
        slot(t)
    dec.others(lambda peer: spread_copy(peer, peer).wait_recv())
    dec.others(lambda peer: spread_copy(peer, me).wait_send())
    for exchange in (pos, msg, back, dec):
        exchange.sends_done()
    decoder_sums[...] = dec_all[...]
    whole_out[...] = whole[...]


def unpack(
    whole,
    decoder_sums,
    small_sums,
    planes,
    lines,
    one,
    two,
    out,
    head,
    bias,
    decoder_in,
    decoder_out,
    objective,
):
    side = STRIPE * G
    unit = eye(WIDE)
    for pair in range(3):
        base = BASES[pair + 1]
        parts = [whole[base + side * t : base + side * t + side, :] for t in range(3)]
        turned = nt(unit, jnp.concatenate(parts, axis=1))
        for h in range(STRIPES):
            planes[0, COMP * pair : COMP * pair + COMP, side * h : side * h + side] = turned[
                COMP * h : COMP * h + COMP
            ]
    one[0] = whole[0:VM, :].astype(F32)
    two[0] = whole[VM : VM + HID, :].astype(F32)
    out[0] = whole[VM + HID : VM + HID + FEAT, :].astype(F32)
    block = whole[VM + HID + FEAT : BASES[1], :]
    row, column = iota((G, 128), 0), iota((G, 128), 1)
    parts = []
    for p in range(3):
        pick = jnp.where(column == row + G * p, 1.0, 0.0).astype(BF16)
        parts.append(nt(pick, block))
    lines[0] = jnp.concatenate(parts, axis=1)
    bias[...] = small_sums[8:9, 0:1]
    head[...] = small_sums[9:10, :]
    for j in range(8):
        decoder_in[8 * j : 8 * j + 8, 0:128] = decoder_sums[j]
        decoder_in[8 * j : 8 * j + 8, 128:256] = decoder_sums[8 + j]
    last = decoder_sums[16]
    decoder_out[:, 0:128] = last[0:3]
    decoder_out[:, 128:256] = last[3:6]
    objective[...] = last[6:7, 0:1]


def shape(dims, kind=F32):
    return jax.ShapeDtypeStruct(dims, kind)


def on_device(
    crossings,
    lattice,
    offsets,
    target,
    planes,
    line_factors,
    layer_one,
    layer_two,
    layer_out,
    density_head,
    density_bias,
    decoder_in,
    decoder_out,
):
    dma = pltpu.SemaphoreType.DMA
    vmem = pltpu.VMEM
    whole, decoder_sums, small_sums = pl.pallas_call(
        train,
        out_shape=(shape((PACK, 128), BF16), shape((BRICKS, 8, 128)), shape((16, 128))),
        in_specs=[VMEM_SPEC] * 10 + [SMEM_SPEC] + [VMEM_SPEC] * 2,
        out_specs=[VMEM_SPEC] * 3,
        scratch_shapes=[vmem((BRICKS, 8, 128), F32)] * 2
        + [vmem((BRICKS, MSG, 128), BF16)] * 4
        + [vmem((BRICKS, 8, 128), F32)] * 3
        + [vmem((16, 128), F32), vmem((BATCH, 16, 128), F32)]
        + [vmem((RAYS, SLOTS), BF16), vmem((8, SLOTS), F32)]
        + [
            vmem((3, WIDE, LOCAL), BF16),
            vmem((VM, 128), BF16),
            vmem((HID, VM), BF16),
            vmem((HID, HID), BF16),
            vmem((AUG, HID), BF16),
            vmem((HID, AUG), BF16),
        ]
        + [vmem((VM, SAMPLES), BF16)] * 3
        + [vmem((HID, SAMPLES), BF16)] * 4
        + [vmem((FEAT, SAMPLES), BF16), vmem((8, SAMPLES), F32)]
        + [
            vmem((FEAT, SLOTS), F32),
            vmem((WIDE, LOCAL), F32),
            vmem((VM, 128), F32),
            vmem((VM, HID), F32),
            vmem((HID, HID), F32),
            vmem((AUG, HID), F32),
            vmem((8, 128), F32),
        ]
        + [
            vmem((PACK, 128), BF16),
            vmem((PACK // 2, 128), BF16),
            vmem((PACK // 2, 128), BF16),
            vmem((PACK // 4, 128), BF16),
            vmem((PACK, 128), BF16),
        ]
        + [dma((BRICKS,))] * 10
        + [dma((BATCH - 1,))] * 2
        + [dma((32,))] * 2,
        compiler_params=pltpu.CompilerParams(collective_id=0, has_side_effects=True),
        name="train",
    )(
        crossings.T,
        lattice,
        offsets,
        target,
        jnp.swapaxes(planes, 1, 2),
        line_factors,
        layer_one,
        layer_two,
        jnp.swapaxes(layer_out, 1, 2),
        density_head,
        density_bias,
        decoder_in,
        decoder_out,
    )
    outs = pl.pallas_call(
        unpack,
        out_shape=(
            shape((1, VM, G * G)),
            shape((1, G, VM)),
            shape((1, VM, HID)),
            shape((1, HID, HID)),
            shape((1, FEAT, HID)),
            shape((1, HID)),
            shape((1, 1)),
            shape((FEAT, DEC)),
            shape((3, DEC)),
            shape((1, 1)),
        ),
        in_specs=[VMEM_SPEC] * 3,
        out_specs=[VMEM_SPEC] * 10,
        name="unpack",
    )(whole, decoder_sums, small_sums)
    outs = list(outs)
    outs[0] = jnp.swapaxes(outs[0], 1, 2)
    outs[4] = jnp.swapaxes(outs[4], 1, 2)
    outs[6] = outs[6].reshape(1)
    outs[9] = outs[9].reshape(())
    return tuple(outs)

def solution(mesh):
    placed = (
        P(("brick", "batch"), None),
        P(None, None, None, ("brick", "batch")),
        P(None, None, None, ("brick", "batch")),
        P(None, ("brick", "batch")),
        P("brick", None, None),
        P("brick", None, None),
        P("brick", None, None),
        P("brick", None, None),
        P("brick", None, None),
        P("brick", None),
        P("brick"),
        P(),
        P(),
    )
    return jax.shard_map(
        on_device,
        mesh=mesh,
        in_specs=placed,
        out_specs=(
            P("brick", None, None),
            P("brick", None, None),
            P("brick", None, None),
            P("brick", None, None),
            P("brick", None, None),
            P("brick", None),
            P("brick"),
            P(),
            P(),
            P(),
        ),
        check_vma=False,
    )
```

```python
import jax
import jax.numpy as jnp
from jax import lax
from jax.experimental import pallas as pl
from jax.experimental.pallas import tpu as pltpu
from jax.sharding import PartitionSpec as P

STEP_LENGTH = 0.1
MESH = pl.DeviceIdType.MESH
F32 = jnp.float32
BF16 = jnp.bfloat16

BRICKS = 32
BATCH = 4
RAYS = 128
CROSS = 8
CAP = 64
SLOTS = BRICKS * CAP
G = 40
VM = 144
COMP = 48
HID = 128
FEAT = 64
AUG = 80
DEC = 256
STRIPE = 5
STRIPES = 8
LOCAL = (STRIPE + 1) * G
WIDE = STRIPES * COMP
PEERS = 4
CHUNK = PEERS * 256
CHUNKS = BRICKS // PEERS
GROUP = 4
SAMPLES = BRICKS * CAP * 4
MSG = 40
HALF = FEAT // 2
UNITS = (48, 80, 80, 80)
BASES = (0, 384, 1024, 1664)
PACK = 2304
PAIRS = ((0, 1, 2), (0, 2, 1), (1, 2, 0))
VMEM_SPEC = pl.BlockSpec(memory_space=pltpu.VMEM)
SMEM_SPEC = pl.BlockSpec(memory_space=pltpu.SMEM)


def mm(a, b):
    return lax.dot_general(a, b, (((1,), (0,)), ((), ())), preferred_element_type=F32)


def nt(a, b):
    return lax.dot_general(a, b, (((1,), (1,)), ((), ())), preferred_element_type=F32)


def tn(a, b):
    return lax.dot_general(a, b, (((0,), (0,)), ((), ())), preferred_element_type=F32)


def split3(x):
    one = x.astype(BF16)
    rest = x - one.astype(F32)
    two = rest.astype(BF16)
    three = (rest - two.astype(F32)).astype(BF16)
    return one, two, three


def iota(shape, axis, kind=jnp.int32):
    return lax.broadcasted_iota(jnp.int32, shape, axis).astype(kind)


def eye(n):
    return jnp.where(iota((n, n), 0) == iota((n, n), 1), 1.0, 0.0).astype(BF16)


def sigmoid(v):
    return 0.5 * jnp.tanh(0.5 * v) + 0.5


def low_half(shape):
    return iota(shape, len(shape) - 1) < CAP


def swap(x):
    return pltpu.roll(x, CAP, 1)


def hat(x):
    return jnp.maximum(0.0, 1.0 - jnp.abs(x))


def place_rays(crossings, lattice, offsets, ray_slots, slot_cross, sent):
    named = crossings[...]
    brick_row = iota((BRICKS, RAYS), 0)
    crosses = jnp.zeros((BRICKS, RAYS), F32)
    order = jnp.zeros((BRICKS, RAYS), F32)
    for k in range(CROSS):
        hit = jnp.where(named[k : k + 1, :] == brick_row, 1.0, 0.0)
        crosses = crosses + hit
        order = order + float(k) * hit
    before = jnp.where(iota((RAYS, RAYS), 0) < iota((RAYS, RAYS), 1), 1.0, 0.0).astype(BF16)
    rank = mm(crosses.astype(BF16), before)
    rank = jnp.where(crosses > 0.0, rank, -1.0)
    lane = iota((BRICKS, SLOTS), 1)
    first = iota((BRICKS, SLOTS), 0) * CAP
    spread = jnp.where((lane >= first) & (lane < first + CAP), 1.0, 0.0).astype(BF16)
    place = (iota((RAYS, SLOTS), 1) & (CAP - 1)).astype(F32)
    chosen = jnp.where(tn(rank.astype(BF16), spread) == place, 1.0, 0.0)
    order_wide = tn(order.astype(BF16), spread)
    cross_of = jnp.sum(chosen * order_wide, axis=0, keepdims=True)
    chosen = chosen.astype(BF16)
    ray_slots[...] = chosen
    slot_cross[...] = jnp.broadcast_to(cross_of, (8, SLOTS))
    pad = jnp.zeros((2, RAYS), F32)
    rows = []
    for k in range(CROSS):
        for odd in range(2):
            for c in range(3):
                for half in range(2):
                    s = 2 * half + odd
                    rows.append(
                        lattice[c, k, s : s + 1, :].astype(F32) + offsets[c, k, s : s + 1, :]
                    )
            rows.append(pad)
    stacked = jnp.concatenate(split3(jnp.concatenate(rows, axis=0)), axis=0)
    height = CROSS * 16
    moved = mm(stacked, chosen)
    moved = moved[:height] + moved[height : 2 * height] + moved[2 * height :]
    picked = jnp.zeros((16, SLOTS), F32)
    for k in range(CROSS):
        picked = jnp.where(cross_of == float(k), moved[16 * k : 16 * k + 16], picked)
    low = low_half((8, 128))
    for tile in range(BRICKS // 2):
        x = picked[:, 128 * tile : 128 * tile + 128]
        even, odd = x[:8], x[8:]
        sent[2 * tile] = jnp.where(low, even, swap(odd))
        sent[2 * tile + 1] = jnp.where(low, swap(even), odd)


def turn_weights(
    planes,
    line_factors,
    layer_one,
    layer_two,
    layer_out,
    density_head,
    plane_t,
    line_t,
    one_t,
    two_t,
    out_t,
    out_aug,
    two_half,
):
    for h in range(STRIPES):
        at = STRIPE * G * h
        width = min(LOCAL, G * G - at)
        part = planes[0, :, at : at + width]
        if width < LOCAL:
            part = jnp.concatenate([part, jnp.zeros((VM, LOCAL - width), BF16)], axis=1)
        for p in range(3):
            plane_t[p, COMP * h : COMP * h + COMP, :] = part[COMP * p : COMP * p + COMP]
    turned = nt(eye(VM), line_factors[0])
    wide = jnp.concatenate([turned, turned, turned, jnp.zeros((VM, 8), F32)], axis=1)
    row, column = iota((VM, 128), 0), iota((VM, 128), 1)
    keep = (
        ((row < 48) & (column < 40))
        | ((row >= 48) & (row < 96) & (column >= 40) & (column < 80))
        | ((row >= 96) & (column >= 80) & (column < 120))
    )
    line_t[...] = jnp.where(keep, wide, 0.0).astype(BF16)
    unit = eye(HID)
    one_t[...] = (0.5 * nt(unit, layer_one[0])).astype(BF16)
    two_t[...] = (0.5 * nt(unit, layer_two[0])).astype(BF16)
    two_half[...] = (0.5 * layer_two[0].astype(F32)).astype(BF16)
    rows = [
        layer_out[0].astype(F32),
        density_head[...].astype(F32),
        jnp.zeros((AUG - FEAT - 1, HID), F32),
    ]
    both = jnp.concatenate(rows, axis=0).astype(BF16)
    out_t[...] = both
    out_aug[...] = (0.5 * nt(unit, both)).astype(BF16)


def coordinate(positions, peers, c):
    parts = [
        positions[p, 2 * c + half : 2 * c + half + 1, :] for p in peers for half in range(2)
    ]
    return jnp.concatenate(parts, axis=1)


def stripe_weights(along, other_hat):
    stripe = jnp.floor(along * (1.0 / STRIPE))
    local = along - float(STRIPE) * stripe
    near = hat(local - iota((8, along.shape[1]), 0, F32))
    weights = jnp.concatenate(
        [near[i : i + 1] * other_hat for i in range(STRIPE + 1)], axis=0
    ).astype(BF16)
    return stripe, weights


def line_table(hats):
    rows = [hats[PAIRS[p][2]] for p in range(3)] + [jnp.zeros((8, hats[0].shape[1]), F32)]
    return jnp.concatenate(rows, axis=0).astype(BF16)


def within_crossing(zeta, peer):
    low = low_half((1, 128))
    depths = []
    for half in range(2):
        at = 256 * peer + 128 * half
        z = zeta[:, at : at + 128]
        density = jnp.maximum(z, 0.0) + jnp.log1p(jnp.exp(-jnp.abs(z)))
        depths.append(STEP_LENGTH * density.astype(BF16).astype(F32))
    d0, d1 = depths
    r0, r1 = swap(d0), swap(d1)
    both = d0 + r0
    b0 = jnp.where(low, 0.0, r0)
    b1 = both + jnp.where(low, 0.0, r1)
    total = both + (d1 + r1)
    return (d0, d1), (b0, b1), total


def by_cross(row, cross_mask, ray_slots):
    out = nt(jnp.concatenate(split3(row * cross_mask), axis=0), ray_slots)
    return out[0:8] + out[8:16] + out[16:24]


def to_slots(table, cross_mask, ray_slots):
    out = mm(jnp.concatenate(split3(table), axis=0), ray_slots)
    out = out[0:8] + out[8:16] + out[16:24]
    return jnp.sum(out * cross_mask, axis=0, keepdims=True)


def silu_of_half(u, hidden, slope, lanes):
    t = jnp.tanh(u)
    p = 1.0 + t
    v = u * p
    h = v.astype(BF16)
    hidden[:, lanes] = h
    slope[:, lanes] = (p + v * (1.0 - t)).astype(BF16)
    return h


def together(*parts):
    parts = list(parts)
    while parts:
        parts = [part for part in parts if next(part, parts) is not parts]


class Brick:
    def __init__(self):
        self.me = lax.axis_index("brick")
        self.z = self.me // 8
        self.y = lax.rem(self.me // 2, 4)
        self.core = lax.rem(self.me, 2)

    def peer(self, q, j, sign=1):
        dz = jnp.minimum(q, CHUNKS - 1 - q)
        dy = 2 * (1 - q // 4) + j // 2
        z = lax.rem(self.z + sign * dz + 4, 4)
        y = lax.rem(self.y + sign * dy + 4, 4)
        return (z * 4 + y) * 2 + lax.rem(self.core + j % 2, 2)


class Exchange:
    def __init__(self, me, sent, got, send_sem, recv_sem):
        self.me, self.sent, self.got = me, sent, got
        self.send_sem, self.recv_sem = send_sem, recv_sem

    def copy(self, peer, slot):
        return pltpu.make_async_remote_copy(
            src_ref=self.sent.at[peer],
            dst_ref=self.got.at[slot],
            send_sem=self.send_sem.at[peer],
            recv_sem=self.recv_sem.at[slot],
            device_id={"brick": peer},
            device_id_type=MESH,
        )

    def send(self, peer):
        self.copy(peer, self.me).start()

    def receive(self, peer):
        self.copy(peer, peer).wait_recv()

    def others(self, act):
        def one(d, carry):
            act(lax.rem(self.me + d, BRICKS))
            return carry

        lax.fori_loop(1, BRICKS, one, 0)

    def sends_done(self):
        self.others(lambda peer: self.copy(peer, self.me).wait_send())


def train(
    crossings,
    lattice,
    offsets,
    target,
    planes,
    line_factors,
    layer_one,
    layer_two,
    layer_out,
    density_head,
    bias,
    decoder_in,
    decoder_out,
    whole_out,
    decoder_sums,
    small_sums,
    pos_sent,
    pos_got,
    msg_sent,
    msg_got,
    back_sent,
    back_got,
    dec_sent,
    dec_got,
    dec_all,
    small_sent,
    small_got,
    ray_slots_ref,
    slot_cross,
    plane_t,
    line_t,
    one_t,
    two_t,
    out_t,
    out_aug,
    two_half,
    vm_s,
    plane_s,
    line_s,
    h1_s,
    s1_s,
    h2_s,
    s2_s,
    feat_s,
    zeta_s,
    gathered,
    acc_planes,
    acc_lines,
    acc_one,
    acc_two,
    acc_out,
    acc_bias,
    own,
    first_got,
    second,
    second_got,
    whole,
    pos_ss,
    pos_rs,
    msg_ss,
    msg_rs,
    back_ss,
    back_rs,
    dec_ss,
    dec_rs,
    all_ss,
    all_rs,
    small_ss,
    small_rs,
    sum_ss,
    sum_rs,
):
    at = Brick()
    me = at.me
    x = lax.axis_index("batch")
    x_peers = [lax.rem(x + d, BATCH) for d in range(1, BATCH)]
    barrier = pltpu.get_barrier_semaphore()

    def greet(d, carry):
        pl.semaphore_signal(
            barrier, inc=1, device_id={"brick": lax.rem(me + d, BRICKS)}, device_id_type=MESH
        )
        return carry

    lax.fori_loop(1, BRICKS, greet, 0)
    for peer in x_peers:
        pl.semaphore_signal(barrier, inc=1, device_id={"batch": peer}, device_id_type=MESH)

    pos = Exchange(me, pos_sent, pos_got, pos_ss, pos_rs)
    msg = Exchange(me, msg_sent, msg_got, msg_ss, msg_rs)
    back = Exchange(me, back_sent, back_got, back_ss, back_rs)
    dec = Exchange(me, dec_sent, dec_got, dec_ss, dec_rs)

    def send_near_first(exchange):
        def one(i, carry):
            for j in range(PEERS):
                peer = at.peer(CHUNKS - 1 - i, j, -1)

                @pl.when(peer != me)
                def _():
                    exchange.send(peer)

            return carry

        lax.fori_loop(0, CHUNKS, one, 0)

    place_rays(crossings, lattice, offsets, ray_slots_ref, slot_cross, pos_sent)
    pl.semaphore_wait(barrier, BRICKS - 1 + BATCH - 1)
    send_near_first(pos)
    pos_got[me] = pos_sent[me]
    turn_weights(
        planes,
        line_factors,
        layer_one,
        layer_two,
        layer_out,
        density_head,
        plane_t,
        line_t,
        one_t,
        two_t,
        out_t,
        out_aug,
        two_half,
    )
    for ref in (acc_lines, acc_one, acc_two, acc_out, acc_bias, dec_sent):
        ref[...] = jnp.zeros_like(ref)

    def look_up(q):
        peers = [at.peer(q, j) for j in range(PEERS)]
        for p in peers:

            @pl.when(p != me)
            def _():
                pos.receive(p)

        lanes = pl.ds(pl.multiple_of(q * CHUNK, CHUNK), CHUNK)
        coords = [coordinate(pos_got, peers, c) for c in range(3)]
        points = iota((G, CHUNK), 0, F32)
        hats = [hat(coord - points) for coord in coords]
        line_value = mm(line_t[...], line_table(hats))
        line_s[:, lanes] = line_value.astype(BF16)
        for pair in range(3):
            a, b, line = PAIRS[pair]
            stripe, weights = stripe_weights(coords[a], hats[b])
            wide = mm(plane_t[pair], weights)
            stripe = jnp.broadcast_to(stripe, (8, CHUNK))
            masks = [stripe == float(h) for h in range(STRIPES)]
            values = []
            for r in range(0, COMP, 8):
                value = wide[r : r + 8]
                for h in range(1, STRIPES):
                    value = jnp.where(masks[h], wide[COMP * h + r : COMP * h + r + 8], value)
                values.append(value)
            value = jnp.concatenate(values, axis=0)
            rows = slice(COMP * pair, COMP * pair + COMP)
            vm_s[rows, lanes] = (value * line_value[rows]).astype(BF16)
            plane_s[rows, lanes] = value.astype(BF16)
            yield

    def network(q):
        peers = [at.peer(q, j) for j in range(PEERS)]
        lanes = pl.ds(pl.multiple_of(q * CHUNK, CHUNK), CHUNK)
        h1 = silu_of_half(mm(one_t[...], vm_s[:, lanes]), h1_s, s1_s, lanes)
        yield
        h2 = silu_of_half(mm(two_t[...], h1), h2_s, s2_s, lanes)
        wide = mm(out_t[...], h2)
        feat = wide[:FEAT].astype(BF16)
        feat_s[:, lanes] = feat
        zeta = wide[FEAT : FEAT + 1] + bias[0]
        zeta_s[:, lanes] = jnp.broadcast_to(zeta, (8, CHUNK))
        yield
        low = low_half((HALF, 128))
        for j, p in enumerate(peers):
            depths, befores, total = within_crossing(zeta, j)
            summed = jnp.zeros((FEAT, 128), F32)
            for half in range(2):
                weight = jnp.exp(-befores[half]) * (1.0 - jnp.exp(-depths[half]))
                lane = 256 * j + 128 * half
                summed = summed + weight * feat[:, lane : lane + 128].astype(F32)
            summed = summed + swap(summed)
            folded = jnp.where(low, summed[:HALF], summed[HALF:])
            parts = [part.astype(F32) for part in split3(total)]
            rows = [folded] + parts + [jnp.zeros((MSG - HALF - 3, 128), F32)]
            msg_sent[p] = jnp.concatenate(rows, axis=0).astype(BF16)
        yield
        for p in peers:

            @pl.when(p != me)
            def _():
                msg.send(p)

    def forward(q, carry):
        together(look_up(q + 1), network(q))
        return carry

    together(look_up(0))
    lax.fori_loop(0, CHUNKS - 1, forward, 0)
    together(network(CHUNKS - 1))
    msg_got[me] = msg_sent[me]

    ray_slots = ray_slots_ref[...]
    cross_mask = jnp.where(slot_cross[...] == iota((8, SLOTS), 0, F32), 1.0, 0.0)
    low = low_half((HALF, 128))
    low_row = low_half((1, 128))
    low8 = low_half((8, 128))
    msg.others(msg.receive)
    depth_rows = []
    for tile in range(BRICKS // 2):
        even, odd = msg_got[2 * tile].astype(F32), msg_got[2 * tile + 1].astype(F32)
        e, o = even[:HALF], odd[:HALF]
        lanes = slice(128 * tile, 128 * tile + 128)
        gathered[:HALF, lanes] = jnp.where(low, e, swap(o))
        gathered[HALF:, lanes] = jnp.where(low, swap(e), o)
        e = even[HALF : HALF + 1] + even[HALF + 1 : HALF + 2] + even[HALF + 2 : HALF + 3]
        o = odd[HALF : HALF + 1] + odd[HALF + 1 : HALF + 2] + odd[HALF + 2 : HALF + 3]
        depth_rows.append(jnp.where(low_row, e, o))
    depth = jnp.concatenate(depth_rows, axis=1)
    by_ray = by_cross(depth, cross_mask, ray_slots)
    running = jnp.zeros((1, RAYS), F32)
    befores = []
    for k in range(CROSS):
        befores.append(running)
        running = running + by_ray[k : k + 1]
    enter = to_slots(jnp.exp(-jnp.concatenate(befores, axis=0)), cross_mask, ray_slots)
    partials = gathered[...]
    scaled = partials * enter
    high = scaled.astype(BF16)
    rest = (scaled - high.astype(F32)).astype(BF16)
    composite = nt(jnp.concatenate([high, rest], axis=0), ray_slots)
    composite = (composite[:FEAT] + composite[FEAT:]).astype(BF16)
    decoder_pre = tn(decoder_in[...], composite)
    gate = sigmoid(decoder_pre)
    decoder_hidden = (decoder_pre * gate).astype(BF16)
    logits = mm(decoder_out[...], decoder_hidden)
    colors = sigmoid(logits)
    errors = colors - target[...]
    scale = float(RAYS * BRICKS * BATCH) ** (-0.5)
    grad_logits = (2.0 * scale * errors * colors * (1.0 - colors)).astype(BF16)
    back_decoder = tn(decoder_out[...], grad_logits)
    grad_pre = (back_decoder * (gate * (1.0 + decoder_pre * (1.0 - gate)))).astype(BF16)
    grad_composite = mm(decoder_in[...], grad_pre).astype(BF16)
    grad_slots = mm(grad_composite, ray_slots)
    along = jnp.sum(partials * grad_slots, axis=0, keepdims=True) * enter
    by_ray = by_cross(along, cross_mask, ray_slots)
    running = jnp.zeros((1, RAYS), F32)
    laters = []
    for k in reversed(range(CROSS)):
        laters.insert(0, running)
        running = running + by_ray[k : k + 1]
    later = to_slots(jnp.concatenate(laters, axis=0), cross_mask, ray_slots)
    for tile in range(BRICKS // 2):
        lanes = slice(128 * tile, 128 * tile + 128)
        top, bottom = grad_slots[:HALF, lanes], grad_slots[HALF:, lanes]
        scalars = [part.astype(F32) for part in split3(enter[:, lanes]) + split3(later[:, lanes])]
        scalars = jnp.concatenate(scalars + [jnp.zeros((2, 128), F32)], axis=0)
        turned = swap(scalars)
        rows = [jnp.where(low, top, swap(bottom)), jnp.where(low8, scalars, turned)]
        back_sent[2 * tile] = jnp.concatenate(rows, axis=0).astype(BF16)
        rows = [jnp.where(low, swap(top), bottom), jnp.where(low8, turned, scalars)]
        back_sent[2 * tile + 1] = jnp.concatenate(rows, axis=0).astype(BF16)
    send_near_first(back)
    back_got[me] = back_sent[me]

    objective = scale * jnp.sum(errors * errors)
    grad_out = nt(grad_logits, decoder_hidden)
    grad_in = nt(composite, grad_pre)
    for j in range(8):
        dec_sent[j] = grad_in[8 * j : 8 * j + 8, :128]
        dec_sent[8 + j] = grad_in[8 * j : 8 * j + 8, 128:]
    rows = [grad_out[:, :128], grad_out[:, 128:], jnp.full((2, 128), objective, F32)]
    dec_sent[16] = jnp.concatenate(rows, axis=0)
    dec.others(dec.send)
    dec_got[me] = dec_sent[me]

    def backward(i, carry):
        q = CHUNKS - 1 - i
        peers = [at.peer(q, j) for j in range(PEERS)]
        for p in peers:

            @pl.when(p != me)
            def _():
                back.receive(p)

        lanes = pl.ds(pl.multiple_of(q * CHUNK, CHUNK), CHUNK)
        zeta = zeta_s[0:1, lanes]
        feat = feat_s[:, lanes].astype(F32)
        grad_feats, grad_zetas = [], []
        for j, p in enumerate(peers):
            depths, befores, total = within_crossing(zeta, j)
            got = back_got[p].astype(F32)
            m = got[:HALF]
            turned = swap(m)
            grads = jnp.concatenate([jnp.where(low, m, turned), jnp.where(low, turned, m)], axis=0)
            enter = got[HALF : HALF + 1] + got[HALF + 1 : HALF + 2] + got[HALF + 2 : HALF + 3]
            later = got[HALF + 3 : HALF + 4] + got[HALF + 4 : HALF + 5] + got[HALF + 5 : HALF + 6]
            carried, lit = [], []
            for half in range(2):
                lane = 256 * j + 128 * half
                transmit = enter * jnp.exp(-befores[half])
                survive = jnp.exp(-depths[half])
                weight = transmit * (1.0 - survive)
                grad_weight = jnp.sum(grads * feat[:, lane : lane + 128], axis=0, keepdims=True)
                grad_feats.append(weight * grads)
                carried.append(grad_weight * weight)
                lit.append(grad_weight * transmit * survive)
            c0, c1 = carried
            r0, r1 = swap(c0), swap(c1)
            laters = (
                jnp.where(low_row, r0, 0.0) + (c1 + r1) + later,
                jnp.where(low_row, r1, 0.0) + later,
            )
            for half in range(2):
                lane = 256 * j + 128 * half
                grad_density = (STEP_LENGTH * (lit[half] - laters[half])).astype(BF16)
                gate = sigmoid(zeta[:, lane : lane + 128])
                grad_zetas.append((grad_density.astype(F32) * gate).astype(BF16).astype(F32))
        grad_zeta = jnp.concatenate(grad_zetas, axis=1)
        acc_bias[...] += jnp.full((8, 128), jnp.sum(grad_zeta), F32)
        rows = [jnp.concatenate(grad_feats, axis=1), grad_zeta]
        rows.append(jnp.zeros((AUG - FEAT - 1, CHUNK), F32))
        grad_aug = jnp.concatenate(rows, axis=0).astype(BF16)
        acc_out[...] += nt(grad_aug, h2_s[:, lanes])
        grad_a2 = (mm(out_aug[...], grad_aug) * s2_s[:, lanes].astype(F32)).astype(BF16)
        acc_two[...] += nt(h1_s[:, lanes], grad_a2)
        grad_a1 = (mm(two_half[...], grad_a2) * s1_s[:, lanes].astype(F32)).astype(BF16)
        acc_one[...] += nt(vm_s[:, lanes], grad_a1)
        grad_vm = mm(layer_one[0], grad_a1)
        grad_line = (grad_vm * plane_s[:, lanes].astype(F32)).astype(BF16)
        line_s[:, lanes] = (grad_vm * line_s[:, lanes].astype(F32)).astype(BF16)
        points = iota((G, CHUNK), 0, F32)
        hats = [hat(coordinate(pos_got, peers, c) - points) for c in range(3)]
        acc_lines[...] += nt(grad_line, line_table(hats))
        return carry

    lax.fori_loop(0, CHUNKS, backward, 0)

    partner_a = x + 1 - 2 * lax.rem(x, 2)
    partner_b = BATCH - 1 - x
    keep_a = lax.rem((x + 1) // 2, 2)
    keep_b = x // 2
    partners = (partner_a, partner_b)
    keeps = (keep_a, keep_b)

    def across(src, dst, stage, step, side, partner):
        n = (stage * 4 + step) * 2 + side
        return pltpu.make_async_remote_copy(
            src_ref=src,
            dst_ref=dst,
            send_sem=sum_ss.at[n],
            recv_sem=sum_rs.at[n],
            device_id={"batch": partner},
            device_id_type=MESH,
        )

    def span(start, size):
        return pl.ds(pl.multiple_of(start, 16), size)

    def transfer(stage, step, side):
        u, base = UNITS[stage], BASES[stage]
        start = base + 4 * u * side
        half_rows = BASES[stage] // 2 + 2 * u * side
        quarter_rows = BASES[stage] // 4 + u * side
        one, two = keeps[side], keeps[1 - side]
        near, far = partners[side], partners[1 - side]
        if step == 0:
            return across(
                own.at[span(start + 2 * u * (1 - one), 2 * u)],
                first_got.at[span(half_rows, 2 * u)],
                stage,
                step,
                side,
                near,
            )
        if step == 1:
            return across(
                second.at[span(half_rows + u * (1 - two), u)],
                second_got.at[span(quarter_rows, u)],
                stage,
                step,
                side,
                far,
            )
        if step == 2:
            rows = span(start + 2 * u * one + u * two, u)
            return across(whole.at[rows], whole.at[rows], stage, step, side, far)
        rows = span(start + 2 * u * one, 2 * u)
        return across(whole.at[rows], whole.at[rows], stage, step, side, near)

    def advance(stage, step):
        u, base = UNITS[stage], BASES[stage]
        for side in range(2):
            start = base + 4 * u * side
            half_rows = BASES[stage] // 2 + 2 * u * side
            quarter_rows = BASES[stage] // 4 + u * side
            one, two = keeps[side], keeps[1 - side]
            if step > 0:
                transfer(stage, step - 1, side).wait()
            if step == 1:
                mine = own[span(start + 2 * u * one, 2 * u), :].astype(F32)
                theirs = first_got[span(half_rows, 2 * u), :].astype(F32)
                second[span(half_rows, 2 * u), :] = (mine + theirs).astype(BF16)
            if step == 2:
                mine = second[span(half_rows + u * two, u), :].astype(F32)
                theirs = second_got[span(quarter_rows, u), :].astype(F32)
                whole[span(start + 2 * u * one + u * two, u), :] = (mine + theirs).astype(BF16)
            if step < 4:
                transfer(stage, step, side).start()

    def slot(t):
        for stage in range(4):
            if 0 <= t - stage <= 4:
                advance(stage, t - stage)

    own[0:VM, :] = acc_one[...].astype(BF16)
    own[VM : VM + HID, :] = acc_two[...].astype(BF16)
    own[VM + HID : VM + HID + FEAT, :] = acc_out[:FEAT, :].astype(BF16)
    column = iota((COMP, 128), 1)
    diagonal = jnp.where(column < G, acc_lines[:COMP, :], 0.0)
    diagonal = jnp.where((column >= G) & (column < 2 * G), acc_lines[COMP : 2 * COMP, :], diagonal)
    diagonal = jnp.where(
        (column >= 2 * G) & (column < 3 * G), acc_lines[2 * COMP :, :], diagonal
    )
    own[VM + HID + FEAT : BASES[1], :] = diagonal.astype(BF16)
    slot(0)

    dec.others(dec.receive)
    total = dec_got[0]
    for j in range(1, BRICKS):
        total = total + dec_got[j]
    small_sent[0:8] = total
    small_sent[8:16] = jnp.concatenate(
        [acc_bias[0:1, :], acc_out[FEAT : FEAT + 1, :], jnp.zeros((6, 128), F32)], axis=0
    )

    def small_copy(d, peer):
        return pltpu.make_async_remote_copy(
            src_ref=small_sent,
            dst_ref=small_got.at[x],
            send_sem=small_ss.at[d],
            recv_sem=small_rs.at[d],
            device_id={"batch": peer},
            device_id_type=MESH,
        )

    for d, peer in enumerate(x_peers):
        small_copy(d, peer).start()
    small_got[x] = small_sent[...]

    def spread_copy(peer, slot):
        return pltpu.make_async_remote_copy(
            src_ref=dec_all.at[me],
            dst_ref=dec_all.at[slot],
            send_sem=all_ss.at[peer],
            recv_sem=all_rs.at[slot],
            device_id={"brick": peer},
            device_id_type=MESH,
        )

    for pair in range(3):
        a, b, line = PAIRS[pair]
        acc_planes[...] = jnp.zeros_like(acc_planes)

        def scatter(g, carry):
            masked, weights = [], []
            for q in range(GROUP):
                q = g * GROUP + q
                peers = [at.peer(q, j) for j in range(PEERS)]
                lanes = pl.ds(pl.multiple_of(q * CHUNK, CHUNK), CHUNK)
                points = iota((G, CHUNK), 0, F32)
                other_hat = hat(coordinate(pos_got, peers, b) - points)
                stripe, weight = stripe_weights(coordinate(pos_got, peers, a), other_hat)
                piece = line_s[COMP * pair : COMP * pair + COMP, lanes]
                rows = [
                    piece * jnp.where(stripe == float(h), 1.0, 0.0).astype(BF16)
                    for h in range(STRIPES)
                ]
                masked.append(jnp.concatenate(rows, axis=0))
                weights.append(weight)
            acc_planes[...] += nt(
                jnp.concatenate(masked, axis=1), jnp.concatenate(weights, axis=1)
            )
            return carry

        lax.fori_loop(0, CHUNKS // GROUP, scatter, 0)
        side = STRIPE * G
        acc_planes[COMP:, :G] += acc_planes[: WIDE - COMP, side:]
        turned = nt(eye(side), acc_planes[:, :side].astype(BF16)).astype(BF16)
        base = BASES[pair + 1]
        for tile in range(3):
            own[base + side * tile : base + side * tile + side, :] = turned[
                :, 128 * tile : 128 * tile + 128
            ]
        own[base + 3 * side : base + 640, :] = jnp.zeros((640 - 3 * side, 128), BF16)
        slot(pair + 1)
        if pair == 0:
            for d, peer in enumerate(x_peers):
                small_copy(d, peer).wait()
            small = (small_got[0] + small_got[1]) + (small_got[2] + small_got[3])
            small_sums[...] = small
            dec_all[me] = small[0:8]
            dec.others(lambda peer: spread_copy(peer, me).start())
    for t in range(4, 8):
        slot(t)
    dec.others(lambda peer: spread_copy(peer, peer).wait_recv())
    dec.others(lambda peer: spread_copy(peer, me).wait_send())
    for exchange in (pos, msg, back, dec):
        exchange.sends_done()
    decoder_sums[...] = dec_all[...]
    whole_out[...] = whole[...]


def unpack(
    whole,
    decoder_sums,
    small_sums,
    planes,
    lines,
    one,
    two,
    out,
    head,
    bias,
    decoder_in,
    decoder_out,
    objective,
):
    side = STRIPE * G
    unit = eye(WIDE)
    for pair in range(3):
        base = BASES[pair + 1]
        parts = [whole[base + side * t : base + side * t + side, :] for t in range(3)]
        turned = nt(unit, jnp.concatenate(parts, axis=1))
        for h in range(STRIPES):
            planes[0, COMP * pair : COMP * pair + COMP, side * h : side * h + side] = turned[
                COMP * h : COMP * h + COMP
            ]
    one[0] = whole[0:VM, :].astype(F32)
    two[0] = whole[VM : VM + HID, :].astype(F32)
    out[0] = whole[VM + HID : VM + HID + FEAT, :].astype(F32)
    block = whole[VM + HID + FEAT : BASES[1], :]
    row, column = iota((G, 128), 0), iota((G, 128), 1)
    parts = []
    for p in range(3):
        pick = jnp.where(column == row + G * p, 1.0, 0.0).astype(BF16)
        parts.append(nt(pick, block))
    lines[0] = jnp.concatenate(parts, axis=1)
    bias[...] = small_sums[8:9, 0:1]
    head[...] = small_sums[9:10, :]
    for j in range(8):
        decoder_in[8 * j : 8 * j + 8, 0:128] = decoder_sums[j]
        decoder_in[8 * j : 8 * j + 8, 128:256] = decoder_sums[8 + j]
    last = decoder_sums[16]
    decoder_out[:, 0:128] = last[0:3]
    decoder_out[:, 128:256] = last[3:6]
    objective[...] = last[6:7, 0:1]


def shape(dims, kind=F32):
    return jax.ShapeDtypeStruct(dims, kind)


def on_device(
    crossings,
    lattice,
    offsets,
    target,
    planes,
    line_factors,
    layer_one,
    layer_two,
    layer_out,
    density_head,
    density_bias,
    decoder_in,
    decoder_out,
):
    dma = pltpu.SemaphoreType.DMA
    vmem = pltpu.VMEM
    whole, decoder_sums, small_sums = pl.pallas_call(
        train,
        out_shape=(shape((PACK, 128), BF16), shape((BRICKS, 8, 128)), shape((16, 128))),
        in_specs=[VMEM_SPEC] * 10 + [SMEM_SPEC] + [VMEM_SPEC] * 2,
        out_specs=[VMEM_SPEC] * 3,
        scratch_shapes=[vmem((BRICKS, 8, 128), F32)] * 2
        + [vmem((BRICKS, MSG, 128), BF16)] * 4
        + [vmem((BRICKS, 8, 128), F32)] * 3
        + [vmem((16, 128), F32), vmem((BATCH, 16, 128), F32)]
        + [vmem((RAYS, SLOTS), BF16), vmem((8, SLOTS), F32)]
        + [
            vmem((3, WIDE, LOCAL), BF16),
            vmem((VM, 128), BF16),
            vmem((HID, VM), BF16),
            vmem((HID, HID), BF16),
            vmem((AUG, HID), BF16),
            vmem((HID, AUG), BF16),
            vmem((HID, HID), BF16),
        ]
        + [vmem((VM, SAMPLES), BF16)] * 3
        + [vmem((HID, SAMPLES), BF16)] * 4
        + [vmem((FEAT, SAMPLES), BF16), vmem((8, SAMPLES), F32)]
        + [
            vmem((FEAT, SLOTS), F32),
            vmem((WIDE, LOCAL), F32),
            vmem((VM, 128), F32),
            vmem((VM, HID), F32),
            vmem((HID, HID), F32),
            vmem((AUG, HID), F32),
            vmem((8, 128), F32),
        ]
        + [
            vmem((PACK, 128), BF16),
            vmem((PACK // 2, 128), BF16),
            vmem((PACK // 2, 128), BF16),
            vmem((PACK // 4, 128), BF16),
            vmem((PACK, 128), BF16),
        ]
        + [dma((BRICKS,))] * 10
        + [dma((BATCH - 1,))] * 2
        + [dma((32,))] * 2,
        compiler_params=pltpu.CompilerParams(collective_id=0, has_side_effects=True),
        name="train",
    )(
        crossings.T,
        lattice,
        offsets,
        target,
        jnp.swapaxes(planes, 1, 2),
        line_factors,
        layer_one,
        layer_two,
        jnp.swapaxes(layer_out, 1, 2),
        density_head,
        density_bias,
        decoder_in,
        decoder_out,
    )
    outs = pl.pallas_call(
        unpack,
        out_shape=(
            shape((1, VM, G * G)),
            shape((1, G, VM)),
            shape((1, VM, HID)),
            shape((1, HID, HID)),
            shape((1, FEAT, HID)),
            shape((1, HID)),
            shape((1, 1)),
            shape((FEAT, DEC)),
            shape((3, DEC)),
            shape((1, 1)),
        ),
        in_specs=[VMEM_SPEC] * 3,
        out_specs=[VMEM_SPEC] * 10,
        name="unpack",
    )(whole, decoder_sums, small_sums)
    outs = list(outs)
    outs[0] = jnp.swapaxes(outs[0], 1, 2)
    outs[4] = jnp.swapaxes(outs[4], 1, 2)
    outs[6] = outs[6].reshape(1)
    outs[9] = outs[9].reshape(())
    return tuple(outs)

def solution(mesh):
    placed = (
        P(("brick", "batch"), None),
        P(None, None, None, ("brick", "batch")),
        P(None, None, None, ("brick", "batch")),
        P(None, ("brick", "batch")),
        P("brick", None, None),
        P("brick", None, None),
        P("brick", None, None),
        P("brick", None, None),
        P("brick", None, None),
        P("brick", None),
        P("brick"),
        P(),
        P(),
    )
    return jax.shard_map(
        on_device,
        mesh=mesh,
        in_specs=placed,
        out_specs=(
            P("brick", None, None),
            P("brick", None, None),
            P("brick", None, None),
            P("brick", None, None),
            P("brick", None, None),
            P("brick", None),
            P("brick"),
            P(),
            P(),
            P(),
        ),
        check_vma=False,
    )
```

```python
import jax
import jax.numpy as jnp
from jax import lax
from jax.experimental import pallas as pl
from jax.experimental.pallas import tpu as pltpu
from jax.sharding import PartitionSpec as P

STEP_LENGTH = 0.1
MESH = pl.DeviceIdType.MESH
F32 = jnp.float32
BF16 = jnp.bfloat16

BRICKS = 32
BATCH = 4
RAYS = 128
CROSS = 8
CAP = 64
SLOTS = BRICKS * CAP
G = 40
VM = 144
COMP = 48
HID = 128
FEAT = 64
AUG = 80
DEC = 256
STRIPE = 5
STRIPES = 8
LOCAL = (STRIPE + 1) * G
WIDE = STRIPES * COMP
PEERS = 4
CHUNK = PEERS * 256
CHUNKS = BRICKS // PEERS
GROUP = 4
SAMPLES = BRICKS * CAP * 4
MSG = 40
HALF = FEAT // 2
UNITS = (80, 80, 80, 48)
BASES = (0, 640, 1280, 1920)
PACK = 2304
PAIRS = ((0, 1, 2), (0, 2, 1), (1, 2, 0))
VMEM_SPEC = pl.BlockSpec(memory_space=pltpu.VMEM)
SMEM_SPEC = pl.BlockSpec(memory_space=pltpu.SMEM)


def mm(a, b):
    return lax.dot_general(a, b, (((1,), (0,)), ((), ())), preferred_element_type=F32)


def nt(a, b):
    return lax.dot_general(a, b, (((1,), (1,)), ((), ())), preferred_element_type=F32)


def tn(a, b):
    return lax.dot_general(a, b, (((0,), (0,)), ((), ())), preferred_element_type=F32)


def split3(x):
    one = x.astype(BF16)
    rest = x - one.astype(F32)
    two = rest.astype(BF16)
    three = (rest - two.astype(F32)).astype(BF16)
    return one, two, three


def iota(shape, axis, kind=jnp.int32):
    return lax.broadcasted_iota(jnp.int32, shape, axis).astype(kind)


def eye(n):
    return jnp.where(iota((n, n), 0) == iota((n, n), 1), 1.0, 0.0).astype(BF16)


def sigmoid(v):
    return 0.5 * jnp.tanh(0.5 * v) + 0.5


def low_half(shape):
    return iota(shape, len(shape) - 1) < CAP


def swap(x):
    return pltpu.roll(x, CAP, 1)


def hat(x):
    return jnp.maximum(0.0, 1.0 - jnp.abs(x))


def place_rays(crossings, lattice, offsets, ray_slots, slot_cross, sent):
    named = crossings[...]
    brick_row = iota((BRICKS, RAYS), 0)
    crosses = jnp.zeros((BRICKS, RAYS), F32)
    order = jnp.zeros((BRICKS, RAYS), F32)
    for k in range(CROSS):
        hit = jnp.where(named[k : k + 1, :] == brick_row, 1.0, 0.0)
        crosses = crosses + hit
        order = order + float(k) * hit
    before = jnp.where(iota((RAYS, RAYS), 0) < iota((RAYS, RAYS), 1), 1.0, 0.0).astype(BF16)
    rank = mm(crosses.astype(BF16), before)
    rank = jnp.where(crosses > 0.0, rank, -1.0)
    lane = iota((BRICKS, SLOTS), 1)
    first = iota((BRICKS, SLOTS), 0) * CAP
    spread = jnp.where((lane >= first) & (lane < first + CAP), 1.0, 0.0).astype(BF16)
    place = (iota((RAYS, SLOTS), 1) & (CAP - 1)).astype(F32)
    chosen = jnp.where(tn(rank.astype(BF16), spread) == place, 1.0, 0.0)
    order_wide = tn(order.astype(BF16), spread)
    cross_of = jnp.sum(chosen * order_wide, axis=0, keepdims=True)
    chosen = chosen.astype(BF16)
    ray_slots[...] = chosen
    slot_cross[...] = jnp.broadcast_to(cross_of, (8, SLOTS))
    pad = jnp.zeros((2, RAYS), F32)
    rows = []
    for k in range(CROSS):
        for odd in range(2):
            for c in range(3):
                for half in range(2):
                    s = 2 * half + odd
                    rows.append(
                        lattice[c, k, s : s + 1, :].astype(F32) + offsets[c, k, s : s + 1, :]
                    )
            rows.append(pad)
    stacked = jnp.concatenate(split3(jnp.concatenate(rows, axis=0)), axis=0)
    height = CROSS * 16
    moved = mm(stacked, chosen)
    moved = moved[:height] + moved[height : 2 * height] + moved[2 * height :]
    picked = jnp.zeros((16, SLOTS), F32)
    for k in range(CROSS):
        picked = jnp.where(cross_of == float(k), moved[16 * k : 16 * k + 16], picked)
    low = low_half((8, 128))
    for tile in range(BRICKS // 2):
        x = picked[:, 128 * tile : 128 * tile + 128]
        even, odd = x[:8], x[8:]
        sent[2 * tile] = jnp.where(low, even, swap(odd))
        sent[2 * tile + 1] = jnp.where(low, swap(even), odd)


def turn_weights(
    planes,
    line_factors,
    layer_one,
    layer_two,
    layer_out,
    density_head,
    plane_t,
    line_t,
    one_t,
    two_t,
    out_t,
    out_aug,
    two_half,
):
    for h in range(STRIPES):
        at = STRIPE * G * h
        width = min(LOCAL, G * G - at)
        part = planes[0, :, at : at + width]
        if width < LOCAL:
            part = jnp.concatenate([part, jnp.zeros((VM, LOCAL - width), BF16)], axis=1)
        for p in range(3):
            plane_t[p, COMP * h : COMP * h + COMP, :] = part[COMP * p : COMP * p + COMP]
    turned = nt(eye(VM), line_factors[0])
    wide = jnp.concatenate([turned, turned, turned, jnp.zeros((VM, 8), F32)], axis=1)
    row, column = iota((VM, 128), 0), iota((VM, 128), 1)
    keep = (
        ((row < 48) & (column < 40))
        | ((row >= 48) & (row < 96) & (column >= 40) & (column < 80))
        | ((row >= 96) & (column >= 80) & (column < 120))
    )
    line_t[...] = jnp.where(keep, wide, 0.0).astype(BF16)
    unit = eye(HID)
    one_t[...] = (0.5 * nt(unit, layer_one[0])).astype(BF16)
    two_t[...] = (0.5 * nt(unit, layer_two[0])).astype(BF16)
    two_half[...] = (0.5 * layer_two[0].astype(F32)).astype(BF16)
    rows = [
        layer_out[0].astype(F32),
        density_head[...].astype(F32),
        jnp.zeros((AUG - FEAT - 1, HID), F32),
    ]
    both = jnp.concatenate(rows, axis=0).astype(BF16)
    out_t[...] = both
    out_aug[...] = (0.5 * nt(unit, both)).astype(BF16)


def coordinate(positions, peers, c):
    parts = [
        positions[p, 2 * c + half : 2 * c + half + 1, :] for p in peers for half in range(2)
    ]
    return jnp.concatenate(parts, axis=1)


def stripe_weights(along, other_hat):
    stripe = jnp.floor(along * (1.0 / STRIPE))
    local = along - float(STRIPE) * stripe
    near = hat(local - iota((8, along.shape[1]), 0, F32))
    weights = jnp.concatenate(
        [near[i : i + 1] * other_hat for i in range(STRIPE + 1)], axis=0
    ).astype(BF16)
    return stripe, weights


def line_table(hats):
    rows = [hats[PAIRS[p][2]] for p in range(3)] + [jnp.zeros((8, hats[0].shape[1]), F32)]
    return jnp.concatenate(rows, axis=0).astype(BF16)


def within_crossing(zeta, peer):
    low = low_half((1, 128))
    depths = []
    for half in range(2):
        at = 256 * peer + 128 * half
        z = zeta[:, at : at + 128]
        density = jnp.maximum(z, 0.0) + jnp.log1p(jnp.exp(-jnp.abs(z)))
        depths.append(STEP_LENGTH * density.astype(BF16).astype(F32))
    d0, d1 = depths
    r0, r1 = swap(d0), swap(d1)
    both = d0 + r0
    b0 = jnp.where(low, 0.0, r0)
    b1 = both + jnp.where(low, 0.0, r1)
    total = both + (d1 + r1)
    return (d0, d1), (b0, b1), total


def by_cross(row, cross_mask, ray_slots):
    out = nt(jnp.concatenate(split3(row * cross_mask), axis=0), ray_slots)
    return out[0:8] + out[8:16] + out[16:24]


def to_slots(table, cross_mask, ray_slots):
    out = mm(jnp.concatenate(split3(table), axis=0), ray_slots)
    out = out[0:8] + out[8:16] + out[16:24]
    return jnp.sum(out * cross_mask, axis=0, keepdims=True)


def silu_of_half(u, hidden, slope, lanes):
    t = jnp.tanh(u)
    p = 1.0 + t
    v = u * p
    h = v.astype(BF16)
    hidden[:, lanes] = h
    slope[:, lanes] = (p + v * (1.0 - t)).astype(BF16)
    return h


def together(*parts):
    parts = list(parts)
    while parts:
        parts = [part for part in parts if next(part, parts) is not parts]


class Brick:
    def __init__(self):
        self.me = lax.axis_index("brick")
        self.z = self.me // 8
        self.y = lax.rem(self.me // 2, 4)
        self.core = lax.rem(self.me, 2)

    def peer(self, q, j, sign=1):
        dz = jnp.minimum(q, CHUNKS - 1 - q)
        dy = 2 * (1 - q // 4) + j // 2
        z = lax.rem(self.z + sign * dz + 4, 4)
        y = lax.rem(self.y + sign * dy + 4, 4)
        return (z * 4 + y) * 2 + lax.rem(self.core + j % 2, 2)


class Exchange:
    def __init__(self, me, sent, got, send_sem, recv_sem):
        self.me, self.sent, self.got = me, sent, got
        self.send_sem, self.recv_sem = send_sem, recv_sem

    def copy(self, peer, slot):
        return pltpu.make_async_remote_copy(
            src_ref=self.sent.at[peer],
            dst_ref=self.got.at[slot],
            send_sem=self.send_sem.at[peer],
            recv_sem=self.recv_sem.at[slot],
            device_id={"brick": peer},
            device_id_type=MESH,
        )

    def send(self, peer):
        self.copy(peer, self.me).start()

    def receive(self, peer):
        self.copy(peer, peer).wait_recv()

    def others(self, act):
        def one(d, carry):
            act(lax.rem(self.me + d, BRICKS))
            return carry

        lax.fori_loop(1, BRICKS, one, 0)

    def sends_done(self):
        self.others(lambda peer: self.copy(peer, self.me).wait_send())


def train(
    crossings,
    lattice,
    offsets,
    target,
    planes,
    line_factors,
    layer_one,
    layer_two,
    layer_out,
    density_head,
    bias,
    decoder_in,
    decoder_out,
    planes_out,
    layers_out,
    decoder_sums,
    small_sums,
    pos_sent,
    pos_got,
    msg_sent,
    msg_got,
    back_sent,
    back_got,
    dec_sent,
    dec_got,
    dec_all,
    small_sent,
    small_got,
    head_sent,
    head_got,
    aug_s,
    ray_slots_ref,
    slot_cross,
    plane_t,
    line_t,
    one_t,
    two_t,
    out_t,
    out_aug,
    two_half,
    vm_s,
    plane_s,
    line_s,
    h1_s,
    s1_s,
    h2_s,
    s2_s,
    feat_s,
    zeta_s,
    gathered,
    acc_planes,
    acc_lines,
    acc_one,
    acc_two,
    acc_out,
    acc_bias,
    own,
    first_got,
    second,
    second_got,
    whole,
    pair_got,
    pair_sum,
    pos_ss,
    pos_rs,
    msg_ss,
    msg_rs,
    back_ss,
    back_rs,
    dec_ss,
    dec_rs,
    all_ss,
    all_rs,
    small_ss,
    small_rs,
    head_ss,
    head_rs,
    sum_ss,
    sum_rs,
):
    at = Brick()
    me = at.me
    x = lax.axis_index("batch")
    x_peers = [lax.rem(x + d, BATCH) for d in range(1, BATCH)]
    barrier = pltpu.get_barrier_semaphore()

    def greet(d, carry):
        pl.semaphore_signal(
            barrier, inc=1, device_id={"brick": lax.rem(me + d, BRICKS)}, device_id_type=MESH
        )
        return carry

    lax.fori_loop(1, BRICKS, greet, 0)
    for peer in x_peers:
        pl.semaphore_signal(barrier, inc=1, device_id={"batch": peer}, device_id_type=MESH)

    pos = Exchange(me, pos_sent, pos_got, pos_ss, pos_rs)
    msg = Exchange(me, msg_sent, msg_got, msg_ss, msg_rs)
    back = Exchange(me, back_sent, back_got, back_ss, back_rs)
    dec = Exchange(me, dec_sent, dec_got, dec_ss, dec_rs)

    def send_near_first(exchange):
        def one(i, carry):
            for j in range(PEERS):
                peer = at.peer(CHUNKS - 1 - i, j, -1)

                @pl.when(peer != me)
                def _():
                    exchange.send(peer)

            return carry

        lax.fori_loop(0, CHUNKS, one, 0)

    place_rays(crossings, lattice, offsets, ray_slots_ref, slot_cross, pos_sent)
    pl.semaphore_wait(barrier, BRICKS - 1 + BATCH - 1)
    send_near_first(pos)
    pos_got[me] = pos_sent[me]
    turn_weights(
        planes,
        line_factors,
        layer_one,
        layer_two,
        layer_out,
        density_head,
        plane_t,
        line_t,
        one_t,
        two_t,
        out_t,
        out_aug,
        two_half,
    )
    for ref in (acc_lines, acc_one, acc_two, acc_out, acc_bias, dec_sent):
        ref[...] = jnp.zeros_like(ref)

    def look_up(q):
        peers = [at.peer(q, j) for j in range(PEERS)]
        for p in peers:

            @pl.when(p != me)
            def _():
                pos.receive(p)

        lanes = pl.ds(pl.multiple_of(q * CHUNK, CHUNK), CHUNK)
        coords = [coordinate(pos_got, peers, c) for c in range(3)]
        points = iota((G, CHUNK), 0, F32)
        hats = [hat(coord - points) for coord in coords]
        line_value = mm(line_t[...], line_table(hats))
        line_s[:, lanes] = line_value.astype(BF16)
        for pair in range(3):
            a, b, line = PAIRS[pair]
            stripe, weights = stripe_weights(coords[a], hats[b])
            wide = mm(plane_t[pair], weights)
            stripe = jnp.broadcast_to(stripe, (8, CHUNK))
            masks = [stripe == float(h) for h in range(STRIPES)]
            values = []
            for r in range(0, COMP, 8):
                value = wide[r : r + 8]
                for h in range(1, STRIPES):
                    value = jnp.where(masks[h], wide[COMP * h + r : COMP * h + r + 8], value)
                values.append(value)
            value = jnp.concatenate(values, axis=0)
            rows = slice(COMP * pair, COMP * pair + COMP)
            vm_s[rows, lanes] = (value * line_value[rows]).astype(BF16)
            plane_s[rows, lanes] = value.astype(BF16)
            yield

    def network(q):
        peers = [at.peer(q, j) for j in range(PEERS)]
        lanes = pl.ds(pl.multiple_of(q * CHUNK, CHUNK), CHUNK)
        h1 = silu_of_half(mm(one_t[...], vm_s[:, lanes]), h1_s, s1_s, lanes)
        yield
        h2 = silu_of_half(mm(two_t[...], h1), h2_s, s2_s, lanes)
        wide = mm(out_t[...], h2)
        feat = wide[:FEAT].astype(BF16)
        feat_s[:, lanes] = feat
        zeta = wide[FEAT : FEAT + 1] + bias[0]
        zeta_s[:, lanes] = jnp.broadcast_to(zeta, (8, CHUNK))
        yield
        low = low_half((HALF, 128))
        for j, p in enumerate(peers):
            depths, befores, total = within_crossing(zeta, j)
            summed = jnp.zeros((FEAT, 128), F32)
            for half in range(2):
                weight = jnp.exp(-befores[half]) * (1.0 - jnp.exp(-depths[half]))
                lane = 256 * j + 128 * half
                summed = summed + weight * feat[:, lane : lane + 128].astype(F32)
            summed = summed + swap(summed)
            folded = jnp.where(low, summed[:HALF], summed[HALF:])
            parts = [part.astype(F32) for part in split3(total)]
            rows = [folded] + parts + [jnp.zeros((MSG - HALF - 3, 128), F32)]
            msg_sent[p] = jnp.concatenate(rows, axis=0).astype(BF16)
        yield
        for p in peers:

            @pl.when(p != me)
            def _():
                msg.send(p)

    def forward(q, carry):
        together(look_up(q + 1), network(q))
        return carry

    together(look_up(0))
    lax.fori_loop(0, CHUNKS - 1, forward, 0)
    together(network(CHUNKS - 1))
    msg_got[me] = msg_sent[me]

    ray_slots = ray_slots_ref[...]
    cross_mask = jnp.where(slot_cross[...] == iota((8, SLOTS), 0, F32), 1.0, 0.0)
    low = low_half((HALF, 128))
    low_row = low_half((1, 128))
    low8 = low_half((8, 128))
    msg.others(msg.receive)
    depth_rows = []
    for tile in range(BRICKS // 2):
        even, odd = msg_got[2 * tile].astype(F32), msg_got[2 * tile + 1].astype(F32)
        e, o = even[:HALF], odd[:HALF]
        lanes = slice(128 * tile, 128 * tile + 128)
        gathered[:HALF, lanes] = jnp.where(low, e, swap(o))
        gathered[HALF:, lanes] = jnp.where(low, swap(e), o)
        e = even[HALF : HALF + 1] + even[HALF + 1 : HALF + 2] + even[HALF + 2 : HALF + 3]
        o = odd[HALF : HALF + 1] + odd[HALF + 1 : HALF + 2] + odd[HALF + 2 : HALF + 3]
        depth_rows.append(jnp.where(low_row, e, o))
    depth = jnp.concatenate(depth_rows, axis=1)
    by_ray = by_cross(depth, cross_mask, ray_slots)
    running = jnp.zeros((1, RAYS), F32)
    befores = []
    for k in range(CROSS):
        befores.append(running)
        running = running + by_ray[k : k + 1]
    enter = to_slots(jnp.exp(-jnp.concatenate(befores, axis=0)), cross_mask, ray_slots)
    partials = gathered[...]
    scaled = partials * enter
    high = scaled.astype(BF16)
    rest = (scaled - high.astype(F32)).astype(BF16)
    composite = nt(jnp.concatenate([high, rest], axis=0), ray_slots)
    composite = (composite[:FEAT] + composite[FEAT:]).astype(BF16)
    decoder_pre = tn(decoder_in[...], composite)
    gate = sigmoid(decoder_pre)
    decoder_hidden = (decoder_pre * gate).astype(BF16)
    logits = mm(decoder_out[...], decoder_hidden)
    colors = sigmoid(logits)
    errors = colors - target[...]
    scale = float(RAYS * BRICKS * BATCH) ** (-0.5)
    grad_logits = (2.0 * scale * errors * colors * (1.0 - colors)).astype(BF16)
    back_decoder = tn(decoder_out[...], grad_logits)
    grad_pre = (back_decoder * (gate * (1.0 + decoder_pre * (1.0 - gate)))).astype(BF16)
    grad_composite = mm(decoder_in[...], grad_pre).astype(BF16)
    grad_slots = mm(grad_composite, ray_slots)
    along = jnp.sum(partials * grad_slots, axis=0, keepdims=True) * enter
    by_ray = by_cross(along, cross_mask, ray_slots)
    running = jnp.zeros((1, RAYS), F32)
    laters = []
    for k in reversed(range(CROSS)):
        laters.insert(0, running)
        running = running + by_ray[k : k + 1]
    later = to_slots(jnp.concatenate(laters, axis=0), cross_mask, ray_slots)
    for tile in range(BRICKS // 2):
        lanes = slice(128 * tile, 128 * tile + 128)
        top, bottom = grad_slots[:HALF, lanes], grad_slots[HALF:, lanes]
        scalars = [part.astype(F32) for part in split3(enter[:, lanes]) + split3(later[:, lanes])]
        scalars = jnp.concatenate(scalars + [jnp.zeros((2, 128), F32)], axis=0)
        turned = swap(scalars)
        rows = [jnp.where(low, top, swap(bottom)), jnp.where(low8, scalars, turned)]
        back_sent[2 * tile] = jnp.concatenate(rows, axis=0).astype(BF16)
        rows = [jnp.where(low, swap(top), bottom), jnp.where(low8, turned, scalars)]
        back_sent[2 * tile + 1] = jnp.concatenate(rows, axis=0).astype(BF16)
    send_near_first(back)
    back_got[me] = back_sent[me]

    objective = scale * jnp.sum(errors * errors)
    grad_out = nt(grad_logits, decoder_hidden)
    grad_in = nt(composite, grad_pre)
    for j in range(8):
        dec_sent[j] = grad_in[8 * j : 8 * j + 8, :128]
        dec_sent[8 + j] = grad_in[8 * j : 8 * j + 8, 128:]
    rows = [grad_out[:, :128], grad_out[:, 128:], jnp.full((2, 128), objective, F32)]
    dec_sent[16] = jnp.concatenate(rows, axis=0)

    def backward(i, carry):
        q = CHUNKS - 1 - i
        peers = [at.peer(q, j) for j in range(PEERS)]
        for p in peers:

            @pl.when(p != me)
            def _():
                back.receive(p)

        lanes = pl.ds(pl.multiple_of(q * CHUNK, CHUNK), CHUNK)
        zeta = zeta_s[0:1, lanes]
        feat = feat_s[:, lanes].astype(F32)
        grad_feats, grad_zetas = [], []
        for j, p in enumerate(peers):
            depths, befores, total = within_crossing(zeta, j)
            got = back_got[p].astype(F32)
            m = got[:HALF]
            turned = swap(m)
            grads = jnp.concatenate([jnp.where(low, m, turned), jnp.where(low, turned, m)], axis=0)
            enter = got[HALF : HALF + 1] + got[HALF + 1 : HALF + 2] + got[HALF + 2 : HALF + 3]
            later = got[HALF + 3 : HALF + 4] + got[HALF + 4 : HALF + 5] + got[HALF + 5 : HALF + 6]
            carried, lit = [], []
            for half in range(2):
                lane = 256 * j + 128 * half
                transmit = enter * jnp.exp(-befores[half])
                survive = jnp.exp(-depths[half])
                weight = transmit * (1.0 - survive)
                grad_weight = jnp.sum(grads * feat[:, lane : lane + 128], axis=0, keepdims=True)
                grad_feats.append(weight * grads)
                carried.append(grad_weight * weight)
                lit.append(grad_weight * transmit * survive)
            c0, c1 = carried
            r0, r1 = swap(c0), swap(c1)
            laters = (
                jnp.where(low_row, r0, 0.0) + (c1 + r1) + later,
                jnp.where(low_row, r1, 0.0) + later,
            )
            for half in range(2):
                lane = 256 * j + 128 * half
                grad_density = (STEP_LENGTH * (lit[half] - laters[half])).astype(BF16)
                gate = sigmoid(zeta[:, lane : lane + 128])
                grad_zetas.append((grad_density.astype(F32) * gate).astype(BF16).astype(F32))
        grad_zeta = jnp.concatenate(grad_zetas, axis=1)
        acc_bias[...] += jnp.full((8, 128), jnp.sum(grad_zeta), F32)
        rows = [jnp.concatenate(grad_feats, axis=1), grad_zeta]
        rows.append(jnp.zeros((AUG - FEAT - 1, CHUNK), F32))
        grad_aug = jnp.concatenate(rows, axis=0).astype(BF16)
        aug_s[:, lanes] = grad_aug
        grad_a2 = (mm(out_aug[...], grad_aug) * s2_s[:, lanes].astype(F32)).astype(BF16)
        s2_s[:, lanes] = grad_a2
        grad_a1 = (mm(two_half[...], grad_a2) * s1_s[:, lanes].astype(F32)).astype(BF16)
        s1_s[:, lanes] = grad_a1
        grad_vm = mm(layer_one[0], grad_a1)
        plane_s[:, lanes] = (grad_vm * plane_s[:, lanes].astype(F32)).astype(BF16)
        line_s[:, lanes] = (grad_vm * line_s[:, lanes].astype(F32)).astype(BF16)
        return carry

    lax.fori_loop(0, CHUNKS, backward, 0)
    dec.others(dec.send)
    dec_got[me] = dec_sent[me]

    partner_a = x + 1 - 2 * lax.rem(x, 2)
    partner_b = BATCH - 1 - x
    keep_a = lax.rem((x + 1) // 2, 2)
    keep_b = x // 2
    partners = (partner_a, partner_b)
    keeps = (keep_a, keep_b)

    def across(src, dst, stage, step, side, partner):
        n = (stage * 4 + step) * 2 + side
        return pltpu.make_async_remote_copy(
            src_ref=src,
            dst_ref=dst,
            send_sem=sum_ss.at[n],
            recv_sem=sum_rs.at[n],
            device_id={"batch": partner},
            device_id_type=MESH,
        )

    def span(start, size):
        return pl.ds(pl.multiple_of(start, 16), size)

    def transfer(stage, step, side):
        u, base = UNITS[stage], BASES[stage]
        start = base + 4 * u * side
        half_rows = BASES[stage] // 2 + 2 * u * side
        quarter_rows = BASES[stage] // 4 + u * side
        one, two = keeps[side], keeps[1 - side]
        near, far = partners[side], partners[1 - side]
        if step == 0:
            return across(
                own.at[span(start + 2 * u * (1 - one), 2 * u)],
                first_got.at[span(half_rows, 2 * u)],
                stage,
                step,
                side,
                near,
            )
        if step == 1:
            return across(
                second.at[span(half_rows + u * (1 - two), u)],
                second_got.at[span(quarter_rows, u)],
                stage,
                step,
                side,
                far,
            )
        if step == 2:
            rows = span(start + 2 * u * one + u * two, u)
            return across(whole.at[rows], whole.at[rows], stage, step, side, far)
        rows = span(start + 2 * u * one, 2 * u)
        return across(whole.at[rows], whole.at[rows], stage, step, side, near)

    def advance(stage, step):
        u, base = UNITS[stage], BASES[stage]
        for side in range(2):
            start = base + 4 * u * side
            half_rows = BASES[stage] // 2 + 2 * u * side
            quarter_rows = BASES[stage] // 4 + u * side
            one, two = keeps[side], keeps[1 - side]
            if step > 0:
                transfer(stage, step - 1, side).wait()
            if step == 1:
                mine = own[span(start + 2 * u * one, 2 * u), :].astype(F32)
                theirs = first_got[span(half_rows, 2 * u), :].astype(F32)
                second[span(half_rows, 2 * u), :] = (mine + theirs).astype(BF16)
            if step == 2:
                mine = second[span(half_rows + u * two, u), :].astype(F32)
                theirs = second_got[span(quarter_rows, u), :].astype(F32)
                whole[span(start + 2 * u * one + u * two, u), :] = (mine + theirs).astype(BF16)
            if step < 4:
                transfer(stage, step, side).start()

    def exchange_half(stage, step, side):
        u = UNITS[stage]
        start = BASES[stage] + 4 * u * side
        at_row = start - BASES[2]
        rows = pl.ds(at_row, 4 * u)
        if step == 0:
            src, partner = own.at[pl.ds(start, 4 * u)], partners[side]
        else:
            src, partner = pair_sum.at[rows], partners[1 - side]
        return across(src, pair_got.at[step].at[rows], stage, step, side, partner)

    def advance_doubling(stage, step):
        u = UNITS[stage]
        for side in range(2):
            start = BASES[stage] + 4 * u * side
            at_row = start - BASES[2]
            if step > 0:
                exchange_half(stage, step - 1, side).wait()
                theirs = pair_got[step - 1, at_row : at_row + 4 * u, :].astype(F32)
            if step == 1:
                mine = own[start : start + 4 * u, :].astype(F32)
                pair_sum[at_row : at_row + 4 * u, :] = (mine + theirs).astype(BF16)
            if step == 2:
                mine = pair_sum[at_row : at_row + 4 * u, :].astype(F32)
                whole[start : start + 4 * u, :] = (mine + theirs).astype(BF16)
            if step < 2:
                exchange_half(stage, step, side).start()

    def slot(t):
        for stage in reversed(range(4)) if t > 3 else range(4):
            step = t - stage
            if stage < 2 and 0 <= step <= 4:
                advance(stage, step)
            if stage >= 2 and 0 <= step <= 2:
                advance_doubling(stage, step)

    def settle(pair):
        side, base = STRIPE * G, BASES[pair]
        parts = [whole[base + side * t : base + side * t + side, :] for t in range(3)]
        turned = nt(eye(WIDE), jnp.concatenate(parts, axis=1)).astype(BF16)
        for h in range(STRIPES):
            planes_out[COMP * pair : COMP * pair + COMP, side * h : side * h + side] = turned[
                COMP * h : COMP * h + COMP
            ]

    def small_copy(d, peer):
        return pltpu.make_async_remote_copy(
            src_ref=small_sent,
            dst_ref=small_got.at[x],
            send_sem=small_ss.at[d],
            recv_sem=small_rs.at[d],
            device_id={"batch": peer},
            device_id_type=MESH,
        )

    def spread_copy(peer, slot):
        return pltpu.make_async_remote_copy(
            src_ref=dec_all.at[me],
            dst_ref=dec_all.at[slot],
            send_sem=all_ss.at[peer],
            recv_sem=all_rs.at[slot],
            device_id={"brick": peer},
            device_id_type=MESH,
        )

    for pair in range(3):
        a, b, line = PAIRS[pair]
        acc_planes[...] = jnp.zeros_like(acc_planes)

        def scatter(g, carry):
            masked, weights = [], []
            for q in range(GROUP):
                q = g * GROUP + q
                peers = [at.peer(q, j) for j in range(PEERS)]
                lanes = pl.ds(pl.multiple_of(q * CHUNK, CHUNK), CHUNK)
                points = iota((G, CHUNK), 0, F32)
                other_hat = hat(coordinate(pos_got, peers, b) - points)
                stripe, weight = stripe_weights(coordinate(pos_got, peers, a), other_hat)
                piece = line_s[COMP * pair : COMP * pair + COMP, lanes]
                rows = [
                    piece * jnp.where(stripe == float(h), 1.0, 0.0).astype(BF16)
                    for h in range(STRIPES)
                ]
                masked.append(jnp.concatenate(rows, axis=0))
                weights.append(weight)
            acc_planes[...] += nt(
                jnp.concatenate(masked, axis=1), jnp.concatenate(weights, axis=1)
            )
            return carry

        lax.fori_loop(0, CHUNKS // GROUP, scatter, 0)
        side = STRIPE * G
        acc_planes[COMP:, :G] += acc_planes[: WIDE - COMP, side:]
        turned = nt(eye(side), acc_planes[:, :side].astype(BF16)).astype(BF16)
        base = BASES[pair]
        for tile in range(3):
            own[base + side * tile : base + side * tile + side, :] = turned[
                :, 128 * tile : 128 * tile + 128
            ]
        own[base + 3 * side : base + 640, :] = jnp.zeros((640 - 3 * side, 128), BF16)
        slot(pair)
        if pair == 0:
            dec.others(dec.receive)
            total = dec_got[0]
            for j in range(1, BRICKS):
                total = total + dec_got[j]
            small_sent[0:8] = total
            small_sent[8:16] = jnp.concatenate(
                [acc_bias[0:1, :], jnp.zeros((7, 128), F32)], axis=0
            )
            for d, peer in enumerate(x_peers):
                small_copy(d, peer).start()
            small_got[x] = small_sent[...]
        if pair == 1:
            for d, peer in enumerate(x_peers):
                small_copy(d, peer).wait()
            small = (small_got[0] + small_got[1]) + (small_got[2] + small_got[3])
            small_sums[0:8] = small[8:16]
            dec_all[me] = small[0:8]
            dec.others(lambda peer: spread_copy(peer, me).start())
    def layers(g, carry):
        tables = []
        for q in range(GROUP):
            q = g * GROUP + q
            peers = [at.peer(q, j) for j in range(PEERS)]
            points = iota((G, CHUNK), 0, F32)
            hats = [hat(coordinate(pos_got, peers, c) - points) for c in range(3)]
            tables.append(line_table(hats))
        lanes = pl.ds(pl.multiple_of(g * GROUP * CHUNK, GROUP * CHUNK), GROUP * CHUNK)
        acc_lines[...] += nt(plane_s[:, lanes], jnp.concatenate(tables, axis=1))
        acc_out[...] += nt(aug_s[:, lanes], h2_s[:, lanes])
        acc_two[...] += nt(h1_s[:, lanes], s2_s[:, lanes])
        acc_one[...] += nt(vm_s[:, lanes], s1_s[:, lanes])
        return carry

    lax.fori_loop(0, CHUNKS // GROUP, layers, 0)
    base = BASES[3]
    own[base : base + VM, :] = acc_one[...].astype(BF16)
    own[base + VM : base + VM + HID, :] = acc_two[...].astype(BF16)
    own[base + VM + HID : base + VM + HID + FEAT, :] = acc_out[:FEAT, :].astype(BF16)
    column = iota((COMP, 128), 1)
    diagonal = jnp.where(column < G, acc_lines[:COMP, :], 0.0)
    diagonal = jnp.where((column >= G) & (column < 2 * G), acc_lines[COMP : 2 * COMP, :], diagonal)
    diagonal = jnp.where(
        (column >= 2 * G) & (column < 3 * G), acc_lines[2 * COMP :, :], diagonal
    )
    own[base + VM + HID + FEAT :, :] = diagonal.astype(BF16)
    slot(3)
    head_sent[...] = jnp.broadcast_to(acc_out[FEAT : FEAT + 1, :], (8, 128))

    def head_copy(d, peer):
        return pltpu.make_async_remote_copy(
            src_ref=head_sent,
            dst_ref=head_got.at[x],
            send_sem=head_ss.at[d],
            recv_sem=head_rs.at[d],
            device_id={"batch": peer},
            device_id_type=MESH,
        )

    for d, peer in enumerate(x_peers):
        head_copy(d, peer).start()
    head_got[x] = head_sent[...]
    for exchange in (pos, msg):
        exchange.sends_done()
    slot(4)
    settle(0)
    settle(2)
    dec.others(lambda peer: spread_copy(peer, peer).wait_recv())
    decoder_sums[...] = dec_all[...]
    dec.others(lambda peer: spread_copy(peer, me).wait_send())
    for exchange in (back, dec):
        exchange.sends_done()
    for d, peer in enumerate(x_peers):
        head_copy(d, peer).wait()
    small_sums[8:16] = (head_got[0] + head_got[1]) + (head_got[2] + head_got[3])
    slot(5)
    settle(1)
    layers_out[...] = whole[BASES[3] :, :]


def unpack(
    planes_in,
    layers,
    decoder_sums,
    small_sums,
    planes,
    lines,
    one,
    two,
    out,
    head,
    bias,
    decoder_in,
    decoder_out,
    objective,
):
    planes[0] = planes_in[...].astype(F32)
    one[0] = layers[0:VM, :].astype(F32)
    two[0] = layers[VM : VM + HID, :].astype(F32)
    out[0] = layers[VM + HID : VM + HID + FEAT, :].astype(F32)
    block = layers[VM + HID + FEAT : PACK - BASES[3], :]
    row, column = iota((G, 128), 0), iota((G, 128), 1)
    parts = []
    for p in range(3):
        pick = jnp.where(column == row + G * p, 1.0, 0.0).astype(BF16)
        parts.append(nt(pick, block))
    lines[0] = jnp.concatenate(parts, axis=1)
    bias[...] = small_sums[0:1, 0:1]
    head[...] = small_sums[8:9, :]
    for j in range(8):
        decoder_in[8 * j : 8 * j + 8, 0:128] = decoder_sums[j]
        decoder_in[8 * j : 8 * j + 8, 128:256] = decoder_sums[8 + j]
    last = decoder_sums[16]
    decoder_out[:, 0:128] = last[0:3]
    decoder_out[:, 128:256] = last[3:6]
    objective[...] = last[6:7, 0:1]


def shape(dims, kind=F32):
    return jax.ShapeDtypeStruct(dims, kind)


def on_device(
    crossings,
    lattice,
    offsets,
    target,
    planes,
    line_factors,
    layer_one,
    layer_two,
    layer_out,
    density_head,
    density_bias,
    decoder_in,
    decoder_out,
):
    dma = pltpu.SemaphoreType.DMA
    vmem = pltpu.VMEM
    planes_sum, layers_sum, decoder_sums, small_sums = pl.pallas_call(
        train,
        out_shape=(
            shape((VM, G * G), BF16),
            shape((PACK - BASES[3], 128), BF16),
            shape((BRICKS, 8, 128)),
            shape((16, 128)),
        ),
        in_specs=[VMEM_SPEC] * 10 + [SMEM_SPEC] + [VMEM_SPEC] * 2,
        out_specs=[VMEM_SPEC] * 4,
        scratch_shapes=[vmem((BRICKS, 8, 128), F32)] * 2
        + [vmem((BRICKS, MSG, 128), BF16)] * 4
        + [vmem((BRICKS, 8, 128), F32)] * 3
        + [vmem((16, 128), F32), vmem((BATCH, 16, 128), F32)]
        + [vmem((8, 128), F32), vmem((BATCH, 8, 128), F32), vmem((AUG, SAMPLES), BF16)]
        + [vmem((RAYS, SLOTS), BF16), vmem((8, SLOTS), F32)]
        + [
            vmem((3, WIDE, LOCAL), BF16),
            vmem((VM, 128), BF16),
            vmem((HID, VM), BF16),
            vmem((HID, HID), BF16),
            vmem((AUG, HID), BF16),
            vmem((HID, AUG), BF16),
            vmem((HID, HID), BF16),
        ]
        + [vmem((VM, SAMPLES), BF16)] * 3
        + [vmem((HID, SAMPLES), BF16)] * 4
        + [vmem((FEAT, SAMPLES), BF16), vmem((8, SAMPLES), F32)]
        + [
            vmem((FEAT, SLOTS), F32),
            vmem((WIDE, LOCAL), F32),
            vmem((VM, 128), F32),
            vmem((VM, HID), F32),
            vmem((HID, HID), F32),
            vmem((AUG, HID), F32),
            vmem((8, 128), F32),
        ]
        + [
            vmem((PACK, 128), BF16),
            vmem((BASES[2] // 2, 128), BF16),
            vmem((BASES[2] // 2, 128), BF16),
            vmem((BASES[2] // 4, 128), BF16),
            vmem((PACK, 128), BF16),
            vmem((2, PACK - BASES[2], 128), BF16),
            vmem((PACK - BASES[2], 128), BF16),
        ]
        + [dma((BRICKS,))] * 10
        + [dma((BATCH - 1,))] * 4
        + [dma((32,))] * 2,
        compiler_params=pltpu.CompilerParams(collective_id=0, has_side_effects=True),
        name="train",
    )(
        crossings.T,
        lattice,
        offsets,
        target,
        jnp.swapaxes(planes, 1, 2),
        line_factors,
        layer_one,
        layer_two,
        jnp.swapaxes(layer_out, 1, 2),
        density_head,
        density_bias,
        decoder_in,
        decoder_out,
    )
    outs = pl.pallas_call(
        unpack,
        out_shape=(
            shape((1, VM, G * G)),
            shape((1, G, VM)),
            shape((1, VM, HID)),
            shape((1, HID, HID)),
            shape((1, FEAT, HID)),
            shape((1, HID)),
            shape((1, 1)),
            shape((FEAT, DEC)),
            shape((3, DEC)),
            shape((1, 1)),
        ),
        in_specs=[VMEM_SPEC] * 4,
        out_specs=[VMEM_SPEC] * 10,
        name="unpack",
    )(planes_sum, layers_sum, decoder_sums, small_sums)
    outs = list(outs)
    outs[0] = jnp.swapaxes(outs[0], 1, 2)
    outs[4] = jnp.swapaxes(outs[4], 1, 2)
    outs[6] = outs[6].reshape(1)
    outs[9] = outs[9].reshape(())
    return tuple(outs)

def solution(mesh):
    placed = (
        P(("brick", "batch"), None),
        P(None, None, None, ("brick", "batch")),
        P(None, None, None, ("brick", "batch")),
        P(None, ("brick", "batch")),
        P("brick", None, None),
        P("brick", None, None),
        P("brick", None, None),
        P("brick", None, None),
        P("brick", None, None),
        P("brick", None),
        P("brick"),
        P(),
        P(),
    )
    return jax.shard_map(
        on_device,
        mesh=mesh,
        in_specs=placed,
        out_specs=(
            P("brick", None, None),
            P("brick", None, None),
            P("brick", None, None),
            P("brick", None, None),
            P("brick", None, None),
            P("brick", None),
            P("brick"),
            P(),
            P(),
            P(),
        ),
        check_vma=False,
    )
```

```python
import jax
import jax.numpy as jnp
from jax import lax
from jax.experimental import pallas as pl
from jax.experimental.pallas import tpu as pltpu
from jax.sharding import PartitionSpec as P

STEP_LENGTH = 0.1
MESH = pl.DeviceIdType.MESH
F32 = jnp.float32
BF16 = jnp.bfloat16

BRICKS = 32
BATCH = 4
RAYS = 128
CROSS = 8
CAP = 64
SLOTS = BRICKS * CAP
G = 40
VM = 144
COMP = 48
HID = 128
FEAT = 64
AUG = 80
DEC = 256
STRIPE = 5
STRIPES = 8
LOCAL = (STRIPE + 1) * G
WIDE = STRIPES * COMP
PEERS = 4
CHUNK = PEERS * 256
CHUNKS = BRICKS // PEERS
GROUP = 4
SAMPLES = BRICKS * CAP * 4
MSG = 40
HALF = FEAT // 2
SIDES = ((0, 304, 600), (600, 904, 1200), (1200, 1504, 1800), (1800, 1992, 2184))
BASES = (0, 600, 1200, 1800)
PACK = 2184
PAIRS = ((0, 1, 2), (0, 2, 1), (1, 2, 0))
VMEM_SPEC = pl.BlockSpec(memory_space=pltpu.VMEM)
SMEM_SPEC = pl.BlockSpec(memory_space=pltpu.SMEM)


def mm(a, b):
    return lax.dot_general(a, b, (((1,), (0,)), ((), ())), preferred_element_type=F32)


def nt(a, b):
    return lax.dot_general(a, b, (((1,), (1,)), ((), ())), preferred_element_type=F32)


def tn(a, b):
    return lax.dot_general(a, b, (((0,), (0,)), ((), ())), preferred_element_type=F32)


def split3(x):
    one = x.astype(BF16)
    rest = x - one.astype(F32)
    two = rest.astype(BF16)
    three = (rest - two.astype(F32)).astype(BF16)
    return one, two, three


def iota(shape, axis, kind=jnp.int32):
    return lax.broadcasted_iota(jnp.int32, shape, axis).astype(kind)


def eye(n):
    return jnp.where(iota((n, n), 0) == iota((n, n), 1), 1.0, 0.0).astype(BF16)


def sigmoid(v):
    return 0.5 * jnp.tanh(0.5 * v) + 0.5


def low_half(shape):
    return iota(shape, len(shape) - 1) < CAP


def swap(x):
    return pltpu.roll(x, CAP, 1)


def hat(x):
    return jnp.maximum(0.0, 1.0 - jnp.abs(x))


def place_rays(crossings, lattice, offsets, ray_slots, slot_cross, sent):
    named = crossings[...]
    brick_row = iota((BRICKS, RAYS), 0)
    crosses = jnp.zeros((BRICKS, RAYS), F32)
    order = jnp.zeros((BRICKS, RAYS), F32)
    for k in range(CROSS):
        hit = jnp.where(named[k : k + 1, :] == brick_row, 1.0, 0.0)
        crosses = crosses + hit
        order = order + float(k) * hit
    before = jnp.where(iota((RAYS, RAYS), 0) < iota((RAYS, RAYS), 1), 1.0, 0.0).astype(BF16)
    rank = mm(crosses.astype(BF16), before)
    rank = jnp.where(crosses > 0.0, rank, -1.0)
    lane = iota((BRICKS, SLOTS), 1)
    first = iota((BRICKS, SLOTS), 0) * CAP
    spread = jnp.where((lane >= first) & (lane < first + CAP), 1.0, 0.0).astype(BF16)
    place = (iota((RAYS, SLOTS), 1) & (CAP - 1)).astype(F32)
    chosen = jnp.where(tn(rank.astype(BF16), spread) == place, 1.0, 0.0)
    order_wide = tn(order.astype(BF16), spread)
    cross_of = jnp.sum(chosen * order_wide, axis=0, keepdims=True)
    chosen = chosen.astype(BF16)
    ray_slots[...] = chosen
    slot_cross[...] = jnp.broadcast_to(cross_of, (8, SLOTS))
    pad = jnp.zeros((2, RAYS), F32)
    rows = []
    for k in range(CROSS):
        for odd in range(2):
            for c in range(3):
                for half in range(2):
                    s = 2 * half + odd
                    rows.append(
                        lattice[c, k, s : s + 1, :].astype(F32) + offsets[c, k, s : s + 1, :]
                    )
            rows.append(pad)
    stacked = jnp.concatenate(split3(jnp.concatenate(rows, axis=0)), axis=0)
    height = CROSS * 16
    moved = mm(stacked, chosen)
    moved = moved[:height] + moved[height : 2 * height] + moved[2 * height :]
    picked = jnp.zeros((16, SLOTS), F32)
    for k in range(CROSS):
        picked = jnp.where(cross_of == float(k), moved[16 * k : 16 * k + 16], picked)
    low = low_half((8, 128))
    for tile in range(BRICKS // 2):
        x = picked[:, 128 * tile : 128 * tile + 128]
        even, odd = x[:8], x[8:]
        sent[2 * tile] = jnp.where(low, even, swap(odd))
        sent[2 * tile + 1] = jnp.where(low, swap(even), odd)


def turn_weights(
    planes,
    line_factors,
    layer_one,
    layer_two,
    layer_out,
    density_head,
    plane_t,
    line_t,
    one_t,
    two_t,
    out_t,
    out_aug,
    two_half,
):
    for h in range(STRIPES):
        at = STRIPE * G * h
        width = min(LOCAL, G * G - at)
        part = planes[0, :, at : at + width]
        if width < LOCAL:
            part = jnp.concatenate([part, jnp.zeros((VM, LOCAL - width), BF16)], axis=1)
        for p in range(3):
            plane_t[p, COMP * h : COMP * h + COMP, :] = part[COMP * p : COMP * p + COMP]
    turned = nt(eye(VM), line_factors[0])
    wide = jnp.concatenate([turned, turned, turned, jnp.zeros((VM, 8), F32)], axis=1)
    row, column = iota((VM, 128), 0), iota((VM, 128), 1)
    keep = (
        ((row < 48) & (column < 40))
        | ((row >= 48) & (row < 96) & (column >= 40) & (column < 80))
        | ((row >= 96) & (column >= 80) & (column < 120))
    )
    line_t[...] = jnp.where(keep, wide, 0.0).astype(BF16)
    unit = eye(HID)
    one_t[...] = (0.5 * nt(unit, layer_one[0])).astype(BF16)
    two_t[...] = (0.5 * nt(unit, layer_two[0])).astype(BF16)
    two_half[...] = (0.5 * layer_two[0].astype(F32)).astype(BF16)
    rows = [
        layer_out[0].astype(F32),
        density_head[...].astype(F32),
        jnp.zeros((AUG - FEAT - 1, HID), F32),
    ]
    both = jnp.concatenate(rows, axis=0).astype(BF16)
    out_t[...] = both
    out_aug[...] = (0.5 * nt(unit, both)).astype(BF16)


def coordinate(positions, peers, c):
    parts = [
        positions[p, 2 * c + half : 2 * c + half + 1, :] for p in peers for half in range(2)
    ]
    return jnp.concatenate(parts, axis=1)


def stripe_weights(along, other_hat):
    stripe = jnp.floor(along * (1.0 / STRIPE))
    local = along - float(STRIPE) * stripe
    near = hat(local - iota((8, along.shape[1]), 0, F32))
    weights = jnp.concatenate(
        [near[i : i + 1] * other_hat for i in range(STRIPE + 1)], axis=0
    ).astype(BF16)
    return stripe, weights


def line_table(hats):
    rows = [hats[PAIRS[p][2]] for p in range(3)] + [jnp.zeros((8, hats[0].shape[1]), F32)]
    return jnp.concatenate(rows, axis=0).astype(BF16)


def within_crossing(zeta, peer):
    low = low_half((1, 128))
    depths = []
    for half in range(2):
        at = 256 * peer + 128 * half
        z = zeta[:, at : at + 128]
        density = jnp.maximum(z, 0.0) + jnp.log1p(jnp.exp(-jnp.abs(z)))
        depths.append(STEP_LENGTH * density.astype(BF16).astype(F32))
    d0, d1 = depths
    r0, r1 = swap(d0), swap(d1)
    both = d0 + r0
    b0 = jnp.where(low, 0.0, r0)
    b1 = both + jnp.where(low, 0.0, r1)
    total = both + (d1 + r1)
    return (d0, d1), (b0, b1), total


def by_cross(row, cross_mask, ray_slots):
    out = nt(jnp.concatenate(split3(row * cross_mask), axis=0), ray_slots)
    return out[0:8] + out[8:16] + out[16:24]


def to_slots(table, cross_mask, ray_slots):
    out = mm(jnp.concatenate(split3(table), axis=0), ray_slots)
    out = out[0:8] + out[8:16] + out[16:24]
    return jnp.sum(out * cross_mask, axis=0, keepdims=True)


def silu_of_half(u, hidden, slope, lanes):
    t = jnp.tanh(u)
    p = 1.0 + t
    v = u * p
    h = v.astype(BF16)
    hidden[:, lanes] = h
    slope[:, lanes] = (p + v * (1.0 - t)).astype(BF16)
    return h


def together(*parts):
    parts = list(parts)
    while parts:
        parts = [part for part in parts if next(part, parts) is not parts]


class Brick:
    def __init__(self):
        self.me = lax.axis_index("brick")
        self.z = self.me // 8
        self.y = lax.rem(self.me // 2, 4)
        self.core = lax.rem(self.me, 2)

    def peer(self, q, j, sign=1):
        dz = jnp.minimum(q, CHUNKS - 1 - q)
        dy = 2 * (1 - q // 4) + j // 2
        z = lax.rem(self.z + sign * dz + 4, 4)
        y = lax.rem(self.y + sign * dy + 4, 4)
        return (z * 4 + y) * 2 + lax.rem(self.core + j % 2, 2)


class Exchange:
    def __init__(self, me, sent, got, send_sem, recv_sem):
        self.me, self.sent, self.got = me, sent, got
        self.send_sem, self.recv_sem = send_sem, recv_sem

    def copy(self, peer, slot):
        return pltpu.make_async_remote_copy(
            src_ref=self.sent.at[peer],
            dst_ref=self.got.at[slot],
            send_sem=self.send_sem.at[peer],
            recv_sem=self.recv_sem.at[slot],
            device_id={"brick": peer},
            device_id_type=MESH,
        )

    def send(self, peer):
        self.copy(peer, self.me).start()

    def receive(self, peer):
        self.copy(peer, peer).wait_recv()

    def others(self, act):
        def one(d, carry):
            act(lax.rem(self.me + d, BRICKS))
            return carry

        lax.fori_loop(1, BRICKS, one, 0)

    def sends_done(self):
        self.others(lambda peer: self.copy(peer, self.me).wait_send())


def train(
    crossings,
    lattice,
    offsets,
    target,
    planes,
    line_factors,
    layer_one,
    layer_two,
    layer_out,
    density_head,
    bias,
    decoder_in,
    decoder_out,
    planes_out,
    layers_out,
    decoder_sums,
    small_sums,
    pos_sent,
    pos_got,
    msg_sent,
    msg_got,
    back_sent,
    back_got,
    dec_sent,
    dec_got,
    dec_all,
    small_sent,
    small_got,
    head_sent,
    head_got,
    aug_s,
    ray_slots_ref,
    slot_cross,
    plane_t,
    line_t,
    one_t,
    two_t,
    out_t,
    out_aug,
    two_half,
    vm_s,
    plane_s,
    line_s,
    h1_s,
    s1_s,
    h2_s,
    s2_s,
    feat_s,
    zeta_s,
    gathered,
    acc_planes,
    acc_lines,
    acc_one,
    acc_two,
    acc_out,
    acc_bias,
    own,
    whole,
    pair_got,
    pair_sum,
    pos_ss,
    pos_rs,
    msg_ss,
    msg_rs,
    back_ss,
    back_rs,
    dec_ss,
    dec_rs,
    all_ss,
    all_rs,
    small_ss,
    small_rs,
    head_ss,
    head_rs,
    sum_ss,
    sum_rs,
):
    at = Brick()
    me = at.me
    x = lax.axis_index("batch")
    x_peers = [lax.rem(x + d, BATCH) for d in range(1, BATCH)]
    barrier = pltpu.get_barrier_semaphore()

    def greet(d, carry):
        pl.semaphore_signal(
            barrier, inc=1, device_id={"brick": lax.rem(me + d, BRICKS)}, device_id_type=MESH
        )
        return carry

    lax.fori_loop(1, BRICKS, greet, 0)
    for peer in x_peers:
        pl.semaphore_signal(barrier, inc=1, device_id={"batch": peer}, device_id_type=MESH)

    pos = Exchange(me, pos_sent, pos_got, pos_ss, pos_rs)
    msg = Exchange(me, msg_sent, msg_got, msg_ss, msg_rs)
    back = Exchange(me, back_sent, back_got, back_ss, back_rs)
    dec = Exchange(me, dec_sent, dec_got, dec_ss, dec_rs)

    def send_near_first(exchange):
        def one(i, carry):
            for j in range(PEERS):
                peer = at.peer(CHUNKS - 1 - i, j, -1)

                @pl.when(peer != me)
                def _():
                    exchange.send(peer)

            return carry

        lax.fori_loop(0, CHUNKS, one, 0)

    place_rays(crossings, lattice, offsets, ray_slots_ref, slot_cross, pos_sent)
    pl.semaphore_wait(barrier, BRICKS - 1 + BATCH - 1)
    send_near_first(pos)
    pos_got[me] = pos_sent[me]
    turn_weights(
        planes,
        line_factors,
        layer_one,
        layer_two,
        layer_out,
        density_head,
        plane_t,
        line_t,
        one_t,
        two_t,
        out_t,
        out_aug,
        two_half,
    )
    for ref in (acc_lines, acc_one, acc_two, acc_out, acc_bias, dec_sent):
        ref[...] = jnp.zeros_like(ref)

    def look_up(q):
        peers = [at.peer(q, j) for j in range(PEERS)]
        for p in peers:

            @pl.when(p != me)
            def _():
                pos.receive(p)

        lanes = pl.ds(pl.multiple_of(q * CHUNK, CHUNK), CHUNK)
        coords = [coordinate(pos_got, peers, c) for c in range(3)]
        points = iota((G, CHUNK), 0, F32)
        hats = [hat(coord - points) for coord in coords]
        line_value = mm(line_t[...], line_table(hats))
        line_s[:, lanes] = line_value.astype(BF16)
        for pair in range(3):
            a, b, line = PAIRS[pair]
            stripe, weights = stripe_weights(coords[a], hats[b])
            wide = mm(plane_t[pair], weights)
            stripe = jnp.broadcast_to(stripe, (8, CHUNK))
            masks = [stripe == float(h) for h in range(STRIPES)]
            values = []
            for r in range(0, COMP, 8):
                value = wide[r : r + 8]
                for h in range(1, STRIPES):
                    value = jnp.where(masks[h], wide[COMP * h + r : COMP * h + r + 8], value)
                values.append(value)
            value = jnp.concatenate(values, axis=0)
            rows = slice(COMP * pair, COMP * pair + COMP)
            vm_s[rows, lanes] = (value * line_value[rows]).astype(BF16)
            plane_s[rows, lanes] = value.astype(BF16)
            yield

    def network(q):
        peers = [at.peer(q, j) for j in range(PEERS)]
        lanes = pl.ds(pl.multiple_of(q * CHUNK, CHUNK), CHUNK)
        h1 = silu_of_half(mm(one_t[...], vm_s[:, lanes]), h1_s, s1_s, lanes)
        yield
        h2 = silu_of_half(mm(two_t[...], h1), h2_s, s2_s, lanes)
        wide = mm(out_t[...], h2)
        feat = wide[:FEAT].astype(BF16)
        feat_s[:, lanes] = feat
        zeta = wide[FEAT : FEAT + 1] + bias[0]
        zeta_s[:, lanes] = jnp.broadcast_to(zeta, (8, CHUNK))
        yield
        low = low_half((HALF, 128))
        for j, p in enumerate(peers):
            depths, befores, total = within_crossing(zeta, j)
            summed = jnp.zeros((FEAT, 128), F32)
            for half in range(2):
                weight = jnp.exp(-befores[half]) * (1.0 - jnp.exp(-depths[half]))
                lane = 256 * j + 128 * half
                summed = summed + weight * feat[:, lane : lane + 128].astype(F32)
            summed = summed + swap(summed)
            folded = jnp.where(low, summed[:HALF], summed[HALF:])
            parts = [part.astype(F32) for part in split3(total)]
            rows = [folded] + parts + [jnp.zeros((MSG - HALF - 3, 128), F32)]
            msg_sent[p] = jnp.concatenate(rows, axis=0).astype(BF16)
        yield
        for p in peers:

            @pl.when(p != me)
            def _():
                msg.send(p)

    def forward(q, carry):
        together(look_up(q + 1), network(q))
        return carry

    together(look_up(0))
    lax.fori_loop(0, CHUNKS - 1, forward, 0)
    together(network(CHUNKS - 1))
    msg_got[me] = msg_sent[me]

    ray_slots = ray_slots_ref[...]
    cross_mask = jnp.where(slot_cross[...] == iota((8, SLOTS), 0, F32), 1.0, 0.0)
    low = low_half((HALF, 128))
    low_row = low_half((1, 128))
    low8 = low_half((8, 128))
    msg.others(msg.receive)
    depth_rows = []
    for tile in range(BRICKS // 2):
        even, odd = msg_got[2 * tile].astype(F32), msg_got[2 * tile + 1].astype(F32)
        e, o = even[:HALF], odd[:HALF]
        lanes = slice(128 * tile, 128 * tile + 128)
        gathered[:HALF, lanes] = jnp.where(low, e, swap(o))
        gathered[HALF:, lanes] = jnp.where(low, swap(e), o)
        e = even[HALF : HALF + 1] + even[HALF + 1 : HALF + 2] + even[HALF + 2 : HALF + 3]
        o = odd[HALF : HALF + 1] + odd[HALF + 1 : HALF + 2] + odd[HALF + 2 : HALF + 3]
        depth_rows.append(jnp.where(low_row, e, o))
    depth = jnp.concatenate(depth_rows, axis=1)
    by_ray = by_cross(depth, cross_mask, ray_slots)
    running = jnp.zeros((1, RAYS), F32)
    befores = []
    for k in range(CROSS):
        befores.append(running)
        running = running + by_ray[k : k + 1]
    enter = to_slots(jnp.exp(-jnp.concatenate(befores, axis=0)), cross_mask, ray_slots)
    partials = gathered[...]
    scaled = partials * enter
    high = scaled.astype(BF16)
    rest = (scaled - high.astype(F32)).astype(BF16)
    composite = nt(jnp.concatenate([high, rest], axis=0), ray_slots)
    composite = (composite[:FEAT] + composite[FEAT:]).astype(BF16)
    decoder_pre = tn(decoder_in[...], composite)
    gate = sigmoid(decoder_pre)
    decoder_hidden = (decoder_pre * gate).astype(BF16)
    logits = mm(decoder_out[...], decoder_hidden)
    colors = sigmoid(logits)
    errors = colors - target[...]
    scale = float(RAYS * BRICKS * BATCH) ** (-0.5)
    grad_logits = (2.0 * scale * errors * colors * (1.0 - colors)).astype(BF16)
    back_decoder = tn(decoder_out[...], grad_logits)
    grad_pre = (back_decoder * (gate * (1.0 + decoder_pre * (1.0 - gate)))).astype(BF16)
    grad_composite = mm(decoder_in[...], grad_pre).astype(BF16)
    grad_slots = mm(grad_composite, ray_slots)
    along = jnp.sum(partials * grad_slots, axis=0, keepdims=True) * enter
    by_ray = by_cross(along, cross_mask, ray_slots)
    running = jnp.zeros((1, RAYS), F32)
    laters = []
    for k in reversed(range(CROSS)):
        laters.insert(0, running)
        running = running + by_ray[k : k + 1]
    later = to_slots(jnp.concatenate(laters, axis=0), cross_mask, ray_slots)
    for tile in range(BRICKS // 2):
        lanes = slice(128 * tile, 128 * tile + 128)
        top, bottom = grad_slots[:HALF, lanes], grad_slots[HALF:, lanes]
        scalars = [part.astype(F32) for part in split3(enter[:, lanes]) + split3(later[:, lanes])]
        scalars = jnp.concatenate(scalars + [jnp.zeros((2, 128), F32)], axis=0)
        turned = swap(scalars)
        rows = [jnp.where(low, top, swap(bottom)), jnp.where(low8, scalars, turned)]
        back_sent[2 * tile] = jnp.concatenate(rows, axis=0).astype(BF16)
        rows = [jnp.where(low, swap(top), bottom), jnp.where(low8, turned, scalars)]
        back_sent[2 * tile + 1] = jnp.concatenate(rows, axis=0).astype(BF16)
    send_near_first(back)
    back_got[me] = back_sent[me]

    objective = scale * jnp.sum(errors * errors)
    grad_out = nt(grad_logits, decoder_hidden)
    grad_in = nt(composite, grad_pre)
    for j in range(8):
        dec_sent[j] = grad_in[8 * j : 8 * j + 8, :128]
        dec_sent[8 + j] = grad_in[8 * j : 8 * j + 8, 128:]
    rows = [grad_out[:, :128], grad_out[:, 128:], jnp.full((2, 128), objective, F32)]
    dec_sent[16] = jnp.concatenate(rows, axis=0)

    def backward(i, carry):
        q = CHUNKS - 1 - i
        peers = [at.peer(q, j) for j in range(PEERS)]
        for p in peers:

            @pl.when(p != me)
            def _():
                back.receive(p)

        lanes = pl.ds(pl.multiple_of(q * CHUNK, CHUNK), CHUNK)
        zeta = zeta_s[0:1, lanes]
        feat = feat_s[:, lanes].astype(F32)
        grad_feats, grad_zetas = [], []
        for j, p in enumerate(peers):
            depths, befores, total = within_crossing(zeta, j)
            got = back_got[p].astype(F32)
            m = got[:HALF]
            turned = swap(m)
            grads = jnp.concatenate([jnp.where(low, m, turned), jnp.where(low, turned, m)], axis=0)
            enter = got[HALF : HALF + 1] + got[HALF + 1 : HALF + 2] + got[HALF + 2 : HALF + 3]
            later = got[HALF + 3 : HALF + 4] + got[HALF + 4 : HALF + 5] + got[HALF + 5 : HALF + 6]
            carried, lit = [], []
            for half in range(2):
                lane = 256 * j + 128 * half
                transmit = enter * jnp.exp(-befores[half])
                survive = jnp.exp(-depths[half])
                weight = transmit * (1.0 - survive)
                grad_weight = jnp.sum(grads * feat[:, lane : lane + 128], axis=0, keepdims=True)
                grad_feats.append(weight * grads)
                carried.append(grad_weight * weight)
                lit.append(grad_weight * transmit * survive)
            c0, c1 = carried
            r0, r1 = swap(c0), swap(c1)
            laters = (
                jnp.where(low_row, r0, 0.0) + (c1 + r1) + later,
                jnp.where(low_row, r1, 0.0) + later,
            )
            for half in range(2):
                lane = 256 * j + 128 * half
                grad_density = (STEP_LENGTH * (lit[half] - laters[half])).astype(BF16)
                gate = sigmoid(zeta[:, lane : lane + 128])
                grad_zetas.append((grad_density.astype(F32) * gate).astype(BF16).astype(F32))
        grad_zeta = jnp.concatenate(grad_zetas, axis=1)
        acc_bias[...] += jnp.full((8, 128), jnp.sum(grad_zeta), F32)
        rows = [jnp.concatenate(grad_feats, axis=1), grad_zeta]
        rows.append(jnp.zeros((AUG - FEAT - 1, CHUNK), F32))
        grad_aug = jnp.concatenate(rows, axis=0).astype(BF16)
        aug_s[:, lanes] = grad_aug
        grad_a2 = (mm(out_aug[...], grad_aug) * s2_s[:, lanes].astype(F32)).astype(BF16)
        s2_s[:, lanes] = grad_a2
        grad_a1 = (mm(two_half[...], grad_a2) * s1_s[:, lanes].astype(F32)).astype(BF16)
        s1_s[:, lanes] = grad_a1
        grad_vm = mm(layer_one[0], grad_a1)
        plane_s[:, lanes] = (grad_vm * plane_s[:, lanes].astype(F32)).astype(BF16)
        line_s[:, lanes] = (grad_vm * line_s[:, lanes].astype(F32)).astype(BF16)
        return carry

    lax.fori_loop(0, CHUNKS, backward, 0)
    dec.others(dec.send)
    dec_got[me] = dec_sent[me]

    partner_a = x + 1 - 2 * lax.rem(x, 2)
    partner_b = BATCH - 1 - x
    partners = (partner_a, partner_b)

    def across(src, dst, stage, step, side, partner):
        n = (stage * 2 + step) * 2 + side
        return pltpu.make_async_remote_copy(
            src_ref=src,
            dst_ref=dst,
            send_sem=sum_ss.at[n],
            recv_sem=sum_rs.at[n],
            device_id={"batch": partner},
            device_id_type=MESH,
        )

    def exchange_half(stage, step, side):
        start, end = SIDES[stage][side : side + 2]
        rows = pl.ds(start, end - start)
        src = (own, pair_sum)[step].at[rows]
        partner = partners[(side + step) % 2]
        return across(src, pair_got.at[step].at[rows], stage, step, side, partner)

    def advance(stage, step):
        for side in range(2):
            start, end = SIDES[stage][side : side + 2]
            if step > 0:
                exchange_half(stage, step - 1, side).wait()
                mine = (own, pair_sum)[step - 1][start:end, :].astype(F32)
                theirs = pair_got[step - 1, start:end, :].astype(F32)
                (pair_sum, whole)[step - 1][start:end, :] = (mine + theirs).astype(BF16)
            if step < 2:
                exchange_half(stage, step, side).start()

    def settle(pair):
        side, base = STRIPE * G, BASES[pair]
        parts = [whole[base + side * t : base + side * t + side, :] for t in range(3)]
        turned = nt(eye(WIDE), jnp.concatenate(parts, axis=1)).astype(BF16)
        for h in range(STRIPES):
            planes_out[COMP * pair : COMP * pair + COMP, side * h : side * h + side] = turned[
                COMP * h : COMP * h + COMP
            ]

    def small_copy(d, peer):
        return pltpu.make_async_remote_copy(
            src_ref=small_sent,
            dst_ref=small_got.at[x],
            send_sem=small_ss.at[d],
            recv_sem=small_rs.at[d],
            device_id={"batch": peer},
            device_id_type=MESH,
        )

    def spread_copy(peer, slot):
        return pltpu.make_async_remote_copy(
            src_ref=dec_all.at[me],
            dst_ref=dec_all.at[slot],
            send_sem=all_ss.at[peer],
            recv_sem=all_rs.at[slot],
            device_id={"brick": peer},
            device_id_type=MESH,
        )

    for pair in range(3):
        a, b, line = PAIRS[pair]
        acc_planes[...] = jnp.zeros_like(acc_planes)

        def scatter(g, carry):
            masked, weights = [], []
            for q in range(GROUP):
                q = g * GROUP + q
                peers = [at.peer(q, j) for j in range(PEERS)]
                lanes = pl.ds(pl.multiple_of(q * CHUNK, CHUNK), CHUNK)
                points = iota((G, CHUNK), 0, F32)
                other_hat = hat(coordinate(pos_got, peers, b) - points)
                stripe, weight = stripe_weights(coordinate(pos_got, peers, a), other_hat)
                piece = line_s[COMP * pair : COMP * pair + COMP, lanes]
                rows = [
                    piece * jnp.where(stripe == float(h), 1.0, 0.0).astype(BF16)
                    for h in range(STRIPES)
                ]
                masked.append(jnp.concatenate(rows, axis=0))
                weights.append(weight)
            acc_planes[...] += nt(
                jnp.concatenate(masked, axis=1), jnp.concatenate(weights, axis=1)
            )
            return carry

        lax.fori_loop(0, CHUNKS // GROUP, scatter, 0)
        side = STRIPE * G
        acc_planes[COMP:, :G] += acc_planes[: WIDE - COMP, side:]
        turned = nt(eye(side), acc_planes[:, :side].astype(BF16)).astype(BF16)
        base = BASES[pair]
        for tile in range(3):
            own[base + side * tile : base + side * tile + side, :] = turned[
                :, 128 * tile : 128 * tile + 128
            ]
        advance(pair, 0)
        if pair > 0:
            advance(pair - 1, 1)
        if pair == 1:
            dec.others(dec.receive)
            total = dec_got[0]
            for j in range(1, BRICKS):
                total = total + dec_got[j]
            small_sent[0:8] = total
            small_sent[8:16] = jnp.concatenate(
                [acc_bias[0:1, :], jnp.zeros((7, 128), F32)], axis=0
            )
            for d, peer in enumerate(x_peers):
                small_copy(d, peer).start()
            small_got[x] = small_sent[...]
        if pair == 2:
            for d, peer in enumerate(x_peers):
                small_copy(d, peer).wait()
            small = (small_got[0] + small_got[1]) + (small_got[2] + small_got[3])
            small_sums[0:8] = small[8:16]
            dec_all[me] = small[0:8]
            dec.others(lambda peer: spread_copy(peer, me).start())
    def layers(g, carry):
        tables = []
        for q in range(GROUP):
            q = g * GROUP + q
            peers = [at.peer(q, j) for j in range(PEERS)]
            points = iota((G, CHUNK), 0, F32)
            hats = [hat(coordinate(pos_got, peers, c) - points) for c in range(3)]
            tables.append(line_table(hats))
        lanes = pl.ds(pl.multiple_of(g * GROUP * CHUNK, GROUP * CHUNK), GROUP * CHUNK)
        acc_lines[...] += nt(plane_s[:, lanes], jnp.concatenate(tables, axis=1))
        acc_out[...] += nt(aug_s[:, lanes], h2_s[:, lanes])
        acc_two[...] += nt(h1_s[:, lanes], s2_s[:, lanes])
        acc_one[...] += nt(vm_s[:, lanes], s1_s[:, lanes])
        return carry

    lax.fori_loop(0, CHUNKS // GROUP, layers, 0)
    base = BASES[3]
    own[base : base + VM, :] = acc_one[...].astype(BF16)
    own[base + VM : base + VM + HID, :] = acc_two[...].astype(BF16)
    own[base + VM + HID : base + VM + HID + FEAT, :] = acc_out[:FEAT, :].astype(BF16)
    column = iota((COMP, 128), 1)
    diagonal = jnp.where(column < G, acc_lines[:COMP, :], 0.0)
    diagonal = jnp.where((column >= G) & (column < 2 * G), acc_lines[COMP : 2 * COMP, :], diagonal)
    diagonal = jnp.where(
        (column >= 2 * G) & (column < 3 * G), acc_lines[2 * COMP :, :], diagonal
    )
    own[base + VM + HID + FEAT :, :] = diagonal.astype(BF16)
    advance(3, 0)
    advance(2, 1)
    head_sent[...] = jnp.broadcast_to(acc_out[FEAT : FEAT + 1, :], (8, 128))

    def head_copy(d, peer):
        return pltpu.make_async_remote_copy(
            src_ref=head_sent,
            dst_ref=head_got.at[x],
            send_sem=head_ss.at[d],
            recv_sem=head_rs.at[d],
            device_id={"batch": peer},
            device_id_type=MESH,
        )

    for d, peer in enumerate(x_peers):
        head_copy(d, peer).start()
    head_got[x] = head_sent[...]
    for exchange in (pos, msg):
        exchange.sends_done()
    advance(0, 2)
    settle(0)
    advance(3, 1)
    advance(1, 2)
    settle(1)
    dec.others(lambda peer: spread_copy(peer, peer).wait_recv())
    decoder_sums[...] = dec_all[...]
    dec.others(lambda peer: spread_copy(peer, me).wait_send())
    for exchange in (back, dec):
        exchange.sends_done()
    for d, peer in enumerate(x_peers):
        head_copy(d, peer).wait()
    small_sums[8:16] = (head_got[0] + head_got[1]) + (head_got[2] + head_got[3])
    advance(2, 2)
    settle(2)
    advance(3, 2)
    layers_out[...] = whole[BASES[3] :, :]


def unpack(
    planes_in,
    layers,
    decoder_sums,
    small_sums,
    planes,
    lines,
    one,
    two,
    out,
    head,
    bias,
    decoder_in,
    decoder_out,
    objective,
):
    planes[0] = planes_in[...].astype(F32)
    one[0] = layers[0:VM, :].astype(F32)
    two[0] = layers[VM : VM + HID, :].astype(F32)
    out[0] = layers[VM + HID : VM + HID + FEAT, :].astype(F32)
    block = layers[VM + HID + FEAT : PACK - BASES[3], :]
    row, column = iota((G, 128), 0), iota((G, 128), 1)
    parts = []
    for p in range(3):
        pick = jnp.where(column == row + G * p, 1.0, 0.0).astype(BF16)
        parts.append(nt(pick, block))
    lines[0] = jnp.concatenate(parts, axis=1)
    bias[...] = small_sums[0:1, 0:1]
    head[...] = small_sums[8:9, :]
    for j in range(8):
        decoder_in[8 * j : 8 * j + 8, 0:128] = decoder_sums[j]
        decoder_in[8 * j : 8 * j + 8, 128:256] = decoder_sums[8 + j]
    last = decoder_sums[16]
    decoder_out[:, 0:128] = last[0:3]
    decoder_out[:, 128:256] = last[3:6]
    objective[...] = last[6:7, 0:1]


def shape(dims, kind=F32):
    return jax.ShapeDtypeStruct(dims, kind)


def on_device(
    crossings,
    lattice,
    offsets,
    target,
    planes,
    line_factors,
    layer_one,
    layer_two,
    layer_out,
    density_head,
    density_bias,
    decoder_in,
    decoder_out,
):
    dma = pltpu.SemaphoreType.DMA
    vmem = pltpu.VMEM
    planes_sum, layers_sum, decoder_sums, small_sums = pl.pallas_call(
        train,
        out_shape=(
            shape((VM, G * G), BF16),
            shape((PACK - BASES[3], 128), BF16),
            shape((BRICKS, 8, 128)),
            shape((16, 128)),
        ),
        in_specs=[VMEM_SPEC] * 10 + [SMEM_SPEC] + [VMEM_SPEC] * 2,
        out_specs=[VMEM_SPEC] * 4,
        scratch_shapes=[vmem((BRICKS, 8, 128), F32)] * 2
        + [vmem((BRICKS, MSG, 128), BF16)] * 4
        + [vmem((BRICKS, 8, 128), F32)] * 3
        + [vmem((16, 128), F32), vmem((BATCH, 16, 128), F32)]
        + [vmem((8, 128), F32), vmem((BATCH, 8, 128), F32), vmem((AUG, SAMPLES), BF16)]
        + [vmem((RAYS, SLOTS), BF16), vmem((8, SLOTS), F32)]
        + [
            vmem((3, WIDE, LOCAL), BF16),
            vmem((VM, 128), BF16),
            vmem((HID, VM), BF16),
            vmem((HID, HID), BF16),
            vmem((AUG, HID), BF16),
            vmem((HID, AUG), BF16),
            vmem((HID, HID), BF16),
        ]
        + [vmem((VM, SAMPLES), BF16)] * 3
        + [vmem((HID, SAMPLES), BF16)] * 4
        + [vmem((FEAT, SAMPLES), BF16), vmem((8, SAMPLES), F32)]
        + [
            vmem((FEAT, SLOTS), F32),
            vmem((WIDE, LOCAL), F32),
            vmem((VM, 128), F32),
            vmem((VM, HID), F32),
            vmem((HID, HID), F32),
            vmem((AUG, HID), F32),
            vmem((8, 128), F32),
        ]
        + [
            vmem((PACK, 128), BF16),
            vmem((PACK, 128), BF16),
            vmem((2, PACK, 128), BF16),
            vmem((PACK, 128), BF16),
        ]
        + [dma((BRICKS,))] * 10
        + [dma((BATCH - 1,))] * 4
        + [dma((16,))] * 2,
        compiler_params=pltpu.CompilerParams(collective_id=0, has_side_effects=True),
        name="train",
    )(
        crossings.T,
        lattice,
        offsets,
        target,
        jnp.swapaxes(planes, 1, 2),
        line_factors,
        layer_one,
        layer_two,
        jnp.swapaxes(layer_out, 1, 2),
        density_head,
        density_bias,
        decoder_in,
        decoder_out,
    )
    outs = pl.pallas_call(
        unpack,
        out_shape=(
            shape((1, VM, G * G)),
            shape((1, G, VM)),
            shape((1, VM, HID)),
            shape((1, HID, HID)),
            shape((1, FEAT, HID)),
            shape((1, HID)),
            shape((1, 1)),
            shape((FEAT, DEC)),
            shape((3, DEC)),
            shape((1, 1)),
        ),
        in_specs=[VMEM_SPEC] * 4,
        out_specs=[VMEM_SPEC] * 10,
        name="unpack",
    )(planes_sum, layers_sum, decoder_sums, small_sums)
    outs = list(outs)
    outs[0] = jnp.swapaxes(outs[0], 1, 2)
    outs[4] = jnp.swapaxes(outs[4], 1, 2)
    outs[6] = outs[6].reshape(1)
    outs[9] = outs[9].reshape(())
    return tuple(outs)

def solution(mesh):
    placed = (
        P(("brick", "batch"), None),
        P(None, None, None, ("brick", "batch")),
        P(None, None, None, ("brick", "batch")),
        P(None, ("brick", "batch")),
        P("brick", None, None),
        P("brick", None, None),
        P("brick", None, None),
        P("brick", None, None),
        P("brick", None, None),
        P("brick", None),
        P("brick"),
        P(),
        P(),
    )
    return jax.shard_map(
        on_device,
        mesh=mesh,
        in_specs=placed,
        out_specs=(
            P("brick", None, None),
            P("brick", None, None),
            P("brick", None, None),
            P("brick", None, None),
            P("brick", None, None),
            P("brick", None),
            P("brick"),
            P(),
            P(),
            P(),
        ),
        check_vma=False,
    )
```
